32 devices in a mesh: grid: 8 (over z, y), snap: 4 (over x, core).
Axes of the slice: x: 2, y: 2, z: 4, core: 2. Of those that a mesh axis runs over, the one named last changes fastest.
Arguments:
- fields: bfloat16 [49152, 1024], P('grid', 'snap'), may hold values from -40 to 40
- start_local: float32 [1024, 128], P('snap'), may hold values from -6 to 6
- start_pair: float32 [2, 256, 128], replicated, may hold values from -6 to 6
- start_root: float32 [256, 128], replicated, may hold values from -6 to 6
Outputs:
- modes: bfloat16 [49152, 128], P(('grid', 'snap'))
The draws below stay inside these ranges and needn't reach their ends.
All inputs are finite; a program needn't handle non-finite values.
Results may differ from the reference program's by a relative error of at most 0.0055.
Values may be sent and summed in bfloat16 or wider, within the bound.
No kernel may reach another device: no remote copies, remote signals or barrier semaphores. Data moves between devices by JAX's collectives and lax.ppermute only.
A program may use at most 64 MiB of HBM per device.

```python
import math
import jax
import jax.numpy as jnp
from jax import lax

ROWS_DEV = 6144
SNAP_DEV = 256
RANK = 128
POWER = 2
NEWTON = 8
MODES = 24
POINTS = 49152
SNAPS = 1024
N_GRID = 8
N_SNAP = 4


def draw_fields(key, part):
    subkeys = jax.random.split(jax.random.fold_in(key, 11), 7)
    regions = 4 * N_GRID
    region_rows = ROWS_DEV // 4
    envelope = jnp.exp(jax.random.uniform(subkeys[0], (regions, MODES), jnp.float32, math.log(0.1), math.log(3.0)))
    spatial = jax.random.normal(subkeys[1], (regions, region_rows, MODES), jnp.float32) * envelope[:, None, :]
    amplitude = 3.0 * 0.8 ** jnp.arange(MODES, dtype=jnp.float32)
    spatial = spatial.reshape(POINTS, MODES) * amplitude
    temporal = jax.random.normal(subkeys[2], (MODES, SNAPS), jnp.float32)
    signal = jnp.dot(spatial, temporal, precision=lax.Precision.HIGHEST)
    ramp = jnp.arange(N_GRID, dtype=jnp.float32) / max(N_GRID - 1, 1)
    local_scale = 0.4 * math.sqrt(N_GRID) * jnp.exp(ramp * math.log(3.0))
    local_space = jax.random.normal(subkeys[5], (N_GRID, ROWS_DEV, 2), jnp.float32) * local_scale[:, None, None]
    local_time = jax.random.normal(subkeys[6], (N_GRID, 2, SNAPS), jnp.float32)
    local_part = jnp.matmul(local_space, local_time, precision=lax.Precision.HIGHEST).reshape(POINTS, SNAPS)
    noise_part = jax.random.normal(subkeys[4], (POINTS, SNAPS), jnp.float32)
    return jnp.clip(signal + local_part + noise_part, -40.0, 40.0).astype(jnp.bfloat16)


def block_scale(own_key, extent, shards, low, largest):
    def one(dim, blocks):
        steps = jax.random.uniform(jax.random.fold_in(jax.random.fold_in(own_key, 6), dim), (blocks,), jnp.float32, low / len(shards), largest / len(shards))
        return jnp.repeat(jnp.exp(steps), extent[dim] // blocks).reshape((-1,) + (1,) * (len(extent) - dim - 1))

    factor_of = one(*shards[0])
    for cut in shards[1:]:
        factor_of = factor_of * one(*cut)
    return factor_of


def normal_values(key, shape, scale, most, shards=(), kind=jnp.bfloat16):
    array = jax.random.normal(key, shape, jnp.float32) * scale
    if len(shards) > 0:
        array = block_scale(key, shape, shards, -0.22, 0.18) * array
    return jnp.clip(array, min=-most, max=most).astype(kind)


def setup_inputs(seed: int = 0) -> dict:
    key_list = jax.random.split(jax.random.key(seed), 5)
    return {
        "fields": draw_fields(jax.random.fold_in(key_list[4], 71), 0),
        "start_local": normal_values(key_list[1], (SNAPS, RANK), 1.0, 6.0, ((0, 4),), jnp.float32),
        "start_pair": normal_values(key_list[2], (2, 2 * RANK, RANK), 1.0, 6.0, (), jnp.float32),
        "start_root": normal_values(key_list[3], (2 * RANK, RANK), 1.0, 6.0, (), jnp.float32),
    }


def polar_basis(gram_matrix, initial):
    current = initial
    for power_step in range(POWER):
        product = jnp.dot(gram_matrix, current, precision=lax.Precision.HIGHEST)
        iterate = product / jnp.sqrt(jnp.sum(product * product) + 1e-06)
        for newton_step in range(NEWTON):
            inner_gram = jnp.dot(iterate.T, iterate, precision=lax.Precision.HIGHEST)
            iterate = 1.5 * iterate - 0.5 * jnp.dot(iterate, inner_gram, precision=lax.Precision.HIGHEST)
        current = iterate
    return current

def reference(fields, start_local, start_pair, start_root):
    inverse_count = 1.0 / POINTS
    leaves = []
    for column_block in range(N_SNAP):
        columns = fields[:, column_block * SNAP_DEV:(column_block + 1) * SNAP_DEV]
        gram_sum = jnp.dot(columns.T, columns, preferred_element_type=jnp.float32) * inverse_count
        rotation = polar_basis(gram_sum, start_local[column_block * SNAP_DEV:(column_block + 1) * SNAP_DEV])
        leaves.append(jnp.dot(columns, rotation.astype(jnp.bfloat16), preferred_element_type=jnp.float32).astype(jnp.bfloat16))
    merged = []
    for pair_index in range(2):
        joined = jnp.concatenate([leaves[2 * pair_index], leaves[2 * pair_index + 1]], axis=1)
        gram_sum = jnp.dot(joined.T, joined, preferred_element_type=jnp.float32) * inverse_count
        rotation = polar_basis(gram_sum, start_pair[pair_index])
        merged.append(jnp.dot(joined, rotation.astype(jnp.bfloat16), preferred_element_type=jnp.float32).astype(jnp.bfloat16))
    joined = jnp.concatenate(merged, axis=1)
    gram_sum = jnp.dot(joined.T, joined, preferred_element_type=jnp.float32) * inverse_count
    rotation = polar_basis(gram_sum, start_root)
    return jnp.dot(joined, rotation.astype(jnp.bfloat16), preferred_element_type=jnp.float32).astype(jnp.bfloat16)
```

```python
import jax
import jax.numpy as jnp
from jax import lax
from jax.experimental import pallas as pl
from jax.experimental.pallas import tpu as pltpu
from jax.sharding import PartitionSpec as P

POWER = 2
NEWTON = 8
F32 = jnp.float32
BF16 = jnp.bfloat16


def exchange(value, axis, bit):
    mask = 2**bit
    pairs = [(source, source ^ mask) for source in range(lax.axis_size(axis))]
    return lax.ppermute(value, axis, pairs)


def bit_of(axis, bit):
    return (lax.axis_index(axis) // 2**bit) % 2


def pick(flag, if_set, if_clear):
    return jnp.where(flag == 1, if_set, if_clear)


def sum_over(value, steps):
    (axis, bit), rest = steps[0], steps[1:]
    side = bit_of(axis, bit)
    half = value.shape[0] // 2
    low, high = value[:half], value[half:]
    kept = pick(side, high, low) + exchange(pick(side, low, high), axis, bit)
    for step in rest:
        kept = kept + exchange(kept, *step)
    other = exchange(kept, axis, bit)
    return jnp.concatenate([pick(side, other, kept), pick(side, kept, other)], axis=0)


def axis_steps(axis):
    return [(axis, bit) for bit in range(lax.axis_size(axis).bit_length() - 1)]


def split(x):
    high = x.astype(BF16)
    return high, (x - high.astype(F32)).astype(BF16)


def product(a, b, transposed=False):
    return lax.dot_general(
        a, b, (((1,), (1 if transposed else 0,)), ((), ())), preferred_element_type=F32
    )


def solve_kernel(gram_ref, start_ref, rotation_ref, kept_ref):
    gram_high, gram_low = split(gram_ref[...])
    rank = start_ref.shape[0]
    rows = lax.broadcasted_iota(jnp.int32, (rank, rank), 0)
    columns = lax.broadcasted_iota(jnp.int32, (rank, rank), 1)
    identity = (rows == columns).astype(F32)

    def times_right(x, right):
        out = product(jnp.concatenate(split(x), axis=1), right)
        return out[:, :rank] + out[:, rank:]

    basis = start_ref[...]
    for _ in range(POWER):
        high, low = split(basis)
        out = product(jnp.concatenate([high, low], axis=0), gram_high)
        image = out[:rank] + out[rank:] + product(high, gram_low)
        image = image * lax.rsqrt(jnp.sum(image * image) + 1e-06)
        image_high, image_low = split(image)
        stacked = jnp.concatenate([image_high, image_low], axis=0)
        out = product(stacked, stacked, transposed=True)
        inner = out[:rank, :rank] + out[:rank, rank:] + out[rank:, :rank]
        total = None
        for step in range(NEWTON):
            factor = 1.5 * identity - 0.5 * inner
            row = jnp.concatenate(split(factor), axis=1)
            right = jnp.concatenate([row, row], axis=0)
            if step < NEWTON - 1:
                inner = times_right(times_right(inner, right), right)
            total = factor if total is None else times_right(total, right)
        total_high, total_low = split(total)
        basis = product(
            jnp.concatenate([total_high, total_low], axis=1),
            jnp.concatenate([image_high, image_high], axis=0),
        ) + product(total_high, image_low)
    rotation = basis.astype(BF16)
    rotation_ref[...] = rotation
    image = product(rotation, gram_high) + product(rotation, gram_low)
    high, low = split(image)
    kept_ref[...] = product(high, rotation, True) + product(low, rotation, True)


def solve(gram, start):
    rank = start.shape[1]
    return pl.pallas_call(
        solve_kernel,
        out_shape=(
            jax.ShapeDtypeStruct((rank, gram.shape[0]), BF16),
            jax.ShapeDtypeStruct((rank, rank), F32),
        ),
        in_specs=[pl.BlockSpec(memory_space=pltpu.VMEM)] * 2,
        out_specs=(pl.BlockSpec(memory_space=pltpu.VMEM),) * 2,
        name="solve",
    )(gram, start.T)


def rotate(rows, rotation):
    return product(rows, rotation, transposed=True).astype(BF16)


def inner_product(left, right):
    return lax.dot_general(
        left, right, (((0,), (0,)), ((), ())), preferred_element_type=F32
    )


def join(first, second, cross):
    top = jnp.concatenate([first, cross], axis=1)
    bottom = jnp.concatenate([cross.T, second], axis=1)
    return jnp.concatenate([top, bottom], axis=0)


def on_device(fields, start_local, start_pair, start_root):
    local_rows = fields.shape[0]
    scale = 1.0 / (local_rows * lax.axis_size("grid"))
    low_bit, high_bit = bit_of("snap", 0), bit_of("snap", 1)
    grid_steps = axis_steps("grid")
    rank = start_local.shape[1]

    gram = inner_product(fields, fields)
    upper = jnp.concatenate([gram[:rank, :rank], gram[:rank, rank:], gram[rank:, rank:]], axis=0)
    upper = sum_over(upper, grid_steps) * scale
    gram = join(upper[:rank], upper[2 * rank :], upper[rank : 2 * rank])
    rotation, kept = solve(gram, start_local)
    leaf = rotate(fields, rotation).reshape(2, 2, local_rows // 4, rank)

    own = pick(low_bit, leaf[:, 1], leaf[:, 0])
    other = exchange(pick(low_bit, leaf[:, 0], leaf[:, 1]), "snap", 0)
    other_kept = exchange(kept, "snap", 0)
    lower = pick(low_bit, other, own)
    upper = pick(low_bit, own, other)
    cross = inner_product(lower.reshape(-1, rank), upper.reshape(-1, rank))
    cross = sum_over(cross, [("snap", 0)] + grid_steps) * scale
    gram = join(pick(low_bit, other_kept, kept), pick(low_bit, kept, other_kept), cross)
    start = pick(high_bit, start_pair[1], start_pair[0])
    rotation, kept = solve(gram, start)
    joined = jnp.concatenate([lower, upper], axis=2)
    branch = rotate(joined.reshape(-1, 2 * rank), rotation).reshape(2, -1, rank)

    own = pick(high_bit, branch[1], branch[0])
    other = exchange(pick(high_bit, branch[0], branch[1]), "snap", 1)
    other_kept = exchange(kept, "snap", 1)
    lower = pick(high_bit, other, own)
    upper = pick(high_bit, own, other)
    cross = inner_product(lower, upper)
    cross = sum_over(cross, [("snap", 0), ("snap", 1)] + grid_steps) * scale
    gram = join(pick(high_bit, other_kept, kept), pick(high_bit, kept, other_kept), cross)
    rotation, _ = solve(gram, start_root)
    return rotate(jnp.concatenate([lower, upper], axis=1), rotation)


def solution(mesh):
    in_specs = (P("grid", "snap"), P("snap", None), P(), P())
    out_specs = P(("grid", "snap"), None)
    return jax.shard_map(
        on_device, mesh=mesh, in_specs=in_specs, out_specs=out_specs, check_vma=False
    )
```

```python
import jax
import jax.numpy as jnp
from jax import lax
from jax.experimental import pallas as pl
from jax.experimental.pallas import tpu as pltpu
from jax.sharding import PartitionSpec as P

POWER = 2
NEWTON = 8
F32 = jnp.float32
BF16 = jnp.bfloat16
MIB = 2**20


def exchange(value, step):
    axis, bit = step
    mask = 2**bit
    pairs = [(source, source ^ mask) for source in range(lax.axis_size(axis))]
    return lax.ppermute(value, axis, pairs)


def bit_of(step):
    axis, bit = step
    return (lax.axis_index(axis) // 2**bit) % 2


def pick(flag, if_set, if_clear):
    return jnp.where(flag == 1, if_set, if_clear)


def axis_steps(axis):
    return [(axis, bit) for bit in range(lax.axis_size(axis).bit_length() - 1)]


def sum_over(value, steps):
    for step in steps:
        value = value + exchange(value, step)
    return value


def split(x):
    high = x.astype(BF16)
    return high, (x - high.astype(F32)).astype(BF16)


def product(a, b, transposed=False):
    return lax.dot_general(
        a, b, (((1,), (1 if transposed else 0,)), ((), ())), preferred_element_type=F32
    )


def inner_product(left, right):
    return lax.dot_general(
        left, right, (((0,), (0,)), ((), ())), preferred_element_type=F32
    )


def solve(gram, basis):
    gram_high, gram_low = split(gram)
    rank = basis.shape[0]
    rows = lax.broadcasted_iota(jnp.int32, (rank, rank), 0)
    columns = lax.broadcasted_iota(jnp.int32, (rank, rank), 1)
    identity = (rows == columns).astype(F32)

    def times_right(x, right):
        out = product(jnp.concatenate(split(x), axis=1), right)
        return out[:, :rank] + out[:, rank:]

    for _ in range(POWER):
        high, low = split(basis)
        out = product(jnp.concatenate([high, low], axis=0), gram_high)
        image = out[:rank] + out[rank:] + product(high, gram_low)
        image = image * lax.rsqrt(jnp.sum(image * image) + 1e-06)
        image_high, image_low = split(image)
        stacked = jnp.concatenate([image_high, image_low], axis=0)
        out = product(stacked, stacked, transposed=True)
        inner = out[:rank, :rank] + out[:rank, rank:] + out[rank:, :rank]
        total = None
        for step in range(NEWTON):
            factor = 1.5 * identity - 0.5 * inner
            row = jnp.concatenate(split(factor), axis=1)
            right = jnp.concatenate([row, row], axis=0)
            if step < NEWTON - 1:
                inner = times_right(times_right(inner, right), right)
            total = factor if total is None else times_right(total, right)
        total_high, total_low = split(total)
        basis = product(
            jnp.concatenate([total_high, total_low], axis=1),
            jnp.concatenate([image_high, image_high], axis=0),
        ) + product(total_high, image_low)
    return basis.astype(BF16), gram_high, gram_low


def kept_gram(rotation, gram_high, gram_low):
    image = product(rotation, gram_high) + product(rotation, gram_low)
    high, low = split(image)
    return product(high, rotation, True) + product(low, rotation, True)


def pack(gram):
    size = gram.shape[0] // 2
    rows = lax.broadcasted_iota(jnp.int32, (size, size), 0)
    columns = lax.broadcasted_iota(jnp.int32, (size, size), 1)
    first, second = gram[:size, :size], gram[size:, size:]
    diagonal = jnp.sum(jnp.where(rows == columns, second, 0.0), axis=0, keepdims=True)
    diagonal = jnp.broadcast_to(diagonal, (8, size))
    low = jnp.concatenate([jnp.where(rows <= columns, first, second), diagonal], axis=0)
    high = jnp.concatenate([gram[:size, size:], diagonal], axis=0)
    return low, high


def unpack(low, high):
    size = low.shape[1]
    rows = lax.broadcasted_iota(jnp.int32, (size, size), 0)
    columns = lax.broadcasted_iota(jnp.int32, (size, size), 1)
    both, cross = low[:size], high[:size]
    flipped = both.T
    first = jnp.where(rows <= columns, both, flipped)
    second = jnp.where(rows > columns, both, flipped)
    diagonal = jnp.broadcast_to(low[size : size + 1], (size, size))
    second = jnp.where(rows == columns, diagonal, second)
    top = jnp.concatenate([first, cross], axis=1)
    return jnp.concatenate([top, jnp.concatenate([cross.T, second], axis=1)], axis=0)


def leaf_kernel(scale, side_step, kept_ref, other_ref, start_ref, out_ref):
    side = bit_of(side_step) == 1
    kept, other = kept_ref[...], other_ref[...]
    low = jnp.where(side, other, kept)
    high = jnp.where(side, kept, other)
    rank = start_ref.shape[0]
    rotation, gram_high, gram_low = solve(unpack(low, high) * scale, start_ref[...])
    out_ref[:rank] = rotation
    out_ref[rank:] = jnp.concatenate(split(kept_gram(rotation, gram_high, gram_low)), axis=1)


def pair_kernel(
    scale, own_ref, other_ref, own_slab_ref, other_slab_ref, start_ref, out_ref, kept_ref
):
    core = bit_of(("snap", 0)) == 1
    rank = start_ref.shape[0]
    own, other = own_ref[...].astype(F32), other_ref[...].astype(F32)
    first, second = jnp.where(core, other, own), jnp.where(core, own, other)
    own = jnp.concatenate([own_slab_ref[0], own_slab_ref[1]], axis=1)
    other = jnp.concatenate([other_slab_ref[0], other_slab_ref[1]], axis=1)
    cross = jnp.concatenate([jnp.where(core, other, own), jnp.where(core, own, other)], axis=0)
    cross_high, cross_low = split(cross * scale)
    first_rotation, second_rotation = first[:rank].astype(BF16), second[:rank].astype(BF16)
    image = product(first_rotation, cross_high) + product(first_rotation, cross_low)
    high, low = split(image)
    cross = product(high, second_rotation, True) + product(low, second_rotation, True)
    first, second = first[rank:], second[rank:]
    top = jnp.concatenate([first[:, :rank] + first[:, rank:], cross], axis=1)
    bottom = jnp.concatenate([cross.T, second[:, :rank] + second[:, rank:]], axis=1)
    rotation, gram_high, gram_low = solve(jnp.concatenate([top, bottom], axis=0), start_ref[...])
    out_ref[...] = rotation
    kept_ref[...] = kept_gram(rotation, gram_high, gram_low)


def branch_kernel(
    chunk, own_ref, near_ref, far_ref, corner_ref, leaves_ref, far_leaves_ref,
    rotation_ref, far_rotation_ref, lower_ref, upper_ref,
):
    core = bit_of(("snap", 0)) == 1
    high_bit = bit_of(("snap", 1)) == 1
    rank = rotation_ref.shape[0]

    def halves(ref):
        value = ref[...].astype(F32)
        left, right = value[:, :rank], value[:, rank:]
        own, other = jnp.where(core, right, left), jnp.where(core, left, right)
        return own.astype(BF16), other.astype(BF16)

    def branch(refs, leaves, parts, rows):
        total = None
        for number, (ref, part) in enumerate(zip(refs, parts)):
            leaf = product(ref[rows], leaves[number * rank : (number + 1) * rank], True)
            term = product(leaf.astype(BF16), part, True)
            total = term if total is None else total + term
        return total

    leaves, far_leaves = leaves_ref[...], far_leaves_ref[...]
    parts, far_parts = halves(rotation_ref), halves(far_rotation_ref)
    for start in range(0, own_ref.shape[0], chunk):
        rows = pl.ds(start, chunk)
        mine = branch((own_ref, near_ref), leaves, parts, rows)
        theirs = branch((far_ref, corner_ref), far_leaves, far_parts, rows)
        lower_ref[rows] = jnp.where(high_bit, theirs, mine).astype(BF16)
        upper_ref[rows] = jnp.where(high_bit, mine, theirs).astype(BF16)


def root_kernel(
    scale, chunk, kept_ref, other_ref, own_cross_ref, other_cross_ref, start_ref,
    lower_ref, upper_ref, out_ref,
):
    core = bit_of(("snap", 0)) == 1
    high_bit = bit_of(("snap", 1)) == 1
    kept, other = kept_ref[...], other_ref[...]
    own_cross, other_cross = own_cross_ref[...], other_cross_ref[...]
    cross = jnp.concatenate(
        [jnp.where(core, other_cross, own_cross), jnp.where(core, own_cross, other_cross)], axis=0
    ) * scale
    top = jnp.concatenate([jnp.where(high_bit, other, kept), cross], axis=1)
    bottom = jnp.concatenate([cross.T, jnp.where(high_bit, kept, other)], axis=1)
    rotation, _, _ = solve(jnp.concatenate([top, bottom], axis=0), start_ref[...])
    for start in range(0, lower_ref.shape[0], chunk):
        rows = pl.ds(start, chunk)
        root = jnp.concatenate([lower_ref[rows], upper_ref[rows]], axis=1)
        out_ref[rows] = product(root, rotation, True).astype(BF16)


def call(kernel, name, out_shape, *operands, microseconds=8, limit=8 * MIB):
    vmem = pl.BlockSpec(memory_space=pltpu.VMEM)
    return pl.pallas_call(
        kernel,
        out_shape=out_shape,
        in_specs=[vmem] * len(operands),
        out_specs=jax.tree.map(lambda _: vmem, out_shape),
        name=name,
        compiler_params=pltpu.CompilerParams(vmem_limit_bytes=limit),
        cost_estimate=pl.CostEstimate(
            flops=microseconds * 10**9, bytes_accessed=MIB, transcendentals=0
        ),
    )(*operands)


def on_device(fields, start_local, start_pair, start_root):
    local_rows, snaps = fields.shape
    rank = start_local.shape[1]
    quarter = local_rows // 4
    chunk = quarter // 4
    scale = 1.0 / (local_rows * lax.axis_size("grid"))
    core_step, far_step = ("snap", 0), ("snap", 1)
    core, far = bit_of(core_step), bit_of(far_step)
    first_step, *grid_steps = axis_steps("grid")
    side = bit_of(first_step)

    quarters = fields.reshape(2, 2, quarter, snaps)
    sent = lax.dynamic_index_in_dim(quarters, 1 - core, 1, keepdims=False)
    mine = lax.dynamic_index_in_dim(quarters, core, 1, keepdims=False)
    near = exchange(sent, core_step)
    own_rows = lax.dynamic_index_in_dim(mine, far, 0, keepdims=False)
    far_rows = exchange(lax.dynamic_index_in_dim(mine, 1 - far, 0, keepdims=False), far_step)

    low, high = pack(inner_product(fields, fields))
    kept = pick(side, high, low) + exchange(pick(side, low, high), first_step)
    kept = sum_over(kept, grid_steps)
    other = exchange(kept, first_step)

    flat, near_flat = mine.reshape(-1, snaps), near.reshape(-1, snaps)
    cross = inner_product(pick(core, near_flat, flat), pick(core, flat, near_flat))
    cross = cross.reshape(2, rank, 2, rank).transpose(0, 2, 1, 3)
    slab = pick(core, cross[1], cross[0]) + exchange(pick(core, cross[0], cross[1]), core_step)
    part = pick(side, slab[1], slab[0]) + exchange(pick(side, slab[0], slab[1]), first_step)
    part = sum_over(part, grid_steps)
    other_part = exchange(part, first_step)
    slab = jnp.stack([pick(side, other_part, part), pick(side, part, other_part)])
    other_slab = exchange(slab, core_step)
    corner_rows = exchange(lax.dynamic_index_in_dim(near, 1 - far, 0, keepdims=False), far_step)
    near_rows = lax.dynamic_index_in_dim(near, far, 0, keepdims=False)

    square = jax.ShapeDtypeStruct((rank, rank), F32)
    leaf = call(
        lambda *refs: leaf_kernel(scale, first_step, *refs),
        "leaf",
        jax.ShapeDtypeStruct((2 * rank, snaps), BF16),
        kept, other, start_local.T,
    )
    other_leaf = exchange(leaf, core_step)
    leaves = jnp.concatenate([leaf[:rank], other_leaf[:rank]], axis=0)
    far_leaves = exchange(leaves, far_step)

    start = lax.dynamic_index_in_dim(start_pair, far, 0, keepdims=False)
    rotation, kept = call(
        lambda *refs: pair_kernel(scale, *refs),
        "pair",
        (jax.ShapeDtypeStruct((rank, 2 * rank), BF16), square),
        leaf, other_leaf, slab, other_slab, start.T,
    )
    far_rotation = exchange(rotation, far_step)
    other = exchange(kept, far_step)
    rows = jax.ShapeDtypeStruct((quarter, rank), BF16)
    lower, upper = call(
        lambda *refs: branch_kernel(chunk, *refs),
        "branch",
        (rows, rows),
        own_rows, near_rows, far_rows, corner_rows, leaves, far_leaves, rotation, far_rotation,
        microseconds=1, limit=16 * MIB,
    )
    cross = inner_product(lower, upper).reshape(2, rank // 2, rank)
    part = pick(core, cross[1], cross[0]) + exchange(pick(core, cross[0], cross[1]), core_step)
    part = sum_over(part, [far_step, first_step] + grid_steps)
    other_part = exchange(part, core_step)
    return call(
        lambda *refs: root_kernel(scale, chunk, *refs),
        "root",
        rows,
        kept, other, part, other_part, start_root.T, lower, upper,
        limit=16 * MIB,
    )


def solution(mesh):
    in_specs = (P("grid", "snap"), P("snap", None), P(), P())
    out_specs = P(("grid", "snap"), None)
    return jax.shard_map(
        on_device, mesh=mesh, in_specs=in_specs, out_specs=out_specs, check_vma=False
    )
```

```python
import jax
import jax.numpy as jnp
from jax import lax
from jax.experimental import pallas as pl
from jax.experimental.pallas import tpu as pltpu
from jax.sharding import PartitionSpec as P


POWER = 2
NEWTON = 8
F32 = jnp.float32
BF16 = jnp.bfloat16
MIB = 2**20


def exchange(value, step):
    axis, bit = step
    mask = 2**bit
    pairs = [(source, source ^ mask) for source in range(lax.axis_size(axis))]
    return lax.ppermute(value, axis, pairs)


def bit_of(step):
    axis, bit = step
    return (lax.axis_index(axis) // 2**bit) % 2


def pick(flag, if_set, if_clear):
    return jnp.where(flag == 1, if_set, if_clear)


def axis_steps(axis):
    return [(axis, bit) for bit in range(lax.axis_size(axis).bit_length() - 1)]


def sum_over(value, steps):
    for step in steps:
        value = value + exchange(value, step)
    return value


def split(x):
    high = x.astype(BF16)
    return high, (x - high.astype(F32)).astype(BF16)


def product(a, b, transposed=False):
    return lax.dot_general(
        a, b, (((1,), (1 if transposed else 0,)), ((), ())), preferred_element_type=F32
    )


def inner_product(left, right):
    return lax.dot_general(
        left, right, (((0,), (0,)), ((), ())), preferred_element_type=F32
    )


def subspace_steps(gram, basis, count):
    gram_high, gram_low = split(gram)
    rank = basis.shape[0]
    rows = lax.broadcasted_iota(jnp.int32, (rank, rank), 0)
    columns = lax.broadcasted_iota(jnp.int32, (rank, rank), 1)
    identity = (rows == columns).astype(F32)

    def times_right(x, right):
        out = product(jnp.concatenate(split(x), axis=1), right)
        return out[:, :rank] + out[:, rank:]

    for _ in range(count):
        high, low = split(basis)
        out = product(jnp.concatenate([high, low], axis=0), gram_high)
        image = out[:rank] + out[rank:] + product(high, gram_low)
        image = image * lax.rsqrt(jnp.sum(image * image) + 1e-06)
        image_high, image_low = split(image)
        stacked = jnp.concatenate([image_high, image_low], axis=0)
        out = product(stacked, stacked, transposed=True)
        inner = out[:rank, :rank] + out[:rank, rank:] + out[rank:, :rank]
        total = None
        for step in range(NEWTON):
            factor = 1.5 * identity - 0.5 * inner
            row = jnp.concatenate(split(factor), axis=1)
            right = jnp.concatenate([row, row], axis=0)
            if step < NEWTON - 1:
                inner = times_right(times_right(inner, right), right)
            total = factor if total is None else times_right(total, right)
        total_high, total_low = split(total)
        basis = product(
            jnp.concatenate([total_high, total_low], axis=1),
            jnp.concatenate([image_high, image_high], axis=0),
        ) + product(total_high, image_low)
    return basis


def kept_gram(rotation, gram):
    gram_high, gram_low = split(gram)
    image = product(rotation, gram_high) + product(rotation, gram_low)
    high, low = split(image)
    return product(high, rotation, True) + product(low, rotation, True)


def pack(gram):
    size = gram.shape[0] // 2
    rows = lax.broadcasted_iota(jnp.int32, (size, size), 0)
    columns = lax.broadcasted_iota(jnp.int32, (size, size), 1)
    first, second = gram[:size, :size], gram[size:, size:]
    diagonal = jnp.sum(jnp.where(rows == columns, second, 0.0), axis=0, keepdims=True)
    diagonal = jnp.broadcast_to(diagonal, (8, size))
    low = jnp.concatenate([jnp.where(rows <= columns, first, second), diagonal], axis=0)
    high = jnp.concatenate([gram[:size, size:], diagonal], axis=0)
    return low, high


def unpack(low, high):
    size = low.shape[1]
    rows = lax.broadcasted_iota(jnp.int32, (size, size), 0)
    columns = lax.broadcasted_iota(jnp.int32, (size, size), 1)
    both, cross = low[:size], high[:size]
    flipped = both.T
    first = jnp.where(rows <= columns, both, flipped)
    second = jnp.where(rows > columns, both, flipped)
    diagonal = jnp.broadcast_to(low[size : size + 1], (size, size))
    second = jnp.where(rows == columns, diagonal, second)
    top = jnp.concatenate([first, cross], axis=1)
    return jnp.concatenate([top, jnp.concatenate([cross.T, second], axis=1)], axis=0)


def place_kernel(rows_ref, own_ref, far_ref, near_ref, corner_ref, semaphores):
    core, far = bit_of(("snap", 0)), bit_of(("snap", 1))
    places = (2 * far + core, 2 - 2 * far + core, 2 * far + 1 - core, 3 - 2 * far - core)
    targets = (own_ref, far_ref, near_ref, corner_ref)
    copies = [
        pltpu.make_async_copy(rows_ref.at[place], target, semaphores.at[number])
        for number, (place, target) in enumerate(zip(places, targets))
    ]
    for copy in copies:
        copy.start()
    for copy in copies:
        copy.wait()


def first_leaf_kernel(scale, side_step, kept_ref, other_ref, start_ref, gram_ref, basis_ref):
    side = bit_of(side_step) == 1
    kept, other = kept_ref[...], other_ref[...]
    low = jnp.where(side, other, kept)
    high = jnp.where(side, kept, other)
    gram = unpack(low, high) * scale
    gram_ref[...] = gram
    basis_ref[...] = subspace_steps(gram, start_ref[...], 1)


def last_leaf_kernel(gram_ref, basis_ref, out_ref):
    gram = gram_ref[...]
    rank = basis_ref.shape[0]
    rotation = subspace_steps(gram, basis_ref[...], POWER - 1).astype(BF16)
    out_ref[:rank] = rotation
    out_ref[rank:] = jnp.concatenate(split(kept_gram(rotation, gram)), axis=1)


def pair_kernel(
    scale, own_ref, other_ref, own_slab_ref, other_slab_ref, start_ref, out_ref, kept_ref
):
    core = bit_of(("snap", 0)) == 1
    rank = start_ref.shape[0]
    own, other = own_ref[...].astype(F32), other_ref[...].astype(F32)
    first, second = jnp.where(core, other, own), jnp.where(core, own, other)
    own = jnp.concatenate([own_slab_ref[0], own_slab_ref[1]], axis=1)
    other = jnp.concatenate([other_slab_ref[0], other_slab_ref[1]], axis=1)
    cross = jnp.concatenate([jnp.where(core, other, own), jnp.where(core, own, other)], axis=0)
    cross_high, cross_low = split(cross * scale)
    first_rotation, second_rotation = first[:rank].astype(BF16), second[:rank].astype(BF16)
    image = product(first_rotation, cross_high) + product(first_rotation, cross_low)
    high, low = split(image)
    cross = product(high, second_rotation, True) + product(low, second_rotation, True)
    first, second = first[rank:], second[rank:]
    top = jnp.concatenate([first[:, :rank] + first[:, rank:], cross], axis=1)
    bottom = jnp.concatenate([cross.T, second[:, :rank] + second[:, rank:]], axis=1)
    gram = jnp.concatenate([top, bottom], axis=0)
    rotation = subspace_steps(gram, start_ref[...], POWER).astype(BF16)
    out_ref[...] = rotation
    kept_ref[...] = kept_gram(rotation, gram)


def branch_kernel(
    chunk, own_ref, near_ref, far_ref, corner_ref, leaves_ref, far_leaves_ref,
    rotation_ref, far_rotation_ref, lower_ref, upper_ref,
):
    core = bit_of(("snap", 0)) == 1
    high_bit = bit_of(("snap", 1)) == 1
    rank = rotation_ref.shape[0]

    def halves(ref):
        value = ref[...].astype(F32)
        left, right = value[:, :rank], value[:, rank:]
        own, other = jnp.where(core, right, left), jnp.where(core, left, right)
        return own.astype(BF16), other.astype(BF16)

    def branch(refs, leaves, parts, rows):
        total = None
        for number, (ref, part) in enumerate(zip(refs, parts)):
            leaf = product(ref[rows], leaves[number * rank : (number + 1) * rank], True)
            term = product(leaf.astype(BF16), part, True)
            total = term if total is None else total + term
        return total

    leaves, far_leaves = leaves_ref[...], far_leaves_ref[...]
    parts, far_parts = halves(rotation_ref), halves(far_rotation_ref)
    for start in range(0, own_ref.shape[0], chunk):
        rows = pl.ds(start, chunk)
        mine = branch((own_ref, near_ref), leaves, parts, rows)
        theirs = branch((far_ref, corner_ref), far_leaves, far_parts, rows)
        lower_ref[rows] = jnp.where(high_bit, theirs, mine).astype(BF16)
        upper_ref[rows] = jnp.where(high_bit, mine, theirs).astype(BF16)


def root_kernel(
    scale, chunk, kept_ref, other_ref, own_cross_ref, other_cross_ref, start_ref,
    lower_ref, upper_ref, out_ref,
):
    core = bit_of(("snap", 0)) == 1
    high_bit = bit_of(("snap", 1)) == 1
    kept, other = kept_ref[...], other_ref[...]
    own_cross, other_cross = own_cross_ref[...], other_cross_ref[...]
    cross = jnp.concatenate(
        [jnp.where(core, other_cross, own_cross), jnp.where(core, own_cross, other_cross)], axis=0
    ) * scale
    top = jnp.concatenate([jnp.where(high_bit, other, kept), cross], axis=1)
    bottom = jnp.concatenate([cross.T, jnp.where(high_bit, kept, other)], axis=1)
    gram = jnp.concatenate([top, bottom], axis=0)
    rotation = subspace_steps(gram, start_ref[...], POWER).astype(BF16)
    for start in range(0, lower_ref.shape[0], chunk):
        rows = pl.ds(start, chunk)
        root = jnp.concatenate([lower_ref[rows], upper_ref[rows]], axis=1)
        out_ref[rows] = product(root, rotation, True).astype(BF16)


def call(kernel, out_shape, *operands, microseconds=8, limit=8 * MIB):
    vmem = pl.BlockSpec(memory_space=pltpu.VMEM)
    return pl.pallas_call(
        kernel,
        out_shape=out_shape,
        in_specs=[vmem] * len(operands),
        out_specs=jax.tree.map(lambda _: vmem, out_shape),
        compiler_params=pltpu.CompilerParams(vmem_limit_bytes=limit),
        cost_estimate=pl.CostEstimate(
            flops=microseconds * 10**9, bytes_accessed=MIB, transcendentals=0
        ),
    )(*operands)


def on_device(fields, start_local, start_pair, start_root):
    local_rows, snaps = fields.shape
    rank = start_local.shape[1]
    quarter = local_rows // 4
    chunk = quarter // 4
    scale = 1.0 / (local_rows * lax.axis_size("grid"))
    core_step, far_step = ("snap", 0), ("snap", 1)
    core, far = bit_of(core_step), bit_of(far_step)
    first_step, *grid_steps = axis_steps("grid")
    side = bit_of(first_step)

    rows = jax.ShapeDtypeStruct((quarter, snaps), fields.dtype)
    own_rows, far_sent, near_sent, corner_sent = pl.pallas_call(
        place_kernel,
        out_shape=(rows,) * 4,
        in_specs=[pl.BlockSpec(memory_space=pltpu.HBM)],
        out_specs=(pl.BlockSpec(memory_space=pltpu.VMEM),) * 4,
        scratch_shapes=[pltpu.SemaphoreType.DMA((4,))],
        name="place",
        compiler_params=pltpu.CompilerParams(vmem_limit_bytes=8 * MIB),
    )(fields.reshape(4, quarter, snaps))
    near_rows = exchange(near_sent, core_step)
    far_core_rows = exchange(corner_sent, core_step)
    far_rows = exchange(far_sent, far_step)
    corner_rows = exchange(far_core_rows, far_step)

    gram = sum(inner_product(x, x) for x in (own_rows, far_sent, near_sent, corner_sent))
    low, high = pack(gram)
    kept = pick(side, high, low) + exchange(pick(side, low, high), first_step)
    kept = sum_over(kept, grid_steps)
    other = exchange(kept, first_step)

    cross = inner_product(own_rows, near_rows) + inner_product(far_sent, far_core_rows)
    cross = pick(core, cross.T, cross).reshape(2, rank, 2, rank)
    slab = pick(core, cross[1], cross[0])
    slab = slab + exchange(pick(core, cross[0], cross[1]), core_step)
    left, right = slab[:, 0], slab[:, 1]
    part = pick(side, right, left) + exchange(pick(side, left, right), first_step)
    part = sum_over(part, grid_steps)
    other_part = exchange(part, first_step)
    slab = jnp.stack([pick(side, other_part, part), pick(side, part, other_part)])
    other_slab = exchange(slab, core_step)

    square = jax.ShapeDtypeStruct((rank, rank), F32)
    gram, basis = call(
        lambda *refs: first_leaf_kernel(scale, first_step, *refs),
        (jax.ShapeDtypeStruct((snaps, snaps), F32), jax.ShapeDtypeStruct((rank, snaps), F32)),
        kept, other, start_local.T,
        microseconds=3,
    )
    leaf = call(
        last_leaf_kernel,
        jax.ShapeDtypeStruct((2 * rank, snaps), BF16),
        gram, basis,
        microseconds=4,
    )
    other_leaf = exchange(leaf, core_step)
    leaves = jnp.concatenate([leaf[:rank], other_leaf[:rank]], axis=0)
    far_leaves = exchange(leaves, far_step)

    start = lax.dynamic_index_in_dim(start_pair, far, 0, keepdims=False)
    rotation, kept = call(
        lambda *refs: pair_kernel(scale, *refs),
        (jax.ShapeDtypeStruct((rank, 2 * rank), BF16), square),
        leaf, other_leaf, slab, other_slab, start.T,
    )
    far_rotation = exchange(rotation, far_step)
    other = exchange(kept, far_step)
    rows = jax.ShapeDtypeStruct((quarter, rank), BF16)
    lower, upper = call(
        lambda *refs: branch_kernel(chunk, *refs),
        (rows, rows),
        own_rows, near_rows, far_rows, corner_rows, leaves, far_leaves, rotation, far_rotation,
        microseconds=1, limit=16 * MIB,
    )
    cross = inner_product(lower, upper).reshape(2, rank // 2, rank)
    part = pick(core, cross[1], cross[0])
    part = part + exchange(pick(core, cross[0], cross[1]), core_step)
    part = sum_over(part, [far_step, first_step] + grid_steps)
    other_part = exchange(part, core_step)
    return call(
        lambda *refs: root_kernel(scale, chunk, *refs),
        rows,
        kept, other, part, other_part, start_root.T, lower, upper,
        limit=16 * MIB,
    )


def solution(mesh):
    in_specs = (P("grid", "snap"), P("snap", None), P(), P())
    out_specs = P(("grid", "snap"), None)
    return jax.shard_map(
        on_device, mesh=mesh, in_specs=in_specs, out_specs=out_specs, check_vma=False
    )
```

```python
import jax
import jax.numpy as jnp
from jax import lax
from jax.experimental import pallas as pl
from jax.experimental.pallas import tpu as pltpu
from jax.sharding import PartitionSpec as P


POWER = 2
NEWTON = 8
F32 = jnp.float32
BF16 = jnp.bfloat16
MIB = 2**20


def permute(value, steps):
    axes = tuple(axis for axis in ("grid", "snap") if any(axis == on for on, _ in steps))
    places = [0]
    for axis in axes:
        mask = sum(2**bit for on, bit in steps if on == axis)
        size = lax.axis_size(axis)
        places = [place * size + (own ^ mask) for place in places for own in range(size)]
    pairs = list(enumerate(places))
    return lax.ppermute(value, axes, pairs)


def exchange(value, step):
    return permute(value, [step])


def bit_of(step):
    axis, bit = step
    return (lax.axis_index(axis) // 2**bit) % 2


def pick(flag, if_set, if_clear):
    return jnp.where(flag == 1, if_set, if_clear)


def axis_steps(axis):
    return [(axis, bit) for bit in range(lax.axis_size(axis).bit_length() - 1)]


def sum_over(value, steps):
    for step in steps:
        value = value + exchange(value, step)
    return value


def sum_everywhere(value, through, steps):
    value = value + exchange(value, through)
    for start in range(0, len(steps), 2):
        group = steps[start : start + 2]
        hops = [[step, through] for step in group]
        if len(group) == 2:
            hops.append(group)
        received = [permute(value, hop) for hop in hops]
        value = value + sum(received[1:], received[0])
    return value


def split(x):
    high = x.astype(BF16)
    return high, (x - high.astype(F32)).astype(BF16)


def product(a, b, transposed=False):
    return lax.dot_general(
        a, b, (((1,), (1 if transposed else 0,)), ((), ())), preferred_element_type=F32
    )


def inner_product(left, right):
    return lax.dot_general(
        left, right, (((0,), (0,)), ((), ())), preferred_element_type=F32
    )


def subspace_steps(gram, basis, count):
    gram_high, gram_low = split(gram)
    rank = basis.shape[0]
    rows = lax.broadcasted_iota(jnp.int32, (rank, rank), 0)
    columns = lax.broadcasted_iota(jnp.int32, (rank, rank), 1)
    identity = (rows == columns).astype(F32)

    def times_right(x, right):
        out = product(jnp.concatenate(split(x), axis=1), right)
        return out[:, :rank] + out[:, rank:]

    for _ in range(count):
        high, low = split(basis)
        out = product(jnp.concatenate([high, low], axis=0), gram_high)
        image = out[:rank] + out[rank:] + product(high, gram_low)
        image = image * lax.rsqrt(jnp.sum(image * image) + 1e-06)
        image_high, image_low = split(image)
        stacked = jnp.concatenate([image_high, image_low], axis=0)
        out = product(stacked, stacked, transposed=True)
        inner = out[:rank, :rank] + out[:rank, rank:] + out[rank:, :rank]
        total = None
        for step in range(NEWTON):
            factor = 1.5 * identity - 0.5 * inner
            row = jnp.concatenate(split(factor), axis=1)
            right = jnp.concatenate([row, row], axis=0)
            if step < NEWTON - 1:
                inner = times_right(times_right(inner, right), right)
            total = factor if total is None else times_right(total, right)
        total_high, total_low = split(total)
        basis = product(
            jnp.concatenate([total_high, total_low], axis=1),
            jnp.concatenate([image_high, image_high], axis=0),
        ) + product(total_high, image_low)
    return basis


def kept_gram(rotation, gram):
    gram_high, gram_low = split(gram)
    image = product(rotation, gram_high) + product(rotation, gram_low)
    high, low = split(image)
    return product(high, rotation, True) + product(low, rotation, True)


def pack(gram):
    size = gram.shape[0] // 2
    rows = lax.broadcasted_iota(jnp.int32, (size, size), 0)
    columns = lax.broadcasted_iota(jnp.int32, (size, size), 1)
    first, second = gram[:size, :size], gram[size:, size:]
    diagonal = jnp.sum(jnp.where(rows == columns, second, 0.0), axis=0, keepdims=True)
    diagonal = jnp.broadcast_to(diagonal, (8, size))
    low = jnp.concatenate([jnp.where(rows <= columns, first, second), diagonal], axis=0)
    high = jnp.concatenate([gram[:size, size:], diagonal], axis=0)
    return low, high


def unpack(low, high):
    size = low.shape[1]
    rows = lax.broadcasted_iota(jnp.int32, (size, size), 0)
    columns = lax.broadcasted_iota(jnp.int32, (size, size), 1)
    both, cross = low[:size], high[:size]
    flipped = both.T
    first = jnp.where(rows <= columns, both, flipped)
    second = jnp.where(rows > columns, both, flipped)
    diagonal = jnp.broadcast_to(low[size : size + 1], (size, size))
    second = jnp.where(rows == columns, diagonal, second)
    top = jnp.concatenate([first, cross], axis=1)
    return jnp.concatenate([top, jnp.concatenate([cross.T, second], axis=1)], axis=0)


def place_kernel(rows_ref, own_ref, far_ref, near_ref, corner_ref, semaphores):
    core, far = bit_of(("snap", 0)), bit_of(("snap", 1))
    places = (2 * far + core, 2 - 2 * far + core, 2 * far + 1 - core, 3 - 2 * far - core)
    targets = (own_ref, far_ref, near_ref, corner_ref)
    copies = [
        pltpu.make_async_copy(rows_ref.at[place], target, semaphores.at[number])
        for number, (place, target) in enumerate(zip(places, targets))
    ]
    for copy in copies:
        copy.start()
    for copy in copies:
        copy.wait()


def turn_kernel(local_ref, pair_ref, root_ref, *turned_refs):
    far = bit_of(("snap", 1))
    turned_refs[0][...] = local_ref[...].T
    turned_refs[1][...] = pair_ref[far].T
    turned_refs[2][...] = root_ref[...].T


def orient_kernel(cross_ref, kept_ref, sent_ref):
    core = bit_of(("snap", 0)) == 1
    rank = kept_ref.shape[0]
    cross = cross_ref[...]
    turned = cross.T
    kept_ref[...] = jnp.where(core, turned[rank:], cross[:rank])
    sent_ref[...] = jnp.where(core, turned[:rank], cross[rank:])


def first_leaf_kernel(scale, side_step, kept_ref, other_ref, start_ref, gram_ref, basis_ref):
    side = bit_of(side_step) == 1
    kept, other = kept_ref[...], other_ref[...]
    low = jnp.where(side, other, kept)
    high = jnp.where(side, kept, other)
    gram = unpack(low, high) * scale
    gram_ref[...] = gram
    basis_ref[...] = subspace_steps(gram, start_ref[...], 1)


def last_leaf_kernel(gram_ref, basis_ref, out_ref):
    gram = gram_ref[...]
    rank = basis_ref.shape[0]
    rotation = subspace_steps(gram, basis_ref[...], POWER - 1).astype(BF16)
    out_ref[:rank] = rotation
    out_ref[rank:] = jnp.concatenate(split(kept_gram(rotation, gram)), axis=1)


def pair_kernel(
    scale, own_ref, other_ref, own_slab_ref, other_slab_ref, start_ref, out_ref, kept_ref
):
    core = bit_of(("snap", 0)) == 1
    rank = start_ref.shape[0]
    own, other = own_ref[...].astype(F32), other_ref[...].astype(F32)
    first, second = jnp.where(core, other, own), jnp.where(core, own, other)
    own, other = own_slab_ref[...], other_slab_ref[...]
    cross = jnp.concatenate([jnp.where(core, other, own), jnp.where(core, own, other)], axis=0)
    cross_high, cross_low = split(cross * scale)
    first_rotation, second_rotation = first[:rank].astype(BF16), second[:rank].astype(BF16)
    image = product(first_rotation, cross_high) + product(first_rotation, cross_low)
    high, low = split(image)
    cross = product(high, second_rotation, True) + product(low, second_rotation, True)
    first, second = first[rank:], second[rank:]
    top = jnp.concatenate([first[:, :rank] + first[:, rank:], cross], axis=1)
    bottom = jnp.concatenate([cross.T, second[:, :rank] + second[:, rank:]], axis=1)
    gram = jnp.concatenate([top, bottom], axis=0)
    rotation = subspace_steps(gram, start_ref[...], POWER).astype(BF16)
    out_ref[...] = rotation
    kept_ref[...] = kept_gram(rotation, gram)


def branch_kernel(
    chunk, own_ref, near_ref, far_ref, corner_ref, leaves_ref, far_leaves_ref,
    rotation_ref, far_rotation_ref, lower_ref, upper_ref,
):
    core = bit_of(("snap", 0)) == 1
    high_bit = bit_of(("snap", 1)) == 1
    rank = rotation_ref.shape[0]

    def halves(ref):
        value = ref[...].astype(F32)
        left, right = value[:, :rank], value[:, rank:]
        own, other = jnp.where(core, right, left), jnp.where(core, left, right)
        return own.astype(BF16), other.astype(BF16)

    def rotations(leaves, parts):
        return [
            product(part, leaves[number * rank : (number + 1) * rank]).astype(BF16)
            for number, part in enumerate(parts)
        ]

    own, near = rotations(leaves_ref[...], halves(rotation_ref))
    far, corner = rotations(far_leaves_ref[...], halves(far_rotation_ref))
    for start in range(0, own_ref.shape[0], chunk):
        rows = pl.ds(start, chunk)
        mine = product(own_ref[rows], own, True) + product(near_ref[rows], near, True)
        theirs = product(far_ref[rows], far, True) + product(corner_ref[rows], corner, True)
        lower_ref[rows] = jnp.where(high_bit, theirs, mine).astype(BF16)
        upper_ref[rows] = jnp.where(high_bit, mine, theirs).astype(BF16)


def root_kernel(
    scale, chunk, kept_ref, other_ref, cross_ref, start_ref, lower_ref, upper_ref, out_ref
):
    high_bit = bit_of(("snap", 1)) == 1
    kept, other = kept_ref[...], other_ref[...]
    cross = cross_ref[...] * scale
    top = jnp.concatenate([jnp.where(high_bit, other, kept), cross], axis=1)
    bottom = jnp.concatenate([cross.T, jnp.where(high_bit, kept, other)], axis=1)
    gram = jnp.concatenate([top, bottom], axis=0)
    rotation = subspace_steps(gram, start_ref[...], POWER).astype(BF16)
    for start in range(0, lower_ref.shape[0], chunk):
        rows = pl.ds(start, chunk)
        root = jnp.concatenate([lower_ref[rows], upper_ref[rows]], axis=1)
        out_ref[rows] = product(root, rotation, True).astype(BF16)


def call(kernel, out_shape, *operands, microseconds=8, limit=8 * MIB):
    vmem = pl.BlockSpec(memory_space=pltpu.VMEM)
    return pl.pallas_call(
        kernel,
        out_shape=out_shape,
        in_specs=[vmem] * len(operands),
        out_specs=jax.tree.map(lambda _: vmem, out_shape),
        compiler_params=pltpu.CompilerParams(vmem_limit_bytes=limit),
        cost_estimate=pl.CostEstimate(
            flops=microseconds * 10**9, bytes_accessed=MIB, transcendentals=0
        ),
    )(*operands)


def on_device(fields, start_local, start_pair, start_root):
    local_rows, snaps = fields.shape
    rank = start_local.shape[1]
    quarter = local_rows // 4
    chunk = quarter // 4
    scale = 1.0 / (local_rows * lax.axis_size("grid"))
    core_step, far_step = ("snap", 0), ("snap", 1)
    first_step, *grid_steps = axis_steps("grid")
    side = bit_of(first_step)

    rows = jax.ShapeDtypeStruct((quarter, snaps), fields.dtype)
    own_rows, far_sent, near_sent, corner_sent = pl.pallas_call(
        place_kernel,
        out_shape=(rows,) * 4,
        in_specs=[pl.BlockSpec(memory_space=pltpu.HBM)],
        out_specs=(pl.BlockSpec(memory_space=pltpu.VMEM),) * 4,
        scratch_shapes=[pltpu.SemaphoreType.DMA((4,))],
        name="place",
        compiler_params=pltpu.CompilerParams(vmem_limit_bytes=8 * MIB),
    )(fields.reshape(4, quarter, snaps))
    near_rows = exchange(near_sent, core_step)
    far_core_rows = exchange(corner_sent, core_step)
    far_rows = exchange(far_sent, far_step)
    corner_rows = exchange(far_core_rows, far_step)

    gram = sum(inner_product(x, x) for x in (own_rows, far_sent, near_sent, corner_sent))
    low, high = pack(gram)
    kept = pick(side, high, low) + exchange(pick(side, low, high), first_step)
    kept = sum_over(kept, grid_steps)
    other = exchange(kept, first_step)

    cross = inner_product(own_rows, near_rows) + inner_product(far_sent, far_core_rows)
    half = jax.ShapeDtypeStruct((rank, snaps), F32)
    slab, slab_sent = call(orient_kernel, (half, half), cross, microseconds=1)
    slab = slab + exchange(slab_sent, core_step)
    slab = sum_over(slab, [first_step] + grid_steps)
    other_slab = exchange(slab, core_step)

    turned = jax.ShapeDtypeStruct((rank, snaps), F32)
    turned_pair = jax.ShapeDtypeStruct((rank, 2 * rank), F32)
    local_basis, pair_basis, root_basis = call(
        turn_kernel, (turned, turned_pair, turned_pair),
        start_local, start_pair, start_root,
        microseconds=1,
    )
    square = jax.ShapeDtypeStruct((rank, rank), F32)
    gram, basis = call(
        lambda *refs: first_leaf_kernel(scale, first_step, *refs),
        (jax.ShapeDtypeStruct((snaps, snaps), F32), jax.ShapeDtypeStruct((rank, snaps), F32)),
        kept, other, local_basis,
        microseconds=3,
    )
    leaf = call(
        last_leaf_kernel,
        jax.ShapeDtypeStruct((2 * rank, snaps), BF16),
        gram, basis,
        microseconds=4,
    )
    other_leaf = exchange(leaf, core_step)
    leaves = jnp.concatenate([leaf[:rank], other_leaf[:rank]], axis=0)
    far_leaves = exchange(leaves, far_step)

    rotation, kept = call(
        lambda *refs: pair_kernel(scale, *refs),
        (jax.ShapeDtypeStruct((rank, 2 * rank), BF16), square),
        leaf, other_leaf, slab, other_slab, pair_basis,
    )
    far_rotation = exchange(rotation, far_step)
    other = exchange(kept, far_step)
    rows = jax.ShapeDtypeStruct((quarter, rank), BF16)
    lower, upper = call(
        lambda *refs: branch_kernel(chunk, *refs),
        (rows, rows),
        own_rows, near_rows, far_rows, corner_rows, leaves, far_leaves, rotation, far_rotation,
        microseconds=1, limit=16 * MIB,
    )
    cross = sum_everywhere(
        inner_product(lower, upper), core_step, [far_step, first_step] + grid_steps
    )
    return call(
        lambda *refs: root_kernel(scale, chunk, *refs),
        rows,
        kept, other, cross, root_basis, lower, upper,
        limit=16 * MIB,
    )


def solution(mesh):
    in_specs = (P("grid", "snap"), P("snap", None), P(), P())
    out_specs = P(("grid", "snap"), None)
    return jax.shard_map(
        on_device, mesh=mesh, in_specs=in_specs, out_specs=out_specs, check_vma=False
    )
```

```python
import jax
import jax.numpy as jnp
from jax import lax
from jax.experimental import pallas as pl
from jax.experimental.pallas import tpu as pltpu
from jax.sharding import PartitionSpec as P


POWER = 2
NEWTON = 8
F32 = jnp.float32
BF16 = jnp.bfloat16
MIB = 2**20


def permute(value, steps):
    axes = tuple(axis for axis in ("grid", "snap") if any(axis == on for on, _ in steps))
    places = [0]
    for axis in axes:
        mask = sum(2**bit for on, bit in steps if on == axis)
        size = lax.axis_size(axis)
        places = [place * size + (own ^ mask) for place in places for own in range(size)]
    pairs = list(enumerate(places))
    return lax.ppermute(value, axes, pairs)


def exchange(value, step):
    return permute(value, [step])


def bit_of(step):
    axis, bit = step
    return (lax.axis_index(axis) // 2**bit) % 2


def axis_steps(axis):
    return [(axis, bit) for bit in range(lax.axis_size(axis).bit_length() - 1)]


def sum_over(value, steps):
    for step in steps:
        value = value + exchange(value, step)
    return value


def sum_everywhere(value, through, steps):
    value = value + exchange(value, through)
    for start in range(0, len(steps), 2):
        group = steps[start : start + 2]
        hops = [[step, through] for step in group]
        if len(group) == 2:
            hops.append(group)
        received = [permute(value, hop) for hop in hops]
        value = value + sum(received[1:], received[0])
    return value


def split(x):
    high = x.astype(BF16)
    return high, (x - high.astype(F32)).astype(BF16)


def product(a, b, transposed=False):
    return lax.dot_general(
        a, b, (((1,), (1 if transposed else 0,)), ((), ())), preferred_element_type=F32
    )


def inner_product(left, right):
    return lax.dot_general(
        left, right, (((0,), (0,)), ((), ())), preferred_element_type=F32
    )


def subspace_steps(gram, basis, count):
    gram_high, gram_low = split(gram)
    rank = basis.shape[0]
    rows = lax.broadcasted_iota(jnp.int32, (rank, rank), 0)
    columns = lax.broadcasted_iota(jnp.int32, (rank, rank), 1)
    identity = (rows == columns).astype(F32)

    def times_right(x, right):
        out = product(jnp.concatenate(split(x), axis=1), right)
        return out[:, :rank] + out[:, rank:]

    for _ in range(count):
        high, low = split(basis)
        out = product(jnp.concatenate([high, low], axis=0), gram_high)
        image = out[:rank] + out[rank:] + product(high, gram_low)
        image = image * lax.rsqrt(jnp.sum(image * image) + 1e-06)
        image_high, image_low = split(image)
        stacked = jnp.concatenate([image_high, image_low], axis=0)
        out = product(stacked, stacked, transposed=True)
        inner = out[:rank, :rank] + out[:rank, rank:] + out[rank:, :rank]
        total = None
        for step in range(NEWTON):
            factor = 1.5 * identity - 0.5 * inner
            row = jnp.concatenate(split(factor), axis=1)
            right = jnp.concatenate([row, row], axis=0)
            if step < NEWTON - 1:
                inner = times_right(times_right(inner, right), right)
            total = factor if total is None else times_right(total, right)
        total_high, total_low = split(total)
        basis = product(
            jnp.concatenate([total_high, total_low], axis=1),
            jnp.concatenate([image_high, image_high], axis=0),
        ) + product(total_high, image_low)
    return basis


def kept_gram(rotation, gram):
    gram_high, gram_low = split(gram)
    image = product(rotation, gram_high) + product(rotation, gram_low)
    high, low = split(image)
    return product(high, rotation, True) + product(low, rotation, True)


def pack(gram):
    size = gram.shape[0] // 2
    rows = lax.broadcasted_iota(jnp.int32, (size, size), 0)
    columns = lax.broadcasted_iota(jnp.int32, (size, size), 1)
    first, second = gram[:size, :size], gram[size:, size:]
    diagonal = jnp.sum(jnp.where(rows == columns, second, 0.0), axis=0, keepdims=True)
    diagonal = jnp.broadcast_to(diagonal, (8, size))
    low = jnp.concatenate([jnp.where(rows <= columns, first, second), diagonal], axis=0)
    high = jnp.concatenate([gram[:size, size:], diagonal], axis=0)
    return low, high


def unpack(low, high):
    size = low.shape[1]
    rows = lax.broadcasted_iota(jnp.int32, (size, size), 0)
    columns = lax.broadcasted_iota(jnp.int32, (size, size), 1)
    both, cross = low[:size], high[:size]
    flipped = both.T
    first = jnp.where(rows <= columns, both, flipped)
    second = jnp.where(rows > columns, both, flipped)
    diagonal = jnp.broadcast_to(low[size : size + 1], (size, size))
    second = jnp.where(rows == columns, diagonal, second)
    top = jnp.concatenate([first, cross], axis=1)
    return jnp.concatenate([top, jnp.concatenate([cross.T, second], axis=1)], axis=0)


def place_kernel(rows_ref, own_ref, far_ref, near_ref, corner_ref, semaphores):
    core, far = bit_of(("snap", 0)), bit_of(("snap", 1))
    places = (2 * far + core, 2 - 2 * far + core, 2 * far + 1 - core, 3 - 2 * far - core)
    targets = (own_ref, far_ref, near_ref, corner_ref)
    copies = [
        pltpu.make_async_copy(rows_ref.at[place], target, semaphores.at[number])
        for number, (place, target) in enumerate(zip(places, targets))
    ]
    for copy in copies:
        copy.start()
    for copy in copies:
        copy.wait()


def turn_kernel(local_ref, pair_ref, root_ref, *turned_refs):
    far = bit_of(("snap", 1))
    turned_refs[0][...] = local_ref[...].T
    turned_refs[1][...] = pair_ref[far].T
    turned_refs[2][...] = root_ref[...].T


def orient_kernel(cross_ref, kept_ref, sent_ref):
    core = bit_of(("snap", 0)) == 1
    rank = kept_ref.shape[0]
    cross = cross_ref[...]
    turned = cross.T
    kept_ref[...] = jnp.where(core, turned[rank:], cross[:rank])
    sent_ref[...] = jnp.where(core, turned[:rank], cross[rank:])


def pack_kernel(side_step, gram_ref, kept_ref, sent_ref):
    side = bit_of(side_step) == 1
    low, high = pack(gram_ref[...])
    kept_ref[...] = jnp.where(side, high, low)
    sent_ref[...] = jnp.where(side, low, high)


def leaf_kernel(scale, side_step, kept_ref, other_ref, start_ref, out_ref):
    side = bit_of(side_step) == 1
    kept, other = kept_ref[...], other_ref[...]
    low = jnp.where(side, other, kept)
    high = jnp.where(side, kept, other)
    gram = unpack(low, high) * scale
    rank = start_ref.shape[0]
    rotation = subspace_steps(gram, start_ref[...], POWER).astype(BF16)
    out_ref[:rank] = rotation
    out_ref[rank:] = jnp.concatenate(split(kept_gram(rotation, gram)), axis=1)


def pair_kernel(
    scale, own_ref, other_ref, own_slab_ref, other_slab_ref, start_ref, out_ref, kept_ref
):
    core = bit_of(("snap", 0)) == 1
    rank = start_ref.shape[0]
    own, other = own_ref[...].astype(F32), other_ref[...].astype(F32)
    first, second = jnp.where(core, other, own), jnp.where(core, own, other)
    own, other = own_slab_ref[...], other_slab_ref[...]
    cross = jnp.concatenate([jnp.where(core, other, own), jnp.where(core, own, other)], axis=0)
    cross_high, cross_low = split(cross * scale)
    first_rotation, second_rotation = first[:rank].astype(BF16), second[:rank].astype(BF16)
    image = product(first_rotation, cross_high) + product(first_rotation, cross_low)
    high, low = split(image)
    cross = product(high, second_rotation, True) + product(low, second_rotation, True)
    first, second = first[rank:], second[rank:]
    top = jnp.concatenate([first[:, :rank] + first[:, rank:], cross], axis=1)
    bottom = jnp.concatenate([cross.T, second[:, :rank] + second[:, rank:]], axis=1)
    gram = jnp.concatenate([top, bottom], axis=0)
    rotation = subspace_steps(gram, start_ref[...], POWER).astype(BF16)
    out_ref[...] = rotation
    kept_ref[...] = kept_gram(rotation, gram)


def branch_kernel(
    chunk, own_ref, near_ref, far_ref, corner_ref, leaves_ref, far_leaves_ref,
    rotation_ref, far_rotation_ref, lower_ref, upper_ref,
):
    core = bit_of(("snap", 0)) == 1
    high_bit = bit_of(("snap", 1)) == 1
    rank = rotation_ref.shape[0]

    def halves(ref):
        value = ref[...].astype(F32)
        left, right = value[:, :rank], value[:, rank:]
        own, other = jnp.where(core, right, left), jnp.where(core, left, right)
        return own.astype(BF16), other.astype(BF16)

    def rotations(leaves, parts):
        return [
            product(part, leaves[number * rank : (number + 1) * rank]).astype(BF16)
            for number, part in enumerate(parts)
        ]

    own, near = rotations(leaves_ref[...], halves(rotation_ref))
    far, corner = rotations(far_leaves_ref[...], halves(far_rotation_ref))
    for start in range(0, own_ref.shape[0], chunk):
        rows = pl.ds(start, chunk)
        mine = product(own_ref[rows], own, True) + product(near_ref[rows], near, True)
        theirs = product(far_ref[rows], far, True) + product(corner_ref[rows], corner, True)
        lower_ref[rows] = jnp.where(high_bit, theirs, mine).astype(BF16)
        upper_ref[rows] = jnp.where(high_bit, mine, theirs).astype(BF16)


def root_kernel(
    scale, chunk, kept_ref, other_ref, cross_ref, start_ref, lower_ref, upper_ref, out_ref
):
    high_bit = bit_of(("snap", 1)) == 1
    kept, other = kept_ref[...], other_ref[...]
    cross = cross_ref[...] * scale
    top = jnp.concatenate([jnp.where(high_bit, other, kept), cross], axis=1)
    bottom = jnp.concatenate([cross.T, jnp.where(high_bit, kept, other)], axis=1)
    gram = jnp.concatenate([top, bottom], axis=0)
    rotation = subspace_steps(gram, start_ref[...], POWER).astype(BF16)
    for start in range(0, lower_ref.shape[0], chunk):
        rows = pl.ds(start, chunk)
        root = jnp.concatenate([lower_ref[rows], upper_ref[rows]], axis=1)
        out_ref[rows] = product(root, rotation, True).astype(BF16)


def call(kernel, out_shape, *operands, microseconds=8, limit=8 * MIB):
    vmem = pl.BlockSpec(memory_space=pltpu.VMEM)
    return pl.pallas_call(
        kernel,
        out_shape=out_shape,
        in_specs=[vmem] * len(operands),
        out_specs=jax.tree.map(lambda _: vmem, out_shape),
        compiler_params=pltpu.CompilerParams(vmem_limit_bytes=limit),
        cost_estimate=pl.CostEstimate(
            flops=microseconds * 10**9, bytes_accessed=MIB, transcendentals=0
        ),
    )(*operands)


def on_device(fields, start_local, start_pair, start_root):
    local_rows, snaps = fields.shape
    rank = start_local.shape[1]
    quarter = local_rows // 4
    chunk = quarter // 4
    scale = 1.0 / (local_rows * lax.axis_size("grid"))
    core_step, far_step = ("snap", 0), ("snap", 1)
    first_step, *grid_steps = axis_steps("grid")

    rows = jax.ShapeDtypeStruct((quarter, snaps), fields.dtype)
    own_rows, far_sent, near_sent, corner_sent = pl.pallas_call(
        place_kernel,
        out_shape=(rows,) * 4,
        in_specs=[pl.BlockSpec(memory_space=pltpu.HBM)],
        out_specs=(pl.BlockSpec(memory_space=pltpu.VMEM),) * 4,
        scratch_shapes=[pltpu.SemaphoreType.DMA((4,))],
        name="place",
        compiler_params=pltpu.CompilerParams(vmem_limit_bytes=8 * MIB),
    )(fields.reshape(4, quarter, snaps))
    near_rows = exchange(near_sent, core_step)
    far_core_rows = exchange(corner_sent, core_step)
    far_rows = exchange(far_sent, far_step)
    corner_rows = exchange(far_core_rows, far_step)

    piece = jax.ShapeDtypeStruct((rank + 8, rank), F32)
    placed = (own_rows, far_sent, near_sent, corner_sent)
    kept, sent = call(
        lambda *refs: pack_kernel(first_step, *refs),
        (piece, piece), sum(inner_product(rows, rows) for rows in placed),
        microseconds=1, limit=2 * MIB,
    )
    kept = sum_over(kept + exchange(sent, first_step), grid_steps)
    other = exchange(kept, first_step)

    cross = inner_product(own_rows, near_rows) + inner_product(far_sent, far_core_rows)
    half = jax.ShapeDtypeStruct((rank, snaps), F32)
    slab, slab_sent = call(orient_kernel, (half, half), cross, microseconds=1)
    slab = slab + exchange(slab_sent, core_step)
    slab = sum_over(slab, [first_step] + grid_steps)
    other_slab = exchange(slab, core_step)

    turned = jax.ShapeDtypeStruct((rank, snaps), F32)
    turned_pair = jax.ShapeDtypeStruct((rank, 2 * rank), F32)
    local_basis, pair_basis, root_basis = call(
        turn_kernel, (turned, turned_pair, turned_pair),
        start_local, start_pair, start_root,
        microseconds=1,
    )
    square = jax.ShapeDtypeStruct((rank, rank), F32)
    leaf = call(
        lambda *refs: leaf_kernel(scale, first_step, *refs),
        jax.ShapeDtypeStruct((2 * rank, snaps), BF16),
        kept, other, local_basis,
    )
    other_leaf = exchange(leaf, core_step)
    leaves = jnp.concatenate([leaf[:rank], other_leaf[:rank]], axis=0)
    far_leaves = exchange(leaves, far_step)

    rotation, kept = call(
        lambda *refs: pair_kernel(scale, *refs),
        (jax.ShapeDtypeStruct((rank, 2 * rank), BF16), square),
        leaf, other_leaf, slab, other_slab, pair_basis,
    )
    far_rotation = exchange(rotation, far_step)
    other = exchange(kept, far_step)
    rows = jax.ShapeDtypeStruct((quarter, rank), BF16)
    lower, upper = call(
        lambda *refs: branch_kernel(chunk, *refs),
        (rows, rows),
        own_rows, near_rows, far_rows, corner_rows, leaves, far_leaves, rotation, far_rotation,
        microseconds=1, limit=16 * MIB,
    )
    cross = sum_everywhere(
        inner_product(lower, upper), core_step, [far_step, first_step] + grid_steps
    )
    return call(
        lambda *refs: root_kernel(scale, chunk, *refs),
        rows,
        kept, other, cross, root_basis, lower, upper,
        limit=16 * MIB,
    )


def solution(mesh):
    in_specs = (P("grid", "snap"), P("snap", None), P(), P())
    out_specs = P(("grid", "snap"), None)
    return jax.shard_map(
        on_device, mesh=mesh, in_specs=in_specs, out_specs=out_specs, check_vma=False
    )
```

```python
import jax
import jax.numpy as jnp
from jax import lax
from jax.experimental import pallas as pl
from jax.experimental.pallas import tpu as pltpu
from jax.sharding import PartitionSpec as P


POWER = 2
NEWTON = 8
F32 = jnp.float32
BF16 = jnp.bfloat16
MIB = 2**20


def permute(value, steps):
    axes = tuple(axis for axis in ("grid", "snap") if any(axis == on for on, _ in steps))
    places = [0]
    for axis in axes:
        mask = sum(2**bit for on, bit in steps if on == axis)
        size = lax.axis_size(axis)
        places = [place * size + (own ^ mask) for place in places for own in range(size)]
    pairs = list(enumerate(places))
    return lax.ppermute(value, axes, pairs)


def exchange(value, step):
    return permute(value, [step])


def bit_of(step):
    axis, bit = step
    return (lax.axis_index(axis) // 2**bit) % 2


def axis_steps(axis):
    return [(axis, bit) for bit in range(lax.axis_size(axis).bit_length() - 1)]


def sum_over(value, steps):
    for step in steps:
        sent = value.astype(BF16)
        received = exchange(sent, step)
        value = sent.astype(F32) + received.astype(F32)
    return value


def sum_everywhere(value, through, steps):
    value = sum_over(value, [through])
    for start in range(0, len(steps), 2):
        group = steps[start : start + 2]
        hops = [[step, through] for step in group]
        if len(group) == 2:
            hops.append(group)
        sent = value.astype(BF16)
        received = [permute(sent, hop) for hop in hops]
        value = sum((part.astype(F32) for part in received), sent.astype(F32))
    return value


def split(x):
    high = x.astype(BF16)
    return high, (x - high.astype(F32)).astype(BF16)


def product(a, b, transposed=False):
    return lax.dot_general(
        a, b, (((1,), (1 if transposed else 0,)), ((), ())), preferred_element_type=F32
    )


def inner_product(left, right):
    return lax.dot_general(
        left, right, (((0,), (0,)), ((), ())), preferred_element_type=F32
    )


def subspace_steps(gram, basis, count):
    gram_high, gram_low = split(gram)
    rank = basis.shape[0]
    rows = lax.broadcasted_iota(jnp.int32, (rank, rank), 0)
    columns = lax.broadcasted_iota(jnp.int32, (rank, rank), 1)
    identity = (rows == columns).astype(F32)

    def times_right(x, right):
        out = product(jnp.concatenate(split(x), axis=1), right)
        return out[:, :rank] + out[:, rank:]

    for _ in range(count):
        high, low = split(basis)
        out = product(jnp.concatenate([high, low], axis=0), gram_high)
        image = out[:rank] + out[rank:] + product(high, gram_low)
        image = image * lax.rsqrt(jnp.sum(image * image) + 1e-06)
        image_high, image_low = split(image)
        stacked = jnp.concatenate([image_high, image_low], axis=0)
        out = product(stacked, stacked, transposed=True)
        inner = out[:rank, :rank] + out[:rank, rank:] + out[rank:, :rank]
        total = None
        for step in range(NEWTON):
            factor = 1.5 * identity - 0.5 * inner
            row = jnp.concatenate(split(factor), axis=1)
            right = jnp.concatenate([row, row], axis=0)
            if step < NEWTON - 1:
                inner = times_right(times_right(inner, right), right)
            total = factor if total is None else times_right(total, right)
        total_high, total_low = split(total)
        basis = product(
            jnp.concatenate([total_high, total_low], axis=1),
            jnp.concatenate([image_high, image_high], axis=0),
        ) + product(total_high, image_low)
    return basis


def kept_gram(rotation, gram):
    gram_high, gram_low = split(gram)
    image = product(rotation, gram_high) + product(rotation, gram_low)
    high, low = split(image)
    return product(high, rotation, True) + product(low, rotation, True)


def pack(gram):
    size = gram.shape[0] // 2
    rows = lax.broadcasted_iota(jnp.int32, (size, size), 0)
    columns = lax.broadcasted_iota(jnp.int32, (size, size), 1)
    first, second = gram[:size, :size], gram[size:, size:]
    both = jnp.where(rows < columns, first, second)
    diagonals = [
        jnp.sum(jnp.where(rows == columns, block, 0.0), axis=0, keepdims=True)
        for block in (first, second)
    ]
    place = lax.broadcasted_iota(jnp.int32, (8, size), 0)
    diagonal = jnp.where(place < 4, *(jnp.broadcast_to(x, (8, size)) for x in diagonals))
    return encode(both, gram[:size, size:], diagonal)


def encode(both, cross, diagonal):
    high, low = split(diagonal)
    pieces = [both, cross, high.astype(F32), low.astype(F32)]
    return jnp.concatenate(pieces, axis=0).astype(BF16)


def decode(sent):
    size = sent.shape[1]
    value = sent.astype(F32)
    end = 2 * size
    return value[:size], value[size:end], value[end : end + 8] + value[end + 8 :]


def add_packed(one, other):
    return [x + y for x, y in zip(decode(one), decode(other))]


def unpack(both, cross, diagonal):
    size = both.shape[1]
    rows = lax.broadcasted_iota(jnp.int32, (size, size), 0)
    columns = lax.broadcasted_iota(jnp.int32, (size, size), 1)
    flipped = both.T

    def block(keep, row):
        row = jnp.broadcast_to(diagonal[row : row + 1], (size, size))
        return jnp.where(rows == columns, row, jnp.where(keep, both, flipped))

    top = jnp.concatenate([block(rows < columns, 0), cross], axis=1)
    bottom = jnp.concatenate([cross.T, block(rows > columns, 4)], axis=1)
    return jnp.concatenate([top, bottom], axis=0)


def place_kernel(rows_ref, own_ref, far_ref, near_ref, corner_ref, semaphores):
    core, far = bit_of(("snap", 0)), bit_of(("snap", 1))
    places = (2 * far + core, 2 - 2 * far + core, 2 * far + 1 - core, 3 - 2 * far - core)
    targets = (own_ref, far_ref, near_ref, corner_ref)
    copies = [
        pltpu.make_async_copy(rows_ref.at[place], target, semaphores.at[number])
        for number, (place, target) in enumerate(zip(places, targets))
    ]
    for copy in copies:
        copy.start()
    for copy in copies:
        copy.wait()


def turn_kernel(local_ref, pair_ref, root_ref, *turned_refs):
    far = bit_of(("snap", 1))
    turned_refs[0][...] = local_ref[...].T
    turned_refs[1][...] = pair_ref[far].T
    turned_refs[2][...] = root_ref[...].T


def orient_kernel(cross_ref, kept_ref, sent_ref):
    core = bit_of(("snap", 0)) == 1
    rank = kept_ref.shape[0]
    cross = cross_ref[...]
    turned = cross.T
    kept_ref[...] = jnp.where(core, turned[rank:], cross[:rank])
    sent_ref[...] = jnp.where(core, turned[:rank], cross[rank:])


def pack_kernel(gram_ref, sent_ref):
    sent_ref[...] = pack(gram_ref[...])


def merge_kernel(own_ref, received_ref, sent_ref):
    sent_ref[...] = encode(*add_packed(own_ref[...], received_ref[...]))


def leaf_kernel(scale, own_ref, received_ref, start_ref, out_ref):
    gram = unpack(*add_packed(own_ref[...], received_ref[...])) * scale
    rank = start_ref.shape[0]
    rotation = subspace_steps(gram, start_ref[...], POWER).astype(BF16)
    out_ref[:rank] = rotation
    out_ref[rank:] = jnp.concatenate(split(kept_gram(rotation, gram)), axis=1)


def pair_kernel(
    scale, own_ref, other_ref, own_slab_ref, other_slab_ref, start_ref, out_ref, kept_ref
):
    core = bit_of(("snap", 0)) == 1
    rank = start_ref.shape[0]
    own, other = own_ref[...].astype(F32), other_ref[...].astype(F32)
    first, second = jnp.where(core, other, own), jnp.where(core, own, other)
    own, other = own_slab_ref[...], other_slab_ref[...]
    cross = jnp.concatenate([jnp.where(core, other, own), jnp.where(core, own, other)], axis=0)
    cross_high, cross_low = split(cross * scale)
    first_rotation, second_rotation = first[:rank].astype(BF16), second[:rank].astype(BF16)
    image = product(first_rotation, cross_high) + product(first_rotation, cross_low)
    high, low = split(image)
    cross = product(high, second_rotation, True) + product(low, second_rotation, True)
    first, second = first[rank:], second[rank:]
    top = jnp.concatenate([first[:, :rank] + first[:, rank:], cross], axis=1)
    bottom = jnp.concatenate([cross.T, second[:, :rank] + second[:, rank:]], axis=1)
    gram = jnp.concatenate([top, bottom], axis=0)
    rotation = subspace_steps(gram, start_ref[...], POWER).astype(BF16)
    out_ref[...] = rotation
    kept_ref[...] = kept_gram(rotation, gram)


def branch_kernel(
    chunk, own_ref, near_ref, far_ref, corner_ref, leaves_ref, far_leaves_ref,
    rotation_ref, far_rotation_ref, lower_ref, upper_ref,
):
    core = bit_of(("snap", 0)) == 1
    high_bit = bit_of(("snap", 1)) == 1
    rank = rotation_ref.shape[0]

    def halves(ref):
        value = ref[...].astype(F32)
        left, right = value[:, :rank], value[:, rank:]
        own, other = jnp.where(core, right, left), jnp.where(core, left, right)
        return own.astype(BF16), other.astype(BF16)

    def rotations(leaves, parts):
        return [
            product(part, leaves[number * rank : (number + 1) * rank]).astype(BF16)
            for number, part in enumerate(parts)
        ]

    own, near = rotations(leaves_ref[...], halves(rotation_ref))
    far, corner = rotations(far_leaves_ref[...], halves(far_rotation_ref))
    for start in range(0, own_ref.shape[0], chunk):
        rows = pl.ds(start, chunk)
        mine = product(own_ref[rows], own, True) + product(near_ref[rows], near, True)
        theirs = product(far_ref[rows], far, True) + product(corner_ref[rows], corner, True)
        lower_ref[rows] = jnp.where(high_bit, theirs, mine).astype(BF16)
        upper_ref[rows] = jnp.where(high_bit, mine, theirs).astype(BF16)


def root_kernel(
    scale, chunk, kept_ref, other_ref, cross_ref, start_ref, lower_ref, upper_ref, out_ref
):
    high_bit = bit_of(("snap", 1)) == 1
    kept, other = kept_ref[...], other_ref[...]
    cross = cross_ref[...] * scale
    top = jnp.concatenate([jnp.where(high_bit, other, kept), cross], axis=1)
    bottom = jnp.concatenate([cross.T, jnp.where(high_bit, kept, other)], axis=1)
    gram = jnp.concatenate([top, bottom], axis=0)
    rotation = subspace_steps(gram, start_ref[...], POWER).astype(BF16)
    for start in range(0, lower_ref.shape[0], chunk):
        rows = pl.ds(start, chunk)
        root = jnp.concatenate([lower_ref[rows], upper_ref[rows]], axis=1)
        out_ref[rows] = product(root, rotation, True).astype(BF16)


def call(kernel, out_shape, *operands, microseconds=8, limit=8 * MIB):
    vmem = pl.BlockSpec(memory_space=pltpu.VMEM)
    return pl.pallas_call(
        kernel,
        out_shape=out_shape,
        in_specs=[vmem] * len(operands),
        out_specs=jax.tree.map(lambda _: vmem, out_shape),
        compiler_params=pltpu.CompilerParams(vmem_limit_bytes=limit),
        cost_estimate=pl.CostEstimate(
            flops=microseconds * 10**9, bytes_accessed=MIB, transcendentals=0
        ),
    )(*operands)


def on_device(fields, start_local, start_pair, start_root):
    local_rows, snaps = fields.shape
    rank = start_local.shape[1]
    quarter = local_rows // 4
    chunk = quarter // 4
    scale = 1.0 / (local_rows * lax.axis_size("grid"))
    core_step, far_step = ("snap", 0), ("snap", 1)
    grid_steps = axis_steps("grid")

    rows = jax.ShapeDtypeStruct((quarter, snaps), fields.dtype)
    own_rows, far_sent, near_sent, corner_sent = pl.pallas_call(
        place_kernel,
        out_shape=(rows,) * 4,
        in_specs=[pl.BlockSpec(memory_space=pltpu.HBM)],
        out_specs=(pl.BlockSpec(memory_space=pltpu.VMEM),) * 4,
        scratch_shapes=[pltpu.SemaphoreType.DMA((4,))],
        name="place",
        compiler_params=pltpu.CompilerParams(vmem_limit_bytes=8 * MIB),
    )(fields.reshape(4, quarter, snaps))
    near_rows = exchange(near_sent, core_step)
    far_core_rows = exchange(corner_sent, core_step)
    far_rows = exchange(far_sent, far_step)
    corner_rows = exchange(far_core_rows, far_step)

    placed = (own_rows, far_sent, near_sent, corner_sent)
    packed = jax.ShapeDtypeStruct((2 * rank + 16, rank), BF16)
    gram = sum(inner_product(rows, rows) for rows in placed)
    sent = call(pack_kernel, packed, gram, microseconds=1, limit=2 * MIB)
    for number, step in enumerate(grid_steps):
        received = exchange(sent, step)
        if number < len(grid_steps) - 1:
            sent = call(merge_kernel, packed, sent, received, microseconds=1, limit=2 * MIB)

    cross = inner_product(own_rows, near_rows) + inner_product(far_sent, far_core_rows)
    half = jax.ShapeDtypeStruct((rank, snaps), F32)
    slab, slab_sent = call(orient_kernel, (half, half), cross, microseconds=1)
    slab = slab + exchange(slab_sent, core_step)
    slab = sum_over(slab, grid_steps)
    other_slab = exchange(slab, core_step)

    turned = jax.ShapeDtypeStruct((rank, snaps), F32)
    turned_pair = jax.ShapeDtypeStruct((rank, 2 * rank), F32)
    local_basis, pair_basis, root_basis = call(
        turn_kernel, (turned, turned_pair, turned_pair),
        start_local, start_pair, start_root,
        microseconds=1,
    )
    square = jax.ShapeDtypeStruct((rank, rank), F32)
    leaf = call(
        lambda *refs: leaf_kernel(scale, *refs),
        jax.ShapeDtypeStruct((2 * rank, snaps), BF16),
        sent, received, local_basis,
    )
    other_leaf = exchange(leaf, core_step)
    leaves = jnp.concatenate([leaf[:rank], other_leaf[:rank]], axis=0)
    far_leaves = exchange(leaves, far_step)

    rotation, kept = call(
        lambda *refs: pair_kernel(scale, *refs),
        (jax.ShapeDtypeStruct((rank, 2 * rank), BF16), square),
        leaf, other_leaf, slab, other_slab, pair_basis,
    )
    far_rotation = exchange(rotation, far_step)
    other = exchange(kept, far_step)
    rows = jax.ShapeDtypeStruct((quarter, rank), BF16)
    lower, upper = call(
        lambda *refs: branch_kernel(chunk, *refs),
        (rows, rows),
        own_rows, near_rows, far_rows, corner_rows, leaves, far_leaves, rotation, far_rotation,
        microseconds=1, limit=16 * MIB,
    )
    cross = sum_everywhere(inner_product(lower, upper), core_step, [far_step] + grid_steps)
    return call(
        lambda *refs: root_kernel(scale, chunk, *refs),
        rows,
        kept, other, cross, root_basis, lower, upper,
        limit=16 * MIB,
    )


def solution(mesh):
    in_specs = (P("grid", "snap"), P("snap", None), P(), P())
    out_specs = P(("grid", "snap"), None)
    return jax.shard_map(
        on_device, mesh=mesh, in_specs=in_specs, out_specs=out_specs, check_vma=False
    )
```

```python
import jax
import jax.numpy as jnp
from jax import lax
from jax.experimental import pallas as pl
from jax.experimental.pallas import tpu as pltpu
from jax.sharding import PartitionSpec as P


POWER = 2
NEWTON = 8
F32 = jnp.float32
BF16 = jnp.bfloat16
MIB = 2**20


def permute(value, steps):
    axes = tuple(axis for axis in ("grid", "snap") if any(axis == on for on, _ in steps))
    places = [0]
    for axis in axes:
        mask = sum(2**bit for on, bit in steps if on == axis)
        size = lax.axis_size(axis)
        places = [place * size + (own ^ mask) for place in places for own in range(size)]
    pairs = list(enumerate(places))
    return lax.ppermute(value, axes, pairs)


def exchange(value, step):
    return permute(value, [step])


def bit_of(step):
    axis, bit = step
    return (lax.axis_index(axis) // 2**bit) % 2


def axis_steps(axis):
    return [(axis, bit) for bit in range(lax.axis_size(axis).bit_length() - 1)]


def sum_over(value, steps):
    for step in steps:
        sent = value.astype(BF16)
        received = exchange(sent, step)
        value = sent.astype(F32) + received.astype(F32)
    return value


def sum_everywhere(value, through, steps):
    value = sum_over(value, [through])
    for start in range(0, len(steps), 2):
        group = steps[start : start + 2]
        hops = [[step, through] for step in group]
        if len(group) == 2:
            hops.append(group)
        sent = value.astype(BF16)
        received = [permute(sent, hop) for hop in hops]
        value = sum((part.astype(F32) for part in received), sent.astype(F32))
    return value


def split(x):
    high = x.astype(BF16)
    return high, (x - high.astype(F32)).astype(BF16)


def product(a, b, transposed=False):
    return lax.dot_general(
        a, b, (((1,), (1 if transposed else 0,)), ((), ())), preferred_element_type=F32
    )


def inner_product(left, right):
    return lax.dot_general(
        left, right, (((0,), (0,)), ((), ())), preferred_element_type=F32
    )


def subspace_steps(gram, basis, count):
    gram_high, gram_low = split(gram)
    rank = basis.shape[0]
    rows = lax.broadcasted_iota(jnp.int32, (rank, rank), 0)
    columns = lax.broadcasted_iota(jnp.int32, (rank, rank), 1)
    identity = (rows == columns).astype(F32)

    def times_right(x, right):
        out = product(jnp.concatenate(split(x), axis=1), right)
        return out[:, :rank] + out[:, rank:]

    for _ in range(count):
        high, low = split(basis)
        out = product(jnp.concatenate([high, low], axis=0), gram_high)
        image = out[:rank] + out[rank:] + product(high, gram_low)
        image = image * lax.rsqrt(jnp.sum(image * image) + 1e-06)
        image_high, image_low = split(image)
        stacked = jnp.concatenate([image_high, image_low], axis=0)
        out = product(stacked, stacked, transposed=True)
        inner = out[:rank, :rank] + out[:rank, rank:] + out[rank:, :rank]
        total = None
        for step in range(NEWTON):
            factor = 1.5 * identity - 0.5 * inner
            row = jnp.concatenate(split(factor), axis=1)
            right = jnp.concatenate([row, row], axis=0)
            if step < NEWTON - 1:
                inner = times_right(times_right(inner, right), right)
            total = factor if total is None else times_right(total, right)
        total_high, total_low = split(total)
        basis = product(
            jnp.concatenate([total_high, total_low], axis=1),
            jnp.concatenate([image_high, image_high], axis=0),
        ) + product(total_high, image_low)
    return basis


def kept_gram(rotation, gram):
    gram_high, gram_low = split(gram)
    image = product(rotation, gram_high) + product(rotation, gram_low)
    high, low = split(image)
    return product(high, rotation, True) + product(low, rotation, True)


def pack(gram):
    size = gram.shape[0] // 2
    rows = lax.broadcasted_iota(jnp.int32, (size, size), 0)
    columns = lax.broadcasted_iota(jnp.int32, (size, size), 1)
    first, second = gram[:size, :size], gram[size:, size:]
    diagonal = jnp.sum(jnp.where(rows == columns, second, 0.0), axis=0, keepdims=True)
    diagonal = jnp.broadcast_to(diagonal, (8, size))
    low = jnp.concatenate([jnp.where(rows <= columns, first, second), diagonal], axis=0)
    high = jnp.concatenate([gram[:size, size:], diagonal], axis=0)
    return low, high


def unpack(low, high):
    size = low.shape[1]
    rows = lax.broadcasted_iota(jnp.int32, (size, size), 0)
    columns = lax.broadcasted_iota(jnp.int32, (size, size), 1)
    both, cross = low[:size], high[:size]
    flipped = both.T
    first = jnp.where(rows <= columns, both, flipped)
    second = jnp.where(rows > columns, both, flipped)
    diagonal = jnp.broadcast_to(low[size : size + 1], (size, size))
    second = jnp.where(rows == columns, diagonal, second)
    top = jnp.concatenate([first, cross], axis=1)
    return jnp.concatenate([top, jnp.concatenate([cross.T, second], axis=1)], axis=0)


def place_kernel(rows_ref, own_ref, far_ref, near_ref, corner_ref, semaphores):
    core, far = bit_of(("snap", 0)), bit_of(("snap", 1))
    places = (2 * far + core, 2 - 2 * far + core, 2 * far + 1 - core, 3 - 2 * far - core)
    targets = (own_ref, far_ref, near_ref, corner_ref)
    copies = [
        pltpu.make_async_copy(rows_ref.at[place], target, semaphores.at[number])
        for number, (place, target) in enumerate(zip(places, targets))
    ]
    for copy in copies:
        copy.start()
    for copy in copies:
        copy.wait()


def turn_kernel(local_ref, pair_ref, root_ref, *turned_refs):
    far = bit_of(("snap", 1))
    turned_refs[0][...] = local_ref[...].T
    turned_refs[1][...] = pair_ref[far].T
    turned_refs[2][...] = root_ref[...].T


def orient_kernel(cross_ref, kept_ref, sent_ref):
    core = bit_of(("snap", 0)) == 1
    rank = kept_ref.shape[0]
    cross = cross_ref[...]
    turned = cross.T
    kept_ref[...] = jnp.where(core, turned[rank:], cross[:rank])
    sent_ref[...] = jnp.where(core, turned[:rank], cross[rank:])


def pack_kernel(side_step, gram_ref, kept_ref, sent_ref):
    side = bit_of(side_step) == 1
    low, high = pack(gram_ref[...])
    kept_ref[...] = jnp.where(side, high, low)
    sent_ref[...] = jnp.where(side, low, high)


def leaf_kernel(scale, side_step, kept_ref, other_ref, start_ref, out_ref):
    side = bit_of(side_step) == 1
    kept, other = kept_ref[...], other_ref[...]
    low = jnp.where(side, other, kept)
    high = jnp.where(side, kept, other)
    gram = unpack(low, high) * scale
    rank = start_ref.shape[0]
    rotation = subspace_steps(gram, start_ref[...], POWER).astype(BF16)
    out_ref[:rank] = rotation
    out_ref[rank:] = jnp.concatenate(split(kept_gram(rotation, gram)), axis=1)


def far_leaf_kernel(chunk, rows_ref, leaf_ref, out_ref):
    rotation = leaf_ref[: leaf_ref.shape[0] // 2]
    for start in range(0, rows_ref.shape[0], chunk):
        rows = pl.ds(start, chunk)
        out_ref[rows] = product(rows_ref[rows], rotation, True).astype(BF16)


def pair_kernel(
    scale, own_ref, other_ref, own_slab_ref, other_slab_ref, start_ref, out_ref, kept_ref
):
    core = bit_of(("snap", 0)) == 1
    rank = start_ref.shape[0]
    own, other = own_ref[...].astype(F32), other_ref[...].astype(F32)
    first, second = jnp.where(core, other, own), jnp.where(core, own, other)
    own, other = own_slab_ref[...], other_slab_ref[...]
    cross = jnp.concatenate([jnp.where(core, other, own), jnp.where(core, own, other)], axis=0)
    cross_high, cross_low = split(cross * scale)
    first_rotation, second_rotation = first[:rank].astype(BF16), second[:rank].astype(BF16)
    image = product(first_rotation, cross_high) + product(first_rotation, cross_low)
    high, low = split(image)
    cross = product(high, second_rotation, True) + product(low, second_rotation, True)
    first, second = first[rank:], second[rank:]
    top = jnp.concatenate([first[:, :rank] + first[:, rank:], cross], axis=1)
    bottom = jnp.concatenate([cross.T, second[:, :rank] + second[:, rank:]], axis=1)
    gram = jnp.concatenate([top, bottom], axis=0)
    rotation = subspace_steps(gram, start_ref[...], POWER).astype(BF16)
    out_ref[...] = rotation
    kept_ref[...] = kept_gram(rotation, gram)


def branch_kernel(
    chunk, own_ref, near_ref, far_ref, corner_ref, leaf_ref, other_leaf_ref, far_leaf_ref,
    rotation_ref, far_rotation_ref, lower_ref, upper_ref,
):
    core = bit_of(("snap", 0)) == 1
    high_bit = bit_of(("snap", 1)) == 1
    rank = rotation_ref.shape[0]

    def halves(ref):
        value = ref[...].astype(F32)
        left, right = value[:, :rank], value[:, rank:]
        own, other = jnp.where(core, right, left), jnp.where(core, left, right)
        return own.astype(BF16), other.astype(BF16)

    def rotation(part, leaf_rotation):
        return product(part, leaf_rotation).astype(BF16)

    own_part, near_part = halves(rotation_ref)
    far_part, corner_part = halves(far_rotation_ref)
    own, near = rotation(own_part, leaf_ref[:rank]), rotation(near_part, other_leaf_ref[:rank])
    corner = rotation(corner_part, far_leaf_ref[...])
    for start in range(0, own_ref.shape[0], chunk):
        rows = pl.ds(start, chunk)
        mine = product(own_ref[rows], own, True) + product(near_ref[rows], near, True)
        theirs = product(far_ref[rows], far_part, True) + product(corner_ref[rows], corner, True)
        lower_ref[rows] = jnp.where(high_bit, theirs, mine).astype(BF16)
        upper_ref[rows] = jnp.where(high_bit, mine, theirs).astype(BF16)


def root_kernel(
    scale, chunk, kept_ref, other_ref, cross_ref, start_ref, lower_ref, upper_ref, out_ref
):
    high_bit = bit_of(("snap", 1)) == 1
    kept, other = kept_ref[...], other_ref[...]
    cross = cross_ref[...] * scale
    top = jnp.concatenate([jnp.where(high_bit, other, kept), cross], axis=1)
    bottom = jnp.concatenate([cross.T, jnp.where(high_bit, kept, other)], axis=1)
    gram = jnp.concatenate([top, bottom], axis=0)
    rotation = subspace_steps(gram, start_ref[...], POWER).astype(BF16)
    for start in range(0, lower_ref.shape[0], chunk):
        rows = pl.ds(start, chunk)
        root = jnp.concatenate([lower_ref[rows], upper_ref[rows]], axis=1)
        out_ref[rows] = product(root, rotation, True).astype(BF16)


def call(kernel, out_shape, *operands, microseconds=8, limit=8 * MIB):
    vmem = pl.BlockSpec(memory_space=pltpu.VMEM)
    return pl.pallas_call(
        kernel,
        out_shape=out_shape,
        in_specs=[vmem] * len(operands),
        out_specs=jax.tree.map(lambda _: vmem, out_shape),
        compiler_params=pltpu.CompilerParams(vmem_limit_bytes=limit),
        cost_estimate=pl.CostEstimate(
            flops=microseconds * 10**9, bytes_accessed=MIB, transcendentals=0
        ),
    )(*operands)


def on_device(fields, start_local, start_pair, start_root):
    local_rows, snaps = fields.shape
    rank = start_local.shape[1]
    quarter = local_rows // 4
    chunk = quarter // 4
    scale = 1.0 / (local_rows * lax.axis_size("grid"))
    core_step, far_step = ("snap", 0), ("snap", 1)
    grid_steps = axis_steps("grid")

    rows = jax.ShapeDtypeStruct((quarter, snaps), fields.dtype)
    own_rows, far_sent, near_sent, corner_sent = pl.pallas_call(
        place_kernel,
        out_shape=(rows,) * 4,
        in_specs=[pl.BlockSpec(memory_space=pltpu.HBM)],
        out_specs=(pl.BlockSpec(memory_space=pltpu.VMEM),) * 4,
        scratch_shapes=[pltpu.SemaphoreType.DMA((4,))],
        name="place",
        compiler_params=pltpu.CompilerParams(vmem_limit_bytes=8 * MIB),
    )(fields.reshape(4, quarter, snaps))
    near_rows = exchange(near_sent, core_step)
    far_core_rows = exchange(corner_sent, core_step)
    corner_rows = exchange(far_core_rows, far_step)

    placed = (own_rows, far_sent, near_sent, corner_sent)
    piece = jax.ShapeDtypeStruct((rank + 8, rank), F32)
    kept, sent = call(
        lambda *refs: pack_kernel(grid_steps[0], *refs),
        (piece, piece), sum(inner_product(rows, rows) for rows in placed),
        microseconds=1, limit=2 * MIB,
    )
    kept = kept + exchange(sent, grid_steps[0])
    for step in grid_steps[1:]:
        kept = kept + exchange(kept, step)
    other = exchange(kept, grid_steps[0])

    cross = inner_product(own_rows, near_rows) + inner_product(far_sent, far_core_rows)
    half = jax.ShapeDtypeStruct((rank, snaps), F32)
    slab, slab_sent = call(orient_kernel, (half, half), cross, microseconds=1)
    slab = slab + exchange(slab_sent, core_step)
    slab = sum_over(slab, grid_steps)
    other_slab = exchange(slab, core_step)

    turned = jax.ShapeDtypeStruct((rank, snaps), F32)
    turned_pair = jax.ShapeDtypeStruct((rank, 2 * rank), F32)
    local_basis, pair_basis, root_basis = call(
        turn_kernel, (turned, turned_pair, turned_pair),
        start_local, start_pair, start_root,
        microseconds=1,
    )
    square = jax.ShapeDtypeStruct((rank, rank), F32)
    leaf = call(
        lambda *refs: leaf_kernel(scale, grid_steps[0], *refs),
        jax.ShapeDtypeStruct((2 * rank, snaps), BF16),
        kept, other, local_basis,
    )
    other_leaf = exchange(leaf, core_step)
    rows = jax.ShapeDtypeStruct((quarter, rank), BF16)
    far_rows = call(
        lambda *refs: far_leaf_kernel(chunk, *refs), rows, far_sent, leaf,
        microseconds=1,
    )
    far_rows = exchange(far_rows, far_step)
    far_leaf = exchange(other_leaf[:rank], far_step)

    rotation, kept = call(
        lambda *refs: pair_kernel(scale, *refs),
        (jax.ShapeDtypeStruct((rank, 2 * rank), BF16), square),
        leaf, other_leaf, slab, other_slab, pair_basis,
    )
    far_rotation = exchange(rotation, far_step)
    other = exchange(kept, far_step)
    lower, upper = call(
        lambda *refs: branch_kernel(chunk, *refs),
        (rows, rows),
        own_rows, near_rows, far_rows, corner_rows, leaf, other_leaf, far_leaf,
        rotation, far_rotation,
        microseconds=1, limit=16 * MIB,
    )
    cross = sum_everywhere(inner_product(lower, upper), core_step, [far_step] + grid_steps)
    return call(
        lambda *refs: root_kernel(scale, chunk, *refs),
        rows,
        kept, other, cross, root_basis, lower, upper,
        limit=16 * MIB,
    )


def solution(mesh):
    in_specs = (P("grid", "snap"), P("snap", None), P(), P())
    out_specs = P(("grid", "snap"), None)
    return jax.shard_map(
        on_device, mesh=mesh, in_specs=in_specs, out_specs=out_specs, check_vma=False
    )
```

```python
import jax
import jax.numpy as jnp
from jax import lax
from jax.experimental import pallas as pl
from jax.experimental.pallas import tpu as pltpu
from jax.sharding import PartitionSpec as P


POWER = 2
NEWTON = 8
F32 = jnp.float32
BF16 = jnp.bfloat16
MIB = 2**20


def permute(value, steps):
    axes = tuple(axis for axis in ("grid", "snap") if any(axis == on for on, _ in steps))
    places = [0]
    for axis in axes:
        mask = sum(2**bit for on, bit in steps if on == axis)
        size = lax.axis_size(axis)
        places = [place * size + (own ^ mask) for place in places for own in range(size)]
    pairs = list(enumerate(places))
    return lax.ppermute(value, axes, pairs)


def exchange(value, step):
    return permute(value, [step])


def bit_of(step):
    axis, bit = step
    return (lax.axis_index(axis) // 2**bit) % 2


def axis_steps(axis):
    return [(axis, bit) for bit in range(lax.axis_size(axis).bit_length() - 1)]


def sum_over(value, steps):
    for step in steps:
        sent = value.astype(BF16)
        received = exchange(sent, step)
        value = sent.astype(F32) + received.astype(F32)
    return value


def sum_everywhere(value, through, steps):
    value = sum_over(value, [through])
    for start in range(0, len(steps), 2):
        group = steps[start : start + 2]
        hops = [[step, through] for step in group]
        if len(group) == 2:
            hops.append(group)
        sent = value.astype(BF16)
        received = [permute(sent, hop) for hop in hops]
        value = sum((part.astype(F32) for part in received), sent.astype(F32))
    return value


def split(x):
    high = x.astype(BF16)
    return high, (x - high.astype(F32)).astype(BF16)


def product(a, b, transposed=False):
    return lax.dot_general(
        a, b, (((1,), (1 if transposed else 0,)), ((), ())), preferred_element_type=F32
    )


def inner_product(left, right):
    return lax.dot_general(
        left, right, (((0,), (0,)), ((), ())), preferred_element_type=F32
    )


def subspace_steps(gram, basis, count):
    gram_high, gram_low = split(gram)
    rank = basis.shape[0]
    rows = lax.broadcasted_iota(jnp.int32, (rank, rank), 0)
    columns = lax.broadcasted_iota(jnp.int32, (rank, rank), 1)
    identity = (rows == columns).astype(F32)

    def times_right(x, right):
        out = product(jnp.concatenate(split(x), axis=1), right)
        return out[:, :rank] + out[:, rank:]

    for _ in range(count):
        high, low = split(basis)
        out = product(jnp.concatenate([high, low], axis=0), gram_high)
        image = out[:rank] + out[rank:] + product(high, gram_low)
        size = jnp.sum(image * image) + 1e-06
        image_high, image_low = split(image)
        stacked = jnp.concatenate([image_high, image_low], axis=0)
        out = product(stacked, stacked, transposed=True)
        inner = (out[:rank, :rank] + out[:rank, rank:] + out[rank:, :rank]) * (1.0 / size)
        total = None
        for step in range(NEWTON):
            factor = 1.5 * identity - 0.5 * inner
            row = jnp.concatenate(split(factor), axis=1)
            right = jnp.concatenate([row, row], axis=0)
            if total is None:
                total = factor
                inner = times_right(times_right(inner, right), right)
            elif step < NEWTON - 1:
                both = times_right(jnp.concatenate([inner, total], axis=0), right)
                inner, total = times_right(both[:rank], right), both[rank:]
            else:
                total = times_right(total, right)
        total_high, total_low = split(total * lax.rsqrt(size))
        basis = product(
            jnp.concatenate([total_high, total_low], axis=1),
            jnp.concatenate([image_high, image_high], axis=0),
        ) + product(total_high, image_low)
    return basis


def kept_gram(rotation, gram):
    gram_high, gram_low = split(gram)
    image = product(rotation, gram_high) + product(rotation, gram_low)
    high, low = split(image)
    return product(high, rotation, True) + product(low, rotation, True)


def pack(gram):
    size = gram.shape[0] // 2
    rows = lax.broadcasted_iota(jnp.int32, (size, size), 0)
    columns = lax.broadcasted_iota(jnp.int32, (size, size), 1)
    first, second = gram[:size, :size], gram[size:, size:]
    diagonal = jnp.sum(jnp.where(rows == columns, second, 0.0), axis=0, keepdims=True)
    diagonal = jnp.broadcast_to(diagonal, (8, size))
    low = jnp.concatenate([jnp.where(rows <= columns, first, second), diagonal], axis=0)
    high = jnp.concatenate([gram[:size, size:], diagonal], axis=0)
    return low, high


def unpack(low, high):
    size = low.shape[1]
    rows = lax.broadcasted_iota(jnp.int32, (size, size), 0)
    columns = lax.broadcasted_iota(jnp.int32, (size, size), 1)
    both, cross = low[:size], high[:size]
    flipped = both.T
    first = jnp.where(rows <= columns, both, flipped)
    second = jnp.where(rows > columns, both, flipped)
    diagonal = jnp.broadcast_to(low[size : size + 1], (size, size))
    second = jnp.where(rows == columns, diagonal, second)
    top = jnp.concatenate([first, cross], axis=1)
    return jnp.concatenate([top, jnp.concatenate([cross.T, second], axis=1)], axis=0)


def place_kernel(rows_ref, own_ref, far_ref, near_ref, corner_ref, semaphores):
    core, far = bit_of(("snap", 0)), bit_of(("snap", 1))
    places = (2 * far + core, 2 - 2 * far + core, 2 * far + 1 - core, 3 - 2 * far - core)
    targets = (own_ref, far_ref, near_ref, corner_ref)
    copies = [
        pltpu.make_async_copy(rows_ref.at[place], target, semaphores.at[number])
        for number, (place, target) in enumerate(zip(places, targets))
    ]
    for copy in copies:
        copy.start()
    for copy in copies:
        copy.wait()


def turn_kernel(local_ref, pair_ref, root_ref, *turned_refs):
    far = bit_of(("snap", 1))
    turned_refs[0][...] = local_ref[...].T
    turned_refs[1][...] = pair_ref[far].T
    turned_refs[2][...] = root_ref[...].T


def orient_kernel(cross_ref, kept_ref, sent_ref):
    core = bit_of(("snap", 0)) == 1
    rank = kept_ref.shape[0]
    cross = cross_ref[...]
    turned = cross.T
    kept_ref[...] = jnp.where(core, turned[rank:], cross[:rank])
    sent_ref[...] = jnp.where(core, turned[:rank], cross[rank:])


def pack_kernel(side_step, gram_ref, kept_ref, sent_ref):
    side = bit_of(side_step) == 1
    low, high = pack(gram_ref[...])
    kept_ref[...] = jnp.where(side, high, low)
    sent_ref[...] = jnp.where(side, low, high)


def leaf_kernel(scale, side_step, kept_ref, other_ref, start_ref, out_ref):
    side = bit_of(side_step) == 1
    kept, other = kept_ref[...], other_ref[...]
    low = jnp.where(side, other, kept)
    high = jnp.where(side, kept, other)
    gram = unpack(low, high) * scale
    rank = start_ref.shape[0]
    rotation = subspace_steps(gram, start_ref[...], POWER).astype(BF16)
    out_ref[:rank] = rotation
    out_ref[rank:] = jnp.concatenate(split(kept_gram(rotation, gram)), axis=1)


def far_leaf_kernel(chunk, rows_ref, leaf_ref, out_ref):
    rotation = leaf_ref[: leaf_ref.shape[0] // 2]
    for start in range(0, rows_ref.shape[0], chunk):
        rows = pl.ds(start, chunk)
        out_ref[rows] = product(rows_ref[rows], rotation, True).astype(BF16)


def pair_kernel(
    scale, own_ref, other_ref, own_slab_ref, other_slab_ref, start_ref, out_ref, kept_ref
):
    core = bit_of(("snap", 0)) == 1
    rank = start_ref.shape[0]
    own, other = own_ref[...].astype(F32), other_ref[...].astype(F32)
    first, second = jnp.where(core, other, own), jnp.where(core, own, other)
    own, other = own_slab_ref[...], other_slab_ref[...]
    cross = jnp.concatenate([jnp.where(core, other, own), jnp.where(core, own, other)], axis=0)
    cross_high, cross_low = split(cross * scale)
    first_rotation, second_rotation = first[:rank].astype(BF16), second[:rank].astype(BF16)
    image = product(first_rotation, cross_high) + product(first_rotation, cross_low)
    high, low = split(image)
    cross = product(high, second_rotation, True) + product(low, second_rotation, True)
    first, second = first[rank:], second[rank:]
    top = jnp.concatenate([first[:, :rank] + first[:, rank:], cross], axis=1)
    bottom = jnp.concatenate([cross.T, second[:, :rank] + second[:, rank:]], axis=1)
    gram = jnp.concatenate([top, bottom], axis=0)
    rotation = subspace_steps(gram, start_ref[...], POWER).astype(BF16)
    out_ref[...] = rotation
    kept_ref[...] = kept_gram(rotation, gram)


def branch_kernel(
    chunk, own_ref, near_ref, far_ref, corner_ref, leaf_ref, other_leaf_ref, far_leaf_ref,
    rotation_ref, far_rotation_ref, lower_ref, upper_ref,
):
    core = bit_of(("snap", 0)) == 1
    high_bit = bit_of(("snap", 1)) == 1
    rank = rotation_ref.shape[0]

    def halves(ref):
        value = ref[...].astype(F32)
        left, right = value[:, :rank], value[:, rank:]
        own, other = jnp.where(core, right, left), jnp.where(core, left, right)
        return own.astype(BF16), other.astype(BF16)

    def rotation(part, leaf_rotation):
        return product(part, leaf_rotation).astype(BF16)

    own_part, near_part = halves(rotation_ref)
    far_part, corner_part = halves(far_rotation_ref)
    own, near = rotation(own_part, leaf_ref[:rank]), rotation(near_part, other_leaf_ref[:rank])
    corner = rotation(corner_part, far_leaf_ref[...])
    for start in range(0, own_ref.shape[0], chunk):
        rows = pl.ds(start, chunk)
        mine = product(own_ref[rows], own, True) + product(near_ref[rows], near, True)
        theirs = product(far_ref[rows], far_part, True) + product(corner_ref[rows], corner, True)
        lower_ref[rows] = jnp.where(high_bit, theirs, mine).astype(BF16)
        upper_ref[rows] = jnp.where(high_bit, mine, theirs).astype(BF16)


def root_kernel(
    scale, chunk, kept_ref, other_ref, cross_ref, start_ref, lower_ref, upper_ref, out_ref
):
    high_bit = bit_of(("snap", 1)) == 1
    kept, other = kept_ref[...], other_ref[...]
    cross = cross_ref[...] * scale
    top = jnp.concatenate([jnp.where(high_bit, other, kept), cross], axis=1)
    bottom = jnp.concatenate([cross.T, jnp.where(high_bit, kept, other)], axis=1)
    gram = jnp.concatenate([top, bottom], axis=0)
    rotation = subspace_steps(gram, start_ref[...], POWER).astype(BF16)
    for start in range(0, lower_ref.shape[0], chunk):
        rows = pl.ds(start, chunk)
        root = jnp.concatenate([lower_ref[rows], upper_ref[rows]], axis=1)
        out_ref[rows] = product(root, rotation, True).astype(BF16)


def call(kernel, out_shape, *operands, microseconds=8, limit=8 * MIB):
    vmem = pl.BlockSpec(memory_space=pltpu.VMEM)
    return pl.pallas_call(
        kernel,
        out_shape=out_shape,
        in_specs=[vmem] * len(operands),
        out_specs=jax.tree.map(lambda _: vmem, out_shape),
        compiler_params=pltpu.CompilerParams(vmem_limit_bytes=limit),
        cost_estimate=pl.CostEstimate(
            flops=microseconds * 10**9, bytes_accessed=MIB, transcendentals=0
        ),
    )(*operands)


def on_device(fields, start_local, start_pair, start_root):
    local_rows, snaps = fields.shape
    rank = start_local.shape[1]
    quarter = local_rows // 4
    chunk = quarter // 4
    scale = 1.0 / (local_rows * lax.axis_size("grid"))
    core_step, far_step = ("snap", 0), ("snap", 1)
    grid_steps = axis_steps("grid")

    rows = jax.ShapeDtypeStruct((quarter, snaps), fields.dtype)
    own_rows, far_sent, near_sent, corner_sent = pl.pallas_call(
        place_kernel,
        out_shape=(rows,) * 4,
        in_specs=[pl.BlockSpec(memory_space=pltpu.HBM)],
        out_specs=(pl.BlockSpec(memory_space=pltpu.VMEM),) * 4,
        scratch_shapes=[pltpu.SemaphoreType.DMA((4,))],
        name="place",
        compiler_params=pltpu.CompilerParams(vmem_limit_bytes=48 * MIB),
    )(fields.reshape(4, quarter, snaps))
    near_rows = exchange(near_sent, core_step)
    far_core_rows = exchange(corner_sent, core_step)
    corner_rows = exchange(far_core_rows, far_step)

    placed = (own_rows, far_sent, near_sent, corner_sent)
    piece = jax.ShapeDtypeStruct((rank + 8, rank), F32)
    kept, sent = call(
        lambda *refs: pack_kernel(grid_steps[0], *refs),
        (piece, piece), sum(inner_product(rows, rows) for rows in placed),
        microseconds=1, limit=2 * MIB,
    )
    kept = kept + exchange(sent, grid_steps[0])
    for step in grid_steps[1:]:
        kept = kept + exchange(kept, step)
    other = exchange(kept, grid_steps[0])

    cross = inner_product(own_rows, near_rows) + inner_product(far_sent, far_core_rows)
    half = jax.ShapeDtypeStruct((rank, snaps), F32)
    slab, slab_sent = call(orient_kernel, (half, half), cross, microseconds=1)
    slab = slab + exchange(slab_sent, core_step)
    slab = sum_over(slab, grid_steps)
    other_slab = exchange(slab, core_step)

    turned = jax.ShapeDtypeStruct((rank, snaps), F32)
    turned_pair = jax.ShapeDtypeStruct((rank, 2 * rank), F32)
    local_basis, pair_basis, root_basis = call(
        turn_kernel, (turned, turned_pair, turned_pair),
        start_local, start_pair, start_root,
        microseconds=1,
    )
    square = jax.ShapeDtypeStruct((rank, rank), F32)
    leaf = call(
        lambda *refs: leaf_kernel(scale, grid_steps[0], *refs),
        jax.ShapeDtypeStruct((2 * rank, snaps), BF16),
        kept, other, local_basis,
    )
    other_leaf = exchange(leaf, core_step)
    rows = jax.ShapeDtypeStruct((quarter, rank), BF16)
    far_rows = call(
        lambda *refs: far_leaf_kernel(chunk, *refs), rows, far_sent, leaf,
        microseconds=1,
    )
    far_rows = exchange(far_rows, far_step)
    far_leaf = exchange(other_leaf[:rank], far_step)

    rotation, kept = call(
        lambda *refs: pair_kernel(scale, *refs),
        (jax.ShapeDtypeStruct((rank, 2 * rank), BF16), square),
        leaf, other_leaf, slab, other_slab, pair_basis,
    )
    far_rotation = exchange(rotation, far_step)
    other = exchange(kept, far_step)
    lower, upper = call(
        lambda *refs: branch_kernel(chunk, *refs),
        (rows, rows),
        own_rows, near_rows, far_rows, corner_rows, leaf, other_leaf, far_leaf,
        rotation, far_rotation,
        microseconds=1, limit=16 * MIB,
    )
    cross = sum_everywhere(inner_product(lower, upper), core_step, [far_step] + grid_steps)
    return call(
        lambda *refs: root_kernel(scale, chunk, *refs),
        rows,
        kept, other, cross, root_basis, lower, upper,
        limit=16 * MIB,
    )


def solution(mesh):
    in_specs = (P("grid", "snap"), P("snap", None), P(), P())
    out_specs = P(("grid", "snap"), None)
    return jax.shard_map(
        on_device, mesh=mesh, in_specs=in_specs, out_specs=out_specs, check_vma=False
    )
```

```python
import jax
import jax.numpy as jnp
from jax import lax
from jax.experimental import pallas as pl
from jax.experimental.pallas import tpu as pltpu
from jax.sharding import PartitionSpec as P


POWER = 2
NEWTON = 8
F32 = jnp.float32
BF16 = jnp.bfloat16
MIB = 2**20


def permute(value, steps):
    axes = tuple(axis for axis in ("grid", "snap") if any(axis == on for on, _ in steps))
    places = [0]
    for axis in axes:
        mask = sum(2**bit for on, bit in steps if on == axis)
        size = lax.axis_size(axis)
        places = [place * size + (own ^ mask) for place in places for own in range(size)]
    pairs = list(enumerate(places))
    return lax.ppermute(value, axes, pairs)


def exchange(value, step):
    return permute(value, [step])


def bit_of(step):
    axis, bit = step
    return (lax.axis_index(axis) // 2**bit) % 2


def axis_steps(axis):
    return [(axis, bit) for bit in range(lax.axis_size(axis).bit_length() - 1)]


def sum_over(value, steps):
    for step in steps:
        sent = value.astype(BF16)
        received = exchange(sent, step)
        value = sent.astype(F32) + received.astype(F32)
    return value


def sum_everywhere(value, through, steps):
    value = sum_over(value, [through])
    groups = [steps[:2]] + [[step] for step in steps[2:]]
    for group in groups:
        hops = [[step, through] for step in group]
        if len(group) == 2:
            hops.append(group)
        sent = value.astype(BF16)
        received = [permute(sent, hop) for hop in hops]
        value = sum((part.astype(F32) for part in received), sent.astype(F32))
    return value


def split(x):
    high = x.astype(BF16)
    return high, (x - high.astype(F32)).astype(BF16)


def product(a, b, transposed=False):
    return lax.dot_general(
        a, b, (((1,), (1 if transposed else 0,)), ((), ())), preferred_element_type=F32
    )


def inner_product(left, right):
    return lax.dot_general(
        left, right, (((0,), (0,)), ((), ())), preferred_element_type=F32
    )


def subspace_steps(gram, basis, count):
    gram_high, gram_low = split(gram)
    rank = basis.shape[0]
    rows = lax.broadcasted_iota(jnp.int32, (rank, rank), 0)
    columns = lax.broadcasted_iota(jnp.int32, (rank, rank), 1)
    identity = (rows == columns).astype(F32)

    def times_right(x, right):
        out = product(jnp.concatenate(split(x), axis=1), right)
        return out[:, :rank] + out[:, rank:]

    for _ in range(count):
        high, low = split(basis)
        out = product(jnp.concatenate([high, low], axis=0), gram_high)
        image = out[:rank] + out[rank:] + product(high, gram_low)
        size = jnp.sum(image * image) + 1e-06
        image_high, image_low = split(image)
        stacked = jnp.concatenate([image_high, image_low], axis=0)
        out = product(stacked, stacked, transposed=True)
        inner = (out[:rank, :rank] + out[:rank, rank:] + out[rank:, :rank]) * (1.0 / size)
        total = None
        for step in range(NEWTON):
            factor = 1.5 * identity - 0.5 * inner
            row = jnp.concatenate(split(factor), axis=1)
            right = jnp.concatenate([row, row], axis=0)
            if total is None:
                total = factor
                inner = times_right(times_right(inner, right), right)
            elif step < NEWTON - 1:
                both = times_right(jnp.concatenate([inner, total], axis=0), right)
                inner, total = times_right(both[:rank], right), both[rank:]
            else:
                total = times_right(total, right)
        total_high, total_low = split(total * lax.rsqrt(size))
        basis = product(
            jnp.concatenate([total_high, total_low], axis=1),
            jnp.concatenate([image_high, image_high], axis=0),
        ) + product(total_high, image_low)
    return basis


def kept_gram(rotation, gram):
    gram_high, gram_low = split(gram)
    image = product(rotation, gram_high) + product(rotation, gram_low)
    high, low = split(image)
    return product(high, rotation, True) + product(low, rotation, True)


def pack(gram):
    size = gram.shape[0] // 2
    rows = lax.broadcasted_iota(jnp.int32, (size, size), 0)
    columns = lax.broadcasted_iota(jnp.int32, (size, size), 1)
    first, second = gram[:size, :size], gram[size:, size:]
    diagonal = jnp.sum(jnp.where(rows == columns, second, 0.0), axis=0, keepdims=True)
    diagonal = jnp.broadcast_to(diagonal, (8, size))
    low = jnp.concatenate([jnp.where(rows <= columns, first, second), diagonal], axis=0)
    high = jnp.concatenate([gram[:size, size:], diagonal], axis=0)
    return low, high


def unpack(low, high):
    size = low.shape[1]
    rows = lax.broadcasted_iota(jnp.int32, (size, size), 0)
    columns = lax.broadcasted_iota(jnp.int32, (size, size), 1)
    both, cross = low[:size], high[:size]
    flipped = both.T
    first = jnp.where(rows <= columns, both, flipped)
    second = jnp.where(rows > columns, both, flipped)
    diagonal = jnp.broadcast_to(low[size : size + 1], (size, size))
    second = jnp.where(rows == columns, diagonal, second)
    top = jnp.concatenate([first, cross], axis=1)
    return jnp.concatenate([top, jnp.concatenate([cross.T, second], axis=1)], axis=0)


def place_kernel(rows_ref, own_ref, near_ref, corner_ref, raw_ref, rest_ref, semaphores):
    core, far = bit_of(("snap", 0)), bit_of(("snap", 1))
    places = (2 * far + core, 2 * far + 1 - core, 3 - 2 * far - core)
    parts = [(rows_ref.at[place], ref) for place, ref in zip(places, (own_ref, near_ref, corner_ref))]
    place, half = 2 - 2 * far + core, raw_ref.shape[0]
    parts.append((rows_ref.at[place, pl.ds(0, half)], raw_ref))
    parts.append((rows_ref.at[place, pl.ds(half, half)], rest_ref))
    copies = [
        pltpu.make_async_copy(source, target, semaphores.at[number])
        for number, (source, target) in enumerate(parts)
    ]
    for copy in copies:
        copy.start()
    for copy in copies:
        copy.wait()


def turn_kernel(local_ref, pair_ref, root_ref, *turned_refs):
    far = bit_of(("snap", 1))
    turned_refs[0][...] = local_ref[...].T
    turned_refs[1][...] = pair_ref[far].T
    turned_refs[2][...] = root_ref[...].T


def orient_kernel(cross_ref, kept_ref, sent_ref):
    core = bit_of(("snap", 0)) == 1
    rank = kept_ref.shape[0]
    cross = cross_ref[...]
    turned = cross.T
    kept_ref[...] = jnp.where(core, turned[rank:], cross[:rank])
    sent_ref[...] = jnp.where(core, turned[:rank], cross[rank:])


def pack_kernel(side_step, gram_ref, kept_ref, sent_ref):
    side = bit_of(side_step) == 1
    low, high = pack(gram_ref[...])
    kept_ref[...] = jnp.where(side, high, low)
    sent_ref[...] = jnp.where(side, low, high)


def leaf_kernel(scale, side_step, kept_ref, other_ref, start_ref, out_ref):
    side = bit_of(side_step) == 1
    kept, other = kept_ref[...], other_ref[...]
    low = jnp.where(side, other, kept)
    high = jnp.where(side, kept, other)
    gram = unpack(low, high) * scale
    rank = start_ref.shape[0]
    rotation = subspace_steps(gram, start_ref[...], POWER).astype(BF16)
    out_ref[:rank] = rotation
    out_ref[rank:] = jnp.concatenate(split(kept_gram(rotation, gram)), axis=1)


def far_leaf_kernel(chunk, rows_ref, leaf_ref, out_ref):
    rank = leaf_ref.shape[0] // 2
    rotation = leaf_ref[:rank]
    count = rows_ref.shape[0]
    for start in range(0, count, chunk):
        rows = pl.ds(start, chunk)
        out_ref[rows] = product(rows_ref[rows], rotation, True).astype(BF16)
    out_ref[pl.ds(count, rank)] = rotation[:, :rank]
    out_ref[pl.ds(count + rank, rank)] = rotation[:, rank:]


def pair_kernel(
    scale, own_ref, other_ref, own_slab_ref, other_slab_ref, start_ref, out_ref, kept_ref
):
    core = bit_of(("snap", 0)) == 1
    rank = start_ref.shape[0]
    own, other = own_ref[...].astype(F32), other_ref[...].astype(F32)
    first, second = jnp.where(core, other, own), jnp.where(core, own, other)
    own, other = own_slab_ref[...], other_slab_ref[...]
    cross = jnp.concatenate([jnp.where(core, other, own), jnp.where(core, own, other)], axis=0)
    cross_high, cross_low = split(cross * scale)
    first_rotation, second_rotation = first[:rank].astype(BF16), second[:rank].astype(BF16)
    image = product(first_rotation, cross_high) + product(first_rotation, cross_low)
    high, low = split(image)
    cross = product(high, second_rotation, True) + product(low, second_rotation, True)
    first, second = first[rank:], second[rank:]
    top = jnp.concatenate([first[:, :rank] + first[:, rank:], cross], axis=1)
    bottom = jnp.concatenate([cross.T, second[:, :rank] + second[:, rank:]], axis=1)
    gram = jnp.concatenate([top, bottom], axis=0)
    rotation = subspace_steps(gram, start_ref[...], POWER).astype(BF16)
    out_ref[...] = rotation
    kept_ref[...] = kept_gram(rotation, gram)


def branch_kernel(
    chunk, own_ref, near_ref, raw_ref, far_ref, corner_ref, leaf_ref, other_leaf_ref,
    far_leaf_ref, rotation_ref, far_rotation_ref, lower_ref, upper_ref,
):
    core = bit_of(("snap", 0)) == 1
    high_bit = bit_of(("snap", 1)) == 1
    rank = rotation_ref.shape[0]

    def halves(ref):
        value = ref[...].astype(F32)
        left, right = value[:, :rank], value[:, rank:]
        own, other = jnp.where(core, right, left), jnp.where(core, left, right)
        return own.astype(BF16), other.astype(BF16)

    def rotation(part, leaf_rotation):
        return product(part, leaf_rotation).astype(BF16)

    own_part, near_part = halves(rotation_ref)
    far_part, corner_part = halves(far_rotation_ref)
    own, near = rotation(own_part, leaf_ref[:rank]), rotation(near_part, other_leaf_ref[:rank])
    corner = rotation(corner_part, far_leaf_ref[...])
    half = raw_ref.shape[0]
    pieces = [far_ref[pl.ds(half + piece * rank, rank)] for piece in range(2)]
    far = rotation(far_part, jnp.concatenate(pieces, axis=1))
    for start in range(0, own_ref.shape[0], chunk):
        rows = pl.ds(start, chunk)
        mine = product(own_ref[rows], own, True) + product(near_ref[rows], near, True)
        if start < half:
            theirs = product(raw_ref[rows], far, True)
        else:
            theirs = product(far_ref[pl.ds(start - half, chunk)], far_part, True)
        theirs = theirs + product(corner_ref[rows], corner, True)
        lower_ref[rows] = jnp.where(high_bit, theirs, mine).astype(BF16)
        upper_ref[rows] = jnp.where(high_bit, mine, theirs).astype(BF16)


def root_kernel(
    scale, chunk, kept_ref, other_ref, cross_ref, start_ref, lower_ref, upper_ref, out_ref
):
    high_bit = bit_of(("snap", 1)) == 1
    kept, other = kept_ref[...], other_ref[...]
    cross = cross_ref[...] * scale
    top = jnp.concatenate([jnp.where(high_bit, other, kept), cross], axis=1)
    bottom = jnp.concatenate([cross.T, jnp.where(high_bit, kept, other)], axis=1)
    gram = jnp.concatenate([top, bottom], axis=0)
    rotation = subspace_steps(gram, start_ref[...], POWER).astype(BF16)
    for start in range(0, lower_ref.shape[0], chunk):
        rows = pl.ds(start, chunk)
        root = jnp.concatenate([lower_ref[rows], upper_ref[rows]], axis=1)
        out_ref[rows] = product(root, rotation, True).astype(BF16)


def call(kernel, out_shape, *operands, microseconds=8, limit=8 * MIB):
    vmem = pl.BlockSpec(memory_space=pltpu.VMEM)
    return pl.pallas_call(
        kernel,
        out_shape=out_shape,
        in_specs=[vmem] * len(operands),
        out_specs=jax.tree.map(lambda _: vmem, out_shape),
        compiler_params=pltpu.CompilerParams(vmem_limit_bytes=limit),
        cost_estimate=pl.CostEstimate(
            flops=microseconds * 10**9, bytes_accessed=MIB, transcendentals=0
        ),
    )(*operands)


def on_device(fields, start_local, start_pair, start_root):
    local_rows, snaps = fields.shape
    rank = start_local.shape[1]
    quarter = local_rows // 4
    chunk = quarter // 4
    scale = 1.0 / (local_rows * lax.axis_size("grid"))
    core_step, far_step = ("snap", 0), ("snap", 1)
    grid_steps = axis_steps("grid")

    rows = jax.ShapeDtypeStruct((quarter, snaps), fields.dtype)
    half_rows = jax.ShapeDtypeStruct((quarter // 2, snaps), fields.dtype)
    placed = pl.pallas_call(
        place_kernel,
        out_shape=(rows,) * 3 + (half_rows,) * 2,
        in_specs=[pl.BlockSpec(memory_space=pltpu.HBM)],
        out_specs=(pl.BlockSpec(memory_space=pltpu.VMEM),) * 5,
        scratch_shapes=[pltpu.SemaphoreType.DMA((5,))],
        name="place",
        compiler_params=pltpu.CompilerParams(vmem_limit_bytes=48 * MIB),
    )(fields.reshape(4, quarter, snaps))
    own_rows, near_sent, corner_sent, raw_sent, rest_sent = placed
    near_rows = exchange(near_sent, core_step)
    far_core_rows = exchange(corner_sent, core_step)
    corner_rows = exchange(far_core_rows, far_step)
    raw_rows = exchange(raw_sent, far_step)

    piece = jax.ShapeDtypeStruct((rank + 8, rank), F32)
    kept, sent = call(
        lambda *refs: pack_kernel(grid_steps[0], *refs),
        (piece, piece), sum(inner_product(rows, rows) for rows in placed),
        microseconds=1, limit=2 * MIB,
    )
    kept = kept + exchange(sent, grid_steps[0])
    for step in grid_steps[1:]:
        kept = kept + exchange(kept, step)
    other = exchange(kept, grid_steps[0])

    cross = inner_product(own_rows, near_rows)
    cross = cross + inner_product(raw_sent, far_core_rows[: quarter // 2])
    cross = cross + inner_product(rest_sent, far_core_rows[quarter // 2 :])
    half = jax.ShapeDtypeStruct((rank, snaps), F32)
    slab, slab_sent = call(orient_kernel, (half, half), cross, microseconds=1)
    slab = slab + exchange(slab_sent, core_step)
    slab = sum_over(slab, grid_steps)
    other_slab = exchange(slab, core_step)

    turned = jax.ShapeDtypeStruct((rank, snaps), F32)
    turned_pair = jax.ShapeDtypeStruct((rank, 2 * rank), F32)
    local_basis, pair_basis, root_basis = call(
        turn_kernel, (turned, turned_pair, turned_pair),
        start_local, start_pair, start_root,
        microseconds=1,
    )
    square = jax.ShapeDtypeStruct((rank, rank), F32)
    leaf = call(
        lambda *refs: leaf_kernel(scale, grid_steps[0], *refs),
        jax.ShapeDtypeStruct((2 * rank, snaps), BF16),
        kept, other, local_basis,
    )
    other_leaf = exchange(leaf, core_step)
    rows = jax.ShapeDtypeStruct((quarter, rank), BF16)
    rest = jax.ShapeDtypeStruct((quarter // 2 + 2 * rank, rank), BF16)
    far_rows = call(
        lambda *refs: far_leaf_kernel(chunk, *refs), rest, rest_sent, leaf,
        microseconds=1,
    )
    far_rows = exchange(far_rows, far_step)
    far_leaf = exchange(other_leaf[:rank], far_step)

    rotation, kept = call(
        lambda *refs: pair_kernel(scale, *refs),
        (jax.ShapeDtypeStruct((rank, 2 * rank), BF16), square),
        leaf, other_leaf, slab, other_slab, pair_basis,
    )
    far_rotation = exchange(rotation, far_step)
    other = exchange(kept, far_step)
    lower, upper = call(
        lambda *refs: branch_kernel(chunk, *refs),
        (rows, rows),
        own_rows, near_rows, raw_rows, far_rows, corner_rows, leaf, other_leaf, far_leaf,
        rotation, far_rotation,
        microseconds=1, limit=16 * MIB,
    )
    cross = sum_everywhere(inner_product(lower, upper), core_step, [far_step] + grid_steps)
    return call(
        lambda *refs: root_kernel(scale, chunk, *refs),
        rows,
        kept, other, cross, root_basis, lower, upper,
        limit=16 * MIB,
    )


def solution(mesh):
    in_specs = (P("grid", "snap"), P("snap", None), P(), P())
    out_specs = P(("grid", "snap"), None)
    return jax.shard_map(
        on_device, mesh=mesh, in_specs=in_specs, out_specs=out_specs, check_vma=False
    )
```

```python
import jax
import jax.numpy as jnp
from jax import lax
from jax.experimental import pallas as pl
from jax.experimental.pallas import tpu as pltpu
from jax.sharding import PartitionSpec as P


POWER = 2
NEWTON = 8
F32 = jnp.float32
BF16 = jnp.bfloat16
MIB = 2**20


def permute(value, steps):
    axes = tuple(axis for axis in ("grid", "snap") if any(axis == on for on, _ in steps))
    places = [0]
    for axis in axes:
        mask = sum(2**bit for on, bit in steps if on == axis)
        size = lax.axis_size(axis)
        places = [place * size + (own ^ mask) for place in places for own in range(size)]
    pairs = list(enumerate(places))
    return lax.ppermute(value, axes, pairs)


def exchange(value, step):
    return permute(value, [step])


def bit_of(step):
    axis, bit = step
    return (lax.axis_index(axis) // 2**bit) % 2


def axis_steps(axis):
    return [(axis, bit) for bit in range(lax.axis_size(axis).bit_length() - 1)]


def sum_over(value, steps):
    for step in steps:
        sent = value.astype(BF16)
        received = exchange(sent, step)
        value = sent.astype(F32) + received.astype(F32)
    return value


def sum_everywhere(value, through, steps):
    value = sum_over(value, [through])
    groups = [steps[:2]] + [[step] for step in steps[2:]]
    for group in groups:
        hops = [[step, through] for step in group]
        if len(group) == 2:
            hops.append(group)
        sent = value.astype(BF16)
        received = [permute(sent, hop) for hop in hops]
        value = sum((part.astype(F32) for part in received), sent.astype(F32))
    return value


def split(x):
    high = x.astype(BF16)
    return high, (x - high.astype(F32)).astype(BF16)


def product(a, b, transposed=False):
    return lax.dot_general(
        a, b, (((1,), (1 if transposed else 0,)), ((), ())), preferred_element_type=F32
    )


def inner_product(left, right):
    return lax.dot_general(
        left, right, (((0,), (0,)), ((), ())), preferred_element_type=F32
    )


def subspace_steps(gram, basis, count):
    gram_high, gram_low = split(gram)
    rank = basis.shape[0]
    rows = lax.broadcasted_iota(jnp.int32, (rank, rank), 0)
    columns = lax.broadcasted_iota(jnp.int32, (rank, rank), 1)
    identity = (rows == columns).astype(F32)

    def times_right(x, right):
        out = product(jnp.concatenate(split(x), axis=1), right)
        return out[:, :rank] + out[:, rank:]

    for _ in range(count):
        high, low = split(basis)
        out = product(jnp.concatenate([high, low], axis=0), gram_high)
        image = out[:rank] + out[rank:] + product(high, gram_low)
        size = jnp.sum(image * image) + 1e-06
        image_high, image_low = split(image)
        stacked = jnp.concatenate([image_high, image_low], axis=0)
        out = product(stacked, stacked, transposed=True)
        inner = (out[:rank, :rank] + out[:rank, rank:] + out[rank:, :rank]) * (1.0 / size)
        total = None
        for step in range(NEWTON):
            factor = 1.5 * identity - 0.5 * inner
            row = jnp.concatenate(split(factor), axis=1)
            right = jnp.concatenate([row, row], axis=0)
            if total is None:
                total = factor
                inner = times_right(times_right(inner, right), right)
            elif step < NEWTON - 1:
                both = times_right(jnp.concatenate([inner, total], axis=0), right)
                inner, total = times_right(both[:rank], right), both[rank:]
            else:
                total = times_right(total, right)
        total_high, total_low = split(total * lax.rsqrt(size))
        basis = product(
            jnp.concatenate([total_high, total_low], axis=1),
            jnp.concatenate([image_high, image_high], axis=0),
        ) + product(total_high, image_low)
    return basis


def kept_gram(rotation, gram):
    gram_high, gram_low = split(gram)
    image = product(rotation, gram_high) + product(rotation, gram_low)
    high, low = split(image)
    return product(high, rotation, True) + product(low, rotation, True)


def pack(gram):
    size = gram.shape[0] // 2
    rows = lax.broadcasted_iota(jnp.int32, (size, size), 0)
    columns = lax.broadcasted_iota(jnp.int32, (size, size), 1)
    first, second = gram[:size, :size], gram[size:, size:]
    diagonal = jnp.sum(jnp.where(rows == columns, second, 0.0), axis=0, keepdims=True)
    diagonal = jnp.broadcast_to(diagonal, (8, size))
    low = jnp.concatenate([jnp.where(rows <= columns, first, second), diagonal], axis=0)
    high = jnp.concatenate([gram[:size, size:], diagonal], axis=0)
    return low, high


def unpack(low, high):
    size = low.shape[1]
    rows = lax.broadcasted_iota(jnp.int32, (size, size), 0)
    columns = lax.broadcasted_iota(jnp.int32, (size, size), 1)
    both, cross = low[:size], high[:size]
    flipped = both.T
    first = jnp.where(rows <= columns, both, flipped)
    second = jnp.where(rows > columns, both, flipped)
    diagonal = jnp.broadcast_to(low[size : size + 1], (size, size))
    second = jnp.where(rows == columns, diagonal, second)
    top = jnp.concatenate([first, cross], axis=1)
    return jnp.concatenate([top, jnp.concatenate([cross.T, second], axis=1)], axis=0)


def place_kernel(rows_ref, own_ref, near_ref, corner_ref, raw_ref, rest_ref, semaphores):
    core, far = bit_of(("snap", 0)), bit_of(("snap", 1))
    places = (2 * far + core, 2 * far + 1 - core, 3 - 2 * far - core)
    parts = [(rows_ref.at[place], ref) for place, ref in zip(places, (own_ref, near_ref, corner_ref))]
    place, half = 2 - 2 * far + core, raw_ref.shape[0]
    parts.append((rows_ref.at[place, pl.ds(0, half)], raw_ref))
    parts.append((rows_ref.at[place, pl.ds(half, half)], rest_ref))
    copies = [
        pltpu.make_async_copy(source, target, semaphores.at[number])
        for number, (source, target) in enumerate(parts)
    ]
    for copy in copies:
        copy.start()
    for copy in copies:
        copy.wait()


def turn_kernel(local_ref, pair_ref, root_ref, *turned_refs):
    far = bit_of(("snap", 1))
    turned_refs[0][...] = local_ref[...].T
    turned_refs[1][...] = pair_ref[far].T
    turned_refs[2][...] = root_ref[...].T


def orient_kernel(cross_ref, kept_ref, sent_ref):
    core = bit_of(("snap", 0)) == 1
    rank = kept_ref.shape[0]
    cross = cross_ref[...]
    turned = cross.T
    kept_ref[...] = jnp.where(core, turned[rank:], cross[:rank])
    sent_ref[...] = jnp.where(core, turned[:rank], cross[rank:])


def pack_kernel(side_step, gram_ref, kept_ref, sent_ref):
    side = bit_of(side_step) == 1
    low, high = pack(gram_ref[...])
    kept_ref[...] = jnp.where(side, high, low)
    sent_ref[...] = jnp.where(side, low, high)


def leaf_kernel(scale, side_step, kept_ref, other_ref, start_ref, out_ref):
    side = bit_of(side_step) == 1
    kept, other = kept_ref[...], other_ref[...]
    low = jnp.where(side, other, kept)
    high = jnp.where(side, kept, other)
    gram = unpack(low, high) * scale
    rank = start_ref.shape[0]
    rotation = subspace_steps(gram, start_ref[...], POWER).astype(BF16)
    out_ref[:rank] = rotation
    out_ref[rank:] = jnp.concatenate(split(kept_gram(rotation, gram)), axis=1)


def far_leaf_kernel(chunk, rows_ref, leaf_ref, out_ref):
    rank = leaf_ref.shape[0] // 2
    rotation = leaf_ref[:rank]
    count = rows_ref.shape[0]
    for start in range(0, count, chunk):
        rows = pl.ds(start, chunk)
        out_ref[rows] = product(rows_ref[rows], rotation, True).astype(BF16)
    out_ref[pl.ds(count, rank)] = rotation[:, :rank]
    out_ref[pl.ds(count + rank, rank)] = rotation[:, rank:]


def pair_kernel(
    scale, own_ref, other_ref, own_slab_ref, other_slab_ref, start_ref, out_ref, kept_ref
):
    core = bit_of(("snap", 0)) == 1
    rank = start_ref.shape[0]
    own, other = own_ref[...].astype(F32), other_ref[...].astype(F32)
    first, second = jnp.where(core, other, own), jnp.where(core, own, other)
    own, other = own_slab_ref[...], other_slab_ref[...]
    cross = jnp.concatenate([jnp.where(core, other, own), jnp.where(core, own, other)], axis=0)
    cross_high, cross_low = split(cross * scale)
    first_rotation, second_rotation = first[:rank].astype(BF16), second[:rank].astype(BF16)
    image = product(first_rotation, cross_high) + product(first_rotation, cross_low)
    high, low = split(image)
    cross = product(high, second_rotation, True) + product(low, second_rotation, True)
    first, second = first[rank:], second[rank:]
    top = jnp.concatenate([first[:, :rank] + first[:, rank:], cross], axis=1)
    bottom = jnp.concatenate([cross.T, second[:, :rank] + second[:, rank:]], axis=1)
    gram = jnp.concatenate([top, bottom], axis=0)
    rotation = subspace_steps(gram, start_ref[...], POWER).astype(BF16)
    out_ref[...] = rotation
    kept_ref[...] = kept_gram(rotation, gram)


def branch_kernel(
    chunk, own_ref, near_ref, raw_ref, far_ref, corner_ref, leaf_ref, other_leaf_ref,
    far_other_ref, rotation_ref, far_rotation_ref, lower_ref, upper_ref,
):
    core = bit_of(("snap", 0)) == 1
    high_bit = bit_of(("snap", 1)) == 1
    rank = rotation_ref.shape[0]

    def halves(ref):
        value = ref[...].astype(F32)
        left, right = value[:, :rank], value[:, rank:]
        own, other = jnp.where(core, right, left), jnp.where(core, left, right)
        return own.astype(BF16), other.astype(BF16)

    def rotation(part, leaf_rotation):
        return product(part, leaf_rotation).astype(BF16)

    own_part, near_part = halves(rotation_ref)
    far_part, corner_part = halves(far_rotation_ref)
    own, near = rotation(own_part, leaf_ref[:rank]), rotation(near_part, other_leaf_ref[:rank])
    half = raw_ref.shape[0]

    def joined(ref, place):
        pieces = [ref[pl.ds(place + offset, rank)] for offset in (0, rank)]
        return jnp.concatenate(pieces, axis=1)

    far = rotation(far_part, joined(far_ref, half))
    corner = rotation(corner_part, joined(far_other_ref, 0))
    for start in range(0, own_ref.shape[0], chunk):
        rows = pl.ds(start, chunk)
        mine = product(own_ref[rows], own, True) + product(near_ref[rows], near, True)
        if start < half:
            theirs = product(raw_ref[rows], far, True)
        else:
            theirs = product(far_ref[pl.ds(start - half, chunk)], far_part, True)
        theirs = theirs + product(corner_ref[rows], corner, True)
        lower_ref[rows] = jnp.where(high_bit, theirs, mine).astype(BF16)
        upper_ref[rows] = jnp.where(high_bit, mine, theirs).astype(BF16)


def root_kernel(
    scale, chunk, kept_ref, other_ref, cross_ref, start_ref, lower_ref, upper_ref, out_ref
):
    high_bit = bit_of(("snap", 1)) == 1
    kept, other = kept_ref[...], other_ref[...]
    cross = cross_ref[...] * scale
    top = jnp.concatenate([jnp.where(high_bit, other, kept), cross], axis=1)
    bottom = jnp.concatenate([cross.T, jnp.where(high_bit, kept, other)], axis=1)
    gram = jnp.concatenate([top, bottom], axis=0)
    rotation = subspace_steps(gram, start_ref[...], POWER).astype(BF16)
    for start in range(0, lower_ref.shape[0], chunk):
        rows = pl.ds(start, chunk)
        root = jnp.concatenate([lower_ref[rows], upper_ref[rows]], axis=1)
        out_ref[rows] = product(root, rotation, True).astype(BF16)


def call(kernel, out_shape, *operands, microseconds=8, limit=8 * MIB):
    vmem = pl.BlockSpec(memory_space=pltpu.VMEM)
    return pl.pallas_call(
        kernel,
        out_shape=out_shape,
        in_specs=[vmem] * len(operands),
        out_specs=jax.tree.map(lambda _: vmem, out_shape),
        compiler_params=pltpu.CompilerParams(vmem_limit_bytes=limit),
        cost_estimate=pl.CostEstimate(
            flops=microseconds * 10**9, bytes_accessed=MIB, transcendentals=0
        ),
    )(*operands)


def on_device(fields, start_local, start_pair, start_root):
    local_rows, snaps = fields.shape
    rank = start_local.shape[1]
    quarter = local_rows // 4
    chunk = quarter // 4
    scale = 1.0 / (local_rows * lax.axis_size("grid"))
    core_step, far_step = ("snap", 0), ("snap", 1)
    grid_steps = axis_steps("grid")

    rows = jax.ShapeDtypeStruct((quarter, snaps), fields.dtype)
    half_rows = jax.ShapeDtypeStruct((quarter // 2, snaps), fields.dtype)
    placed = pl.pallas_call(
        place_kernel,
        out_shape=(rows,) * 3 + (half_rows,) * 2,
        in_specs=[pl.BlockSpec(memory_space=pltpu.HBM)],
        out_specs=(pl.BlockSpec(memory_space=pltpu.VMEM),) * 5,
        scratch_shapes=[pltpu.SemaphoreType.DMA((5,))],
        name="place",
        compiler_params=pltpu.CompilerParams(vmem_limit_bytes=48 * MIB),
    )(fields.reshape(4, quarter, snaps))
    own_rows, near_sent, corner_sent, raw_sent, rest_sent = placed
    near_rows = exchange(near_sent, core_step)
    far_core_rows = exchange(corner_sent, core_step)
    corner_rows = exchange(far_core_rows, far_step)
    raw_rows = exchange(raw_sent, far_step)

    piece = jax.ShapeDtypeStruct((rank + 8, rank), F32)
    kept, sent = call(
        lambda *refs: pack_kernel(grid_steps[0], *refs),
        (piece, piece), sum(inner_product(rows, rows) for rows in placed),
        microseconds=1, limit=2 * MIB,
    )
    kept = kept + exchange(sent, grid_steps[0])
    for step in grid_steps[1:]:
        kept = kept + exchange(kept, step)
    other = exchange(kept, grid_steps[0])

    cross = inner_product(own_rows, near_rows)
    cross = cross + inner_product(raw_sent, far_core_rows[: quarter // 2])
    cross = cross + inner_product(rest_sent, far_core_rows[quarter // 2 :])
    half = jax.ShapeDtypeStruct((rank, snaps), F32)
    slab, slab_sent = call(orient_kernel, (half, half), cross, microseconds=1)
    slab = slab + exchange(slab_sent, core_step)
    slab = sum_over(slab, grid_steps)
    other_slab = exchange(slab, core_step)

    turned = jax.ShapeDtypeStruct((rank, snaps), F32)
    turned_pair = jax.ShapeDtypeStruct((rank, 2 * rank), F32)
    local_basis, pair_basis, root_basis = call(
        turn_kernel, (turned, turned_pair, turned_pair),
        start_local, start_pair, start_root,
        microseconds=1,
    )
    square = jax.ShapeDtypeStruct((rank, rank), F32)
    leaf = call(
        lambda *refs: leaf_kernel(scale, grid_steps[0], *refs),
        jax.ShapeDtypeStruct((2 * rank, snaps), BF16),
        kept, other, local_basis,
    )
    other_leaf = exchange(leaf, core_step)
    rows = jax.ShapeDtypeStruct((quarter, rank), BF16)
    rest = jax.ShapeDtypeStruct((quarter // 2 + 2 * rank, rank), BF16)
    far_rows = call(
        lambda *refs: far_leaf_kernel(chunk, *refs), rest, rest_sent, leaf,
        microseconds=1,
    )
    far_rows = exchange(far_rows, far_step)
    far_other = exchange(far_rows[quarter // 2 :], core_step)

    rotation, kept = call(
        lambda *refs: pair_kernel(scale, *refs),
        (jax.ShapeDtypeStruct((rank, 2 * rank), BF16), square),
        leaf, other_leaf, slab, other_slab, pair_basis,
    )
    far_rotation = exchange(rotation, far_step)
    other = exchange(kept, far_step)
    lower, upper = call(
        lambda *refs: branch_kernel(chunk, *refs),
        (rows, rows),
        own_rows, near_rows, raw_rows, far_rows, corner_rows, leaf, other_leaf, far_other,
        rotation, far_rotation,
        microseconds=1, limit=16 * MIB,
    )
    cross = sum_everywhere(inner_product(lower, upper), core_step, [far_step] + grid_steps)
    return call(
        lambda *refs: root_kernel(scale, chunk, *refs),
        rows,
        kept, other, cross, root_basis, lower, upper,
        limit=16 * MIB,
    )


def solution(mesh):
    in_specs = (P("grid", "snap"), P("snap", None), P(), P())
    out_specs = P(("grid", "snap"), None)
    return jax.shard_map(
        on_device, mesh=mesh, in_specs=in_specs, out_specs=out_specs, check_vma=False
    )
```

```python
import jax
import jax.numpy as jnp
from jax import lax
from jax.experimental import pallas as pl
from jax.experimental.pallas import tpu as pltpu
from jax.sharding import PartitionSpec as P


POWER = 2
NEWTON = 8
F32 = jnp.float32
BF16 = jnp.bfloat16
MIB = 2**20


def permute(value, steps):
    axes = tuple(axis for axis in ("grid", "snap") if any(axis == on for on, _ in steps))
    places = [0]
    for axis in axes:
        mask = sum(2**bit for on, bit in steps if on == axis)
        size = lax.axis_size(axis)
        places = [place * size + (own ^ mask) for place in places for own in range(size)]
    pairs = list(enumerate(places))
    return lax.ppermute(value, axes, pairs)


def exchange(value, step):
    return permute(value, [step])


def bit_of(step):
    axis, bit = step
    return (lax.axis_index(axis) // 2**bit) % 2


def axis_steps(axis):
    return [(axis, bit) for bit in range(lax.axis_size(axis).bit_length() - 1)]


def sum_over(value, steps):
    for step in steps:
        sent = value.astype(BF16)
        received = exchange(sent, step)
        value = sent.astype(F32) + received.astype(F32)
    return value


def sum_everywhere(value, through, steps):
    value = sum_over(value, [through])
    groups = [steps[start : start + 2] for start in range(0, len(steps), 2)]
    for group in groups:
        hops = [[step, through] for step in group]
        if len(group) == 2:
            hops.append(group)
        sent = value.astype(BF16)
        received = [permute(sent, hop) for hop in hops]
        value = sum((part.astype(F32) for part in received), sent.astype(F32))
    return value


def split(x):
    high = x.astype(BF16)
    return high, (x - high.astype(F32)).astype(BF16)


def product(a, b, transposed=False):
    return lax.dot_general(
        a, b, (((1,), (1 if transposed else 0,)), ((), ())), preferred_element_type=F32
    )


def inner_product(left, right):
    return lax.dot_general(
        left, right, (((0,), (0,)), ((), ())), preferred_element_type=F32
    )


def subspace_steps(gram, basis, count):
    gram_high, gram_low = split(gram)
    rank = basis.shape[0]
    rows = lax.broadcasted_iota(jnp.int32, (rank, rank), 0)
    columns = lax.broadcasted_iota(jnp.int32, (rank, rank), 1)
    identity = (rows == columns).astype(F32)

    def times_right(x, right):
        out = product(jnp.concatenate(split(x), axis=1), right)
        return out[:, :rank] + out[:, rank:]

    for _ in range(count):
        high, low = split(basis)
        out = product(jnp.concatenate([high, low], axis=0), gram_high)
        image = out[:rank] + out[rank:] + product(high, gram_low)
        size = jnp.sum(image * image) + 1e-06
        image_high, image_low = split(image)
        stacked = jnp.concatenate([image_high, image_low], axis=0)
        out = product(stacked, stacked, transposed=True)
        inner = (out[:rank, :rank] + out[:rank, rank:] + out[rank:, :rank]) * (1.0 / size)
        total = None
        for step in range(NEWTON):
            factor = 1.5 * identity - 0.5 * inner
            row = jnp.concatenate(split(factor), axis=1)
            right = jnp.concatenate([row, row], axis=0)
            if total is None:
                total = factor
                inner = times_right(times_right(inner, right), right)
            elif step < NEWTON - 1:
                both = times_right(jnp.concatenate([inner, total], axis=0), right)
                inner, total = times_right(both[:rank], right), both[rank:]
            else:
                total = times_right(total, right)
        total_high, total_low = split(total * lax.rsqrt(size))
        basis = product(
            jnp.concatenate([total_high, total_low], axis=1),
            jnp.concatenate([image_high, image_high], axis=0),
        ) + product(total_high, image_low)
    return basis


def kept_gram(rotation, gram):
    gram_high, gram_low = split(gram)
    image = product(rotation, gram_high) + product(rotation, gram_low)
    high, low = split(image)
    return product(high, rotation, True) + product(low, rotation, True)


def pack(gram):
    size = gram.shape[0] // 2
    rows = lax.broadcasted_iota(jnp.int32, (size, size), 0)
    columns = lax.broadcasted_iota(jnp.int32, (size, size), 1)
    first, second = gram[:size, :size], gram[size:, size:]
    diagonal = jnp.sum(jnp.where(rows == columns, second, 0.0), axis=0, keepdims=True)
    diagonal = jnp.broadcast_to(diagonal, (8, size))
    low = jnp.concatenate([jnp.where(rows <= columns, first, second), diagonal], axis=0)
    high = jnp.concatenate([gram[:size, size:], diagonal], axis=0)
    return low, high


def unpack(low, high):
    size = low.shape[1]
    rows = lax.broadcasted_iota(jnp.int32, (size, size), 0)
    columns = lax.broadcasted_iota(jnp.int32, (size, size), 1)
    both, cross = low[:size], high[:size]
    flipped = both.T
    first = jnp.where(rows <= columns, both, flipped)
    second = jnp.where(rows > columns, both, flipped)
    diagonal = jnp.broadcast_to(low[size : size + 1], (size, size))
    second = jnp.where(rows == columns, diagonal, second)
    top = jnp.concatenate([first, cross], axis=1)
    return jnp.concatenate([top, jnp.concatenate([cross.T, second], axis=1)], axis=0)


def place_kernel(rows_ref, own_ref, near_ref, corner_ref, raw_ref, rest_ref, semaphores):
    core, far = bit_of(("snap", 0)), bit_of(("snap", 1))
    places = (2 * far + core, 2 * far + 1 - core, 3 - 2 * far - core)
    parts = [(rows_ref.at[place], ref) for place, ref in zip(places, (own_ref, near_ref, corner_ref))]
    place, half = 2 - 2 * far + core, raw_ref.shape[0]
    parts.append((rows_ref.at[place, pl.ds(0, half)], raw_ref))
    parts.append((rows_ref.at[place, pl.ds(half, half)], rest_ref))
    copies = [
        pltpu.make_async_copy(source, target, semaphores.at[number])
        for number, (source, target) in enumerate(parts)
    ]
    for copy in copies:
        copy.start()
    for copy in copies:
        copy.wait()


def turn_kernel(local_ref, pair_ref, root_ref, *turned_refs):
    far = bit_of(("snap", 1))
    turned_refs[0][...] = local_ref[...].T
    turned_refs[1][...] = pair_ref[far].T
    turned_refs[2][...] = root_ref[...].T


def orient_kernel(cross_ref, kept_ref, sent_ref):
    core = bit_of(("snap", 0)) == 1
    rank = kept_ref.shape[0]
    cross = cross_ref[...]
    turned = cross.T
    kept_ref[...] = jnp.where(core, turned[rank:], cross[:rank])
    sent_ref[...] = jnp.where(core, turned[:rank], cross[rank:])


def pack_kernel(side_step, gram_ref, kept_ref, sent_ref):
    side = bit_of(side_step) == 1
    low, high = pack(gram_ref[...])
    kept_ref[...] = jnp.where(side, high, low)
    sent_ref[...] = jnp.where(side, low, high)


def leaf_kernel(scale, side_step, kept_ref, other_ref, start_ref, out_ref):
    side = bit_of(side_step) == 1
    kept, other = kept_ref[...], other_ref[...]
    low = jnp.where(side, other, kept)
    high = jnp.where(side, kept, other)
    gram = unpack(low, high) * scale
    rank = start_ref.shape[0]
    rotation = subspace_steps(gram, start_ref[...], POWER).astype(BF16)
    out_ref[:rank] = rotation
    out_ref[rank:] = jnp.concatenate(split(kept_gram(rotation, gram)), axis=1)


def far_leaf_kernel(chunk, rows_ref, leaf_ref, out_ref):
    rank = leaf_ref.shape[0] // 2
    rotation = leaf_ref[:rank]
    count = rows_ref.shape[0]
    for start in range(0, count, chunk):
        rows = pl.ds(start, chunk)
        out_ref[rows] = product(rows_ref[rows], rotation, True).astype(BF16)
    out_ref[pl.ds(count, rank)] = rotation[:, :rank]
    out_ref[pl.ds(count + rank, rank)] = rotation[:, rank:]


def pair_kernel(
    scale, own_ref, other_ref, own_slab_ref, other_slab_ref, start_ref, out_ref, gram_ref
):
    core = bit_of(("snap", 0)) == 1
    rank = start_ref.shape[0]
    own, other = own_ref[...].astype(F32), other_ref[...].astype(F32)
    first, second = jnp.where(core, other, own), jnp.where(core, own, other)
    own, other = own_slab_ref[...], other_slab_ref[...]
    cross = jnp.concatenate([jnp.where(core, other, own), jnp.where(core, own, other)], axis=0)
    cross_high, cross_low = split(cross * scale)
    first_rotation, second_rotation = first[:rank].astype(BF16), second[:rank].astype(BF16)
    image = product(first_rotation, cross_high) + product(first_rotation, cross_low)
    high, low = split(image)
    cross = product(high, second_rotation, True) + product(low, second_rotation, True)
    first, second = first[rank:], second[rank:]
    top = jnp.concatenate([first[:, :rank] + first[:, rank:], cross], axis=1)
    bottom = jnp.concatenate([cross.T, second[:, :rank] + second[:, rank:]], axis=1)
    gram = jnp.concatenate([top, bottom], axis=0)
    gram_ref[...] = gram
    out_ref[...] = subspace_steps(gram, start_ref[...], POWER).astype(BF16)


def kept_kernel(rotation_ref, gram_ref, kept_ref):
    kept_ref[...] = kept_gram(rotation_ref[...], gram_ref[...])


def branch_kernel(
    chunk, own_ref, near_ref, raw_ref, far_ref, corner_ref, leaf_ref, other_leaf_ref,
    far_other_ref, rotation_ref, far_rotation_ref, lower_ref, upper_ref,
):
    core = bit_of(("snap", 0)) == 1
    high_bit = bit_of(("snap", 1)) == 1
    rank = rotation_ref.shape[0]

    def halves(ref):
        value = ref[...].astype(F32)
        left, right = value[:, :rank], value[:, rank:]
        own, other = jnp.where(core, right, left), jnp.where(core, left, right)
        return own.astype(BF16), other.astype(BF16)

    def rotation(part, leaf_rotation):
        return product(part, leaf_rotation).astype(BF16)

    own_part, near_part = halves(rotation_ref)
    far_part, corner_part = halves(far_rotation_ref)
    own, near = rotation(own_part, leaf_ref[:rank]), rotation(near_part, other_leaf_ref[:rank])
    half = raw_ref.shape[0]

    def joined(ref, place):
        pieces = [ref[pl.ds(place + offset, rank)] for offset in (0, rank)]
        return jnp.concatenate(pieces, axis=1)

    far = rotation(far_part, joined(far_ref, half))
    corner = rotation(corner_part, joined(far_other_ref, 0))
    for start in range(0, own_ref.shape[0], chunk):
        rows = pl.ds(start, chunk)
        mine = product(own_ref[rows], own, True) + product(near_ref[rows], near, True)
        if start < half:
            theirs = product(raw_ref[rows], far, True)
        else:
            theirs = product(far_ref[pl.ds(start - half, chunk)], far_part, True)
        theirs = theirs + product(corner_ref[rows], corner, True)
        lower_ref[rows] = jnp.where(high_bit, theirs, mine).astype(BF16)
        upper_ref[rows] = jnp.where(high_bit, mine, theirs).astype(BF16)


def root_kernel(
    scale, chunk, kept_ref, other_ref, cross_ref, start_ref, lower_ref, upper_ref, out_ref
):
    high_bit = bit_of(("snap", 1)) == 1
    kept, other = kept_ref[...], other_ref[...]
    cross = cross_ref[...] * scale
    top = jnp.concatenate([jnp.where(high_bit, other, kept), cross], axis=1)
    bottom = jnp.concatenate([cross.T, jnp.where(high_bit, kept, other)], axis=1)
    gram = jnp.concatenate([top, bottom], axis=0)
    rotation = subspace_steps(gram, start_ref[...], POWER).astype(BF16)
    for start in range(0, lower_ref.shape[0], chunk):
        rows = pl.ds(start, chunk)
        root = jnp.concatenate([lower_ref[rows], upper_ref[rows]], axis=1)
        out_ref[rows] = product(root, rotation, True).astype(BF16)


def call(kernel, out_shape, *operands, microseconds=8, limit=8 * MIB):
    vmem = pl.BlockSpec(memory_space=pltpu.VMEM)
    return pl.pallas_call(
        kernel,
        out_shape=out_shape,
        in_specs=[vmem] * len(operands),
        out_specs=jax.tree.map(lambda _: vmem, out_shape),
        compiler_params=pltpu.CompilerParams(vmem_limit_bytes=limit),
        cost_estimate=pl.CostEstimate(
            flops=microseconds * 10**9, bytes_accessed=MIB, transcendentals=0
        ),
    )(*operands)


def on_device(fields, start_local, start_pair, start_root):
    local_rows, snaps = fields.shape
    rank = start_local.shape[1]
    quarter = local_rows // 4
    chunk = quarter // 4
    scale = 1.0 / (local_rows * lax.axis_size("grid"))
    core_step, far_step = ("snap", 0), ("snap", 1)
    grid_steps = axis_steps("grid")

    rows = jax.ShapeDtypeStruct((quarter, snaps), fields.dtype)
    half_rows = jax.ShapeDtypeStruct((quarter // 2, snaps), fields.dtype)
    placed = pl.pallas_call(
        place_kernel,
        out_shape=(rows,) * 3 + (half_rows,) * 2,
        in_specs=[pl.BlockSpec(memory_space=pltpu.HBM)],
        out_specs=(pl.BlockSpec(memory_space=pltpu.VMEM),) * 5,
        scratch_shapes=[pltpu.SemaphoreType.DMA((5,))],
        name="place",
        compiler_params=pltpu.CompilerParams(vmem_limit_bytes=48 * MIB),
    )(fields.reshape(4, quarter, snaps))
    own_rows, near_sent, corner_sent, raw_sent, rest_sent = placed
    near_rows = exchange(near_sent, core_step)
    far_core_rows = exchange(corner_sent, core_step)
    corner_rows = exchange(far_core_rows, far_step)
    raw_rows = exchange(raw_sent, far_step)

    piece = jax.ShapeDtypeStruct((rank + 8, rank), F32)
    kept, sent = call(
        lambda *refs: pack_kernel(grid_steps[0], *refs),
        (piece, piece), sum(inner_product(rows, rows) for rows in placed),
        microseconds=1, limit=2 * MIB,
    )
    kept = kept + exchange(sent, grid_steps[0])
    for step in grid_steps[1:]:
        kept = kept + exchange(kept, step)
    other = exchange(kept, grid_steps[0])

    cross = inner_product(own_rows, near_rows)
    cross = cross + inner_product(raw_sent, far_core_rows[: quarter // 2])
    cross = cross + inner_product(rest_sent, far_core_rows[quarter // 2 :])
    half = jax.ShapeDtypeStruct((rank, snaps), F32)
    slab, slab_sent = call(orient_kernel, (half, half), cross, microseconds=1)
    slab = slab + exchange(slab_sent, core_step)
    slab = sum_over(slab, grid_steps)
    other_slab = exchange(slab, core_step)

    turned = jax.ShapeDtypeStruct((rank, snaps), F32)
    turned_pair = jax.ShapeDtypeStruct((rank, 2 * rank), F32)
    local_basis, pair_basis, root_basis = call(
        turn_kernel, (turned, turned_pair, turned_pair),
        start_local, start_pair, start_root,
        microseconds=1,
    )
    square = jax.ShapeDtypeStruct((rank, rank), F32)
    leaf = call(
        lambda *refs: leaf_kernel(scale, grid_steps[0], *refs),
        jax.ShapeDtypeStruct((2 * rank, snaps), BF16),
        kept, other, local_basis,
    )
    other_leaf = exchange(leaf, core_step)
    rows = jax.ShapeDtypeStruct((quarter, rank), BF16)
    rest = jax.ShapeDtypeStruct((quarter // 2 + 2 * rank, rank), BF16)
    far_rows = call(
        lambda *refs: far_leaf_kernel(chunk, *refs), rest, rest_sent, leaf,
        microseconds=1,
    )
    far_rows = exchange(far_rows, far_step)
    far_other = exchange(far_rows[quarter // 2 :], core_step)

    rotation, gram = call(
        lambda *refs: pair_kernel(scale, *refs),
        (
            jax.ShapeDtypeStruct((rank, 2 * rank), BF16),
            jax.ShapeDtypeStruct((2 * rank, 2 * rank), F32),
        ),
        leaf, other_leaf, slab, other_slab, pair_basis,
    )
    kept = call(kept_kernel, square, rotation, gram, microseconds=1)
    far_rotation = permute(rotation, [far_step, core_step])
    other = permute(kept, [far_step, core_step])
    lower, upper = call(
        lambda *refs: branch_kernel(chunk, *refs),
        (rows, rows),
        own_rows, near_rows, raw_rows, far_rows, corner_rows, leaf, other_leaf, far_other,
        rotation, far_rotation,
        microseconds=1, limit=16 * MIB,
    )
    steps = grid_steps[:2] + [far_step] + grid_steps[2:]
    cross = sum_everywhere(inner_product(lower, upper), core_step, steps)
    return call(
        lambda *refs: root_kernel(scale, chunk, *refs),
        rows,
        kept, other, cross, root_basis, lower, upper,
        limit=16 * MIB,
    )


def solution(mesh):
    in_specs = (P("grid", "snap"), P("snap", None), P(), P())
    out_specs = P(("grid", "snap"), None)
    return jax.shard_map(
        on_device, mesh=mesh, in_specs=in_specs, out_specs=out_specs, check_vma=False
    )
```

```python
import jax
import jax.numpy as jnp
from jax import lax
from jax.experimental import pallas as pl
from jax.experimental.pallas import tpu as pltpu
from jax.sharding import PartitionSpec as P


POWER = 2
NEWTON = 8
F32 = jnp.float32
BF16 = jnp.bfloat16
MIB = 2**20


def permute(value, steps):
    axes = tuple(axis for axis in ("grid", "snap") if any(axis == on for on, _ in steps))
    places = [0]
    for axis in axes:
        mask = sum(2**bit for on, bit in steps if on == axis)
        size = lax.axis_size(axis)
        places = [place * size + (own ^ mask) for place in places for own in range(size)]
    pairs = list(enumerate(places))
    return lax.ppermute(value, axes, pairs)


def exchange(value, step):
    return permute(value, [step])


def bit_of(step):
    axis, bit = step
    return (lax.axis_index(axis) // 2**bit) % 2


def axis_steps(axis):
    return [(axis, bit) for bit in range(lax.axis_size(axis).bit_length() - 1)]


def sum_over(value, steps):
    for step in steps:
        sent = value.astype(BF16)
        received = exchange(sent, step)
        value = sent.astype(F32) + received.astype(F32)
    return value


def sum_everywhere(value, through, steps):
    value = sum_over(value, [through])
    groups = [steps[:2]] + [[step] for step in steps[2:]]
    for group in groups:
        hops = [[step, through] for step in group]
        if len(group) == 2:
            hops.append(group)
        sent = value.astype(BF16)
        received = [permute(sent, hop) for hop in hops]
        value = sum((part.astype(F32) for part in received), sent.astype(F32))
    return value


def split(x):
    high = x.astype(BF16)
    return high, (x - high.astype(F32)).astype(BF16)


def product(a, b, transposed=False):
    return lax.dot_general(
        a, b, (((1,), (1 if transposed else 0,)), ((), ())), preferred_element_type=F32
    )


def inner_product(left, right):
    return lax.dot_general(
        left, right, (((0,), (0,)), ((), ())), preferred_element_type=F32
    )


def subspace_steps(gram, basis, count):
    gram_high, gram_low = split(gram)
    rank = basis.shape[0]
    rows = lax.broadcasted_iota(jnp.int32, (rank, rank), 0)
    columns = lax.broadcasted_iota(jnp.int32, (rank, rank), 1)
    identity = (rows == columns).astype(F32)

    def times_right(x, right):
        out = product(jnp.concatenate(split(x), axis=1), right)
        return out[:, :rank] + out[:, rank:]

    for _ in range(count):
        high, low = split(basis)
        out = product(jnp.concatenate([high, low], axis=0), gram_high)
        image = out[:rank] + out[rank:] + product(high, gram_low)
        size = jnp.sum(image * image) + 1e-06
        image_high, image_low = split(image)
        stacked = jnp.concatenate([image_high, image_low], axis=0)
        out = product(stacked, stacked, transposed=True)
        inner = (out[:rank, :rank] + out[:rank, rank:] + out[rank:, :rank]) * (1.0 / size)
        total = None
        for step in range(NEWTON):
            factor = 1.5 * identity - 0.5 * inner
            row = jnp.concatenate(split(factor), axis=1)
            right = jnp.concatenate([row, row], axis=0)
            if total is None:
                total = factor
                inner = times_right(times_right(inner, right), right)
            elif step < NEWTON - 1:
                both = times_right(jnp.concatenate([inner, total], axis=0), right)
                inner, total = times_right(both[:rank], right), both[rank:]
            else:
                total = times_right(total, right)
        total_high, total_low = split(total * lax.rsqrt(size))
        basis = product(
            jnp.concatenate([total_high, total_low], axis=1),
            jnp.concatenate([image_high, image_high], axis=0),
        ) + product(total_high, image_low)
    return basis


def kept_gram(rotation, gram):
    gram_high, gram_low = split(gram)
    image = product(rotation, gram_high) + product(rotation, gram_low)
    high, low = split(image)
    return product(high, rotation, True) + product(low, rotation, True)


def pack(gram):
    size = gram.shape[0] // 2
    rows = lax.broadcasted_iota(jnp.int32, (size, size), 0)
    columns = lax.broadcasted_iota(jnp.int32, (size, size), 1)
    first, second = gram[:size, :size], gram[size:, size:]
    diagonal = jnp.sum(jnp.where(rows == columns, second, 0.0), axis=0, keepdims=True)
    diagonal = jnp.broadcast_to(diagonal, (8, size))
    low = jnp.concatenate([jnp.where(rows <= columns, first, second), diagonal], axis=0)
    high = jnp.concatenate([gram[:size, size:], diagonal], axis=0)
    return low, high


def unpack(low, high):
    size = low.shape[1]
    rows = lax.broadcasted_iota(jnp.int32, (size, size), 0)
    columns = lax.broadcasted_iota(jnp.int32, (size, size), 1)
    both, cross = low[:size], high[:size]
    flipped = both.T
    first = jnp.where(rows <= columns, both, flipped)
    second = jnp.where(rows > columns, both, flipped)
    diagonal = jnp.broadcast_to(low[size : size + 1], (size, size))
    second = jnp.where(rows == columns, diagonal, second)
    top = jnp.concatenate([first, cross], axis=1)
    return jnp.concatenate([top, jnp.concatenate([cross.T, second], axis=1)], axis=0)


def place_kernel(rows_ref, all_ref, own_ref, near_ref, corner_ref, raw_ref, rest_ref, semaphores):
    core, far = bit_of(("snap", 0)), bit_of(("snap", 1))
    quarters = (
        (2 * far + 1 - core, (near_ref,)),
        (3 - 2 * far - core, (corner_ref,)),
        (2 - 2 * far + core, (raw_ref, rest_ref)),
        (2 * far + core, (own_ref,)),
    )
    copies = [
        pltpu.make_async_copy(rows_ref.at[place], all_ref.at[number], semaphores.at[number])
        for number, (place, _) in enumerate(quarters)
    ]
    for copy in copies:
        copy.start()
    moves = []
    for number, (_, targets) in enumerate(quarters):
        copies[number].wait()
        start = 0
        for target in targets:
            source = all_ref.at[number, pl.ds(start, target.shape[0])]
            moves.append(pltpu.make_async_copy(source, target, semaphores.at[4 + len(moves)]))
            moves[-1].start()
            start += target.shape[0]
    for move in moves:
        move.wait()


def turn_kernel(local_ref, pair_ref, root_ref, *turned_refs):
    far = bit_of(("snap", 1))
    turned_refs[0][...] = local_ref[...].T
    turned_refs[1][...] = pair_ref[far].T
    turned_refs[2][...] = root_ref[...].T


def orient_kernel(cross_ref, kept_ref, sent_ref):
    core = bit_of(("snap", 0)) == 1
    rank = kept_ref.shape[0]
    cross = cross_ref[...]
    turned = cross.T
    kept_ref[...] = jnp.where(core, turned[rank:], cross[:rank])
    sent_ref[...] = jnp.where(core, turned[:rank], cross[rank:])


def pack_kernel(side_step, gram_ref, kept_ref, sent_ref):
    side = bit_of(side_step) == 1
    low, high = pack(gram_ref[...])
    kept_ref[...] = jnp.where(side, high, low)
    sent_ref[...] = jnp.where(side, low, high)


def leaf_kernel(scale, side_step, kept_ref, other_ref, start_ref, out_ref):
    side = bit_of(side_step) == 1
    kept, other = kept_ref[...], other_ref[...]
    low = jnp.where(side, other, kept)
    high = jnp.where(side, kept, other)
    gram = unpack(low, high) * scale
    rank = start_ref.shape[0]
    rotation = subspace_steps(gram, start_ref[...], POWER).astype(BF16)
    out_ref[:rank] = rotation
    out_ref[rank:] = jnp.concatenate(split(kept_gram(rotation, gram)), axis=1)


def far_leaf_kernel(chunk, rows_ref, leaf_ref, out_ref):
    rank = leaf_ref.shape[0] // 2
    rotation = leaf_ref[:rank]
    count = rows_ref.shape[0]
    for start in range(0, count, chunk):
        rows = pl.ds(start, chunk)
        out_ref[rows] = product(rows_ref[rows], rotation, True).astype(BF16)
    out_ref[pl.ds(count, rank)] = rotation[:, :rank]
    out_ref[pl.ds(count + rank, rank)] = rotation[:, rank:]


def pair_kernel(
    scale, own_ref, other_ref, own_slab_ref, other_slab_ref, start_ref, out_ref, gram_ref
):
    core = bit_of(("snap", 0)) == 1
    rank = start_ref.shape[0]
    own, other = own_ref[...].astype(F32), other_ref[...].astype(F32)
    first, second = jnp.where(core, other, own), jnp.where(core, own, other)
    own, other = own_slab_ref[...], other_slab_ref[...]
    cross = jnp.concatenate([jnp.where(core, other, own), jnp.where(core, own, other)], axis=0)
    cross_high, cross_low = split(cross * scale)
    first_rotation, second_rotation = first[:rank].astype(BF16), second[:rank].astype(BF16)
    image = product(first_rotation, cross_high) + product(first_rotation, cross_low)
    high, low = split(image)
    cross = product(high, second_rotation, True) + product(low, second_rotation, True)
    first, second = first[rank:], second[rank:]
    top = jnp.concatenate([first[:, :rank] + first[:, rank:], cross], axis=1)
    bottom = jnp.concatenate([cross.T, second[:, :rank] + second[:, rank:]], axis=1)
    gram = jnp.concatenate([top, bottom], axis=0)
    gram_ref[...] = gram
    out_ref[...] = subspace_steps(gram, start_ref[...], POWER).astype(BF16)


def kept_kernel(rotation_ref, gram_ref, kept_ref):
    kept_ref[...] = kept_gram(rotation_ref[...], gram_ref[...])


def branch_kernel(
    chunk, own_ref, near_ref, raw_ref, far_ref, corner_ref, leaf_ref, other_leaf_ref,
    far_other_ref, rotation_ref, far_rotation_ref, lower_ref, upper_ref,
):
    core = bit_of(("snap", 0)) == 1
    high_bit = bit_of(("snap", 1)) == 1
    rank = rotation_ref.shape[0]

    def halves(ref):
        value = ref[...].astype(F32)
        left, right = value[:, :rank], value[:, rank:]
        own, other = jnp.where(core, right, left), jnp.where(core, left, right)
        return own.astype(BF16), other.astype(BF16)

    def rotation(part, leaf_rotation):
        return product(part, leaf_rotation).astype(BF16)

    own_part, near_part = halves(rotation_ref)
    far_part, corner_part = halves(far_rotation_ref)
    own, near = rotation(own_part, leaf_ref[:rank]), rotation(near_part, other_leaf_ref[:rank])
    raw, below = raw_ref.shape[0], own_ref.shape[0] - raw_ref.shape[0]

    def joined(ref, place):
        pieces = [ref[pl.ds(place + offset, rank)] for offset in (0, rank)]
        return jnp.concatenate(pieces, axis=1)

    far = rotation(far_part, joined(far_ref, below))
    corner = rotation(corner_part, joined(far_other_ref, 0))
    for start in range(0, own_ref.shape[0], chunk):
        rows = pl.ds(start, chunk)
        mine = product(own_ref[rows], own, True) + product(near_ref[rows], near, True)
        if start < raw:
            theirs = product(raw_ref[rows], far, True)
        else:
            theirs = product(far_ref[pl.ds(start - raw, chunk)], far_part, True)
        theirs = theirs + product(corner_ref[rows], corner, True)
        lower_ref[rows] = jnp.where(high_bit, theirs, mine).astype(BF16)
        upper_ref[rows] = jnp.where(high_bit, mine, theirs).astype(BF16)


def root_kernel(
    scale, chunk, kept_ref, other_ref, cross_ref, start_ref, lower_ref, upper_ref, out_ref
):
    high_bit = bit_of(("snap", 1)) == 1
    kept, other = kept_ref[...], other_ref[...]
    cross = cross_ref[...] * scale
    top = jnp.concatenate([jnp.where(high_bit, other, kept), cross], axis=1)
    bottom = jnp.concatenate([cross.T, jnp.where(high_bit, kept, other)], axis=1)
    gram = jnp.concatenate([top, bottom], axis=0)
    rotation = subspace_steps(gram, start_ref[...], POWER).astype(BF16)
    for start in range(0, lower_ref.shape[0], chunk):
        rows = pl.ds(start, chunk)
        root = jnp.concatenate([lower_ref[rows], upper_ref[rows]], axis=1)
        out_ref[rows] = product(root, rotation, True).astype(BF16)


def call(kernel, out_shape, *operands, microseconds=8, limit=8 * MIB):
    vmem = pl.BlockSpec(memory_space=pltpu.VMEM)
    return pl.pallas_call(
        kernel,
        out_shape=out_shape,
        in_specs=[vmem] * len(operands),
        out_specs=jax.tree.map(lambda _: vmem, out_shape),
        compiler_params=pltpu.CompilerParams(vmem_limit_bytes=limit),
        cost_estimate=pl.CostEstimate(
            flops=microseconds * 10**9, bytes_accessed=MIB, transcendentals=0
        ),
    )(*operands)


def on_device(fields, start_local, start_pair, start_root):
    local_rows, snaps = fields.shape
    rank = start_local.shape[1]
    quarter = local_rows // 4
    chunk = quarter // 6
    scale = 1.0 / (local_rows * lax.axis_size("grid"))
    core_step, far_step = ("snap", 0), ("snap", 1)
    grid_steps = axis_steps("grid")

    rows = jax.ShapeDtypeStruct((quarter, snaps), fields.dtype)
    raw = quarter // 3
    raw_part = jax.ShapeDtypeStruct((raw, snaps), fields.dtype)
    rest_part = jax.ShapeDtypeStruct((quarter - raw, snaps), fields.dtype)
    everything = jax.ShapeDtypeStruct((4, quarter, snaps), fields.dtype)
    placed = pl.pallas_call(
        place_kernel,
        out_shape=(everything,) + (rows,) * 3 + (raw_part, rest_part),
        in_specs=[pl.BlockSpec(memory_space=pltpu.HBM)],
        out_specs=(pl.BlockSpec(memory_space=pltpu.VMEM),) * 6,
        scratch_shapes=[pltpu.SemaphoreType.DMA((9,))],
        name="place",
        compiler_params=pltpu.CompilerParams(vmem_limit_bytes=46 * MIB),
    )(fields.reshape(4, quarter, snaps))
    everything, own_rows, near_sent, corner_sent, raw_sent, rest_sent = placed
    everything = everything.reshape(local_rows, snaps)
    near_rows = exchange(near_sent, core_step)
    far_core_rows = exchange(corner_sent, core_step)
    corner_rows = exchange(far_core_rows, far_step)
    raw_rows = exchange(raw_sent, far_step)

    piece = jax.ShapeDtypeStruct((rank + 8, rank), F32)
    kept, sent = call(
        lambda *refs: pack_kernel(grid_steps[0], *refs),
        (piece, piece), inner_product(everything, everything),
        microseconds=1, limit=2 * MIB,
    )
    kept = kept + exchange(sent, grid_steps[0])
    for step in grid_steps[1:]:
        kept = kept + exchange(kept, step)
    other = exchange(kept, grid_steps[0])

    cross = inner_product(own_rows, near_rows)
    cross = cross + inner_product(raw_sent, far_core_rows[:raw])
    cross = cross + inner_product(rest_sent, far_core_rows[raw:])
    half = jax.ShapeDtypeStruct((rank, snaps), F32)
    slab, slab_sent = call(orient_kernel, (half, half), cross, microseconds=1)
    slab = slab + exchange(slab_sent, core_step)
    slab = sum_over(slab, grid_steps)
    other_slab = exchange(slab, core_step)

    turned = jax.ShapeDtypeStruct((rank, snaps), F32)
    turned_pair = jax.ShapeDtypeStruct((rank, 2 * rank), F32)
    local_basis, pair_basis, root_basis = call(
        turn_kernel, (turned, turned_pair, turned_pair),
        start_local, start_pair, start_root,
        microseconds=1,
    )
    square = jax.ShapeDtypeStruct((rank, rank), F32)
    leaf = call(
        lambda *refs: leaf_kernel(scale, grid_steps[0], *refs),
        jax.ShapeDtypeStruct((2 * rank, snaps), BF16),
        kept, other, local_basis,
    )
    other_leaf = exchange(leaf, core_step)
    rows = jax.ShapeDtypeStruct((quarter, rank), BF16)
    rest = jax.ShapeDtypeStruct((quarter - raw + 2 * rank, rank), BF16)
    far_rows = call(
        lambda *refs: far_leaf_kernel(chunk, *refs), rest, rest_sent, leaf,
        microseconds=1,
    )
    far_rows = exchange(far_rows, far_step)
    far_other = exchange(far_rows[quarter - raw :], core_step)

    rotation, gram = call(
        lambda *refs: pair_kernel(scale, *refs),
        (
            jax.ShapeDtypeStruct((rank, 2 * rank), BF16),
            jax.ShapeDtypeStruct((2 * rank, 2 * rank), F32),
        ),
        leaf, other_leaf, slab, other_slab, pair_basis,
    )
    kept = call(kept_kernel, square, rotation, gram, microseconds=1)
    far_rotation = permute(rotation, [far_step, core_step])
    other = permute(kept, [far_step, core_step])
    lower, upper = call(
        lambda *refs: branch_kernel(chunk, *refs),
        (rows, rows),
        own_rows, near_rows, raw_rows, far_rows, corner_rows, leaf, other_leaf, far_other,
        rotation, far_rotation,
        microseconds=1, limit=16 * MIB,
    )
    steps = [far_step] + grid_steps
    cross = sum_everywhere(inner_product(lower, upper), core_step, steps)
    return call(
        lambda *refs: root_kernel(scale, chunk, *refs),
        rows,
        kept, other, cross, root_basis, lower, upper,
        limit=16 * MIB,
    )


def solution(mesh):
    in_specs = (P("grid", "snap"), P("snap", None), P(), P())
    out_specs = P(("grid", "snap"), None)
    return jax.shard_map(
        on_device, mesh=mesh, in_specs=in_specs, out_specs=out_specs, check_vma=False
    )
```

```python
import itertools

import jax
import jax.numpy as jnp
from jax import lax
from jax.experimental import pallas as pl
from jax.experimental.pallas import tpu as pltpu
from jax.sharding import PartitionSpec as P


POWER = 2
NEWTON = 8
F32 = jnp.float32
BF16 = jnp.bfloat16
MIB = 2**20


def permute(value, steps):
    axes = tuple(axis for axis in ("grid", "snap") if any(axis == on for on, _ in steps))
    places = [0]
    for axis in axes:
        mask = sum(2**bit for on, bit in steps if on == axis)
        size = lax.axis_size(axis)
        places = [place * size + (own ^ mask) for place in places for own in range(size)]
    pairs = list(enumerate(places))
    return lax.ppermute(value, axes, pairs)


def exchange(value, step):
    return permute(value, [step])


def bit_of(step):
    axis, bit = step
    return (lax.axis_index(axis) // 2**bit) % 2


def axis_steps(axis):
    return [(axis, bit) for bit in range(lax.axis_size(axis).bit_length() - 1)]


def sum_over(value, steps):
    for step in steps:
        sent = value.astype(BF16)
        received = exchange(sent, step)
        value = sent.astype(F32) + received.astype(F32)
    return value


def sum_everywhere(value, through, steps):
    value = sum_over(value, [through])
    groups = [steps[:3]] + [[step] for step in steps[3:]]
    for group in groups:
        hops = [
            list(chosen) + [through] * (size % 2)
            for size in range(len(group), 0, -1)
            for chosen in itertools.combinations(group, size)
        ]
        sent = value.astype(BF16)
        received = [permute(sent, hop) for hop in hops]
        value = sum((part.astype(F32) for part in received), sent.astype(F32))
    return value


def split(x):
    high = x.astype(BF16)
    return high, (x - high.astype(F32)).astype(BF16)


def product(a, b, transposed=False):
    return lax.dot_general(
        a, b, (((1,), (1 if transposed else 0,)), ((), ())), preferred_element_type=F32
    )


def inner_product(left, right):
    return lax.dot_general(
        left, right, (((0,), (0,)), ((), ())), preferred_element_type=F32
    )


def subspace_steps(gram, basis, count):
    gram_high, gram_low = split(gram)
    rank = basis.shape[0]
    rows = lax.broadcasted_iota(jnp.int32, (rank, rank), 0)
    columns = lax.broadcasted_iota(jnp.int32, (rank, rank), 1)
    identity = (rows == columns).astype(F32)

    def times_right(x, right):
        out = product(jnp.concatenate(split(x), axis=1), right)
        return out[:, :rank] + out[:, rank:]

    for _ in range(count):
        high, low = split(basis)
        out = product(jnp.concatenate([high, low], axis=0), gram_high)
        image = out[:rank] + out[rank:] + product(high, gram_low)
        size = jnp.sum(image * image) + 1e-06
        image_high, image_low = split(image)
        stacked = jnp.concatenate([image_high, image_low], axis=0)
        out = product(stacked, stacked, transposed=True)
        inner = (out[:rank, :rank] + out[:rank, rank:] + out[rank:, :rank]) * (1.0 / size)
        total = None
        for step in range(NEWTON):
            factor = 1.5 * identity - 0.5 * inner
            row = jnp.concatenate(split(factor), axis=1)
            right = jnp.concatenate([row, row], axis=0)
            if total is None:
                total = factor
                inner = times_right(times_right(inner, right), right)
            elif step < NEWTON - 1:
                both = times_right(jnp.concatenate([inner, total], axis=0), right)
                inner, total = times_right(both[:rank], right), both[rank:]
            else:
                total = times_right(total, right)
        total_high, total_low = split(total * lax.rsqrt(size))
        basis = product(
            jnp.concatenate([total_high, total_low], axis=1),
            jnp.concatenate([image_high, image_high], axis=0),
        ) + product(total_high, image_low)
    return basis


def kept_gram(rotation, gram):
    gram_high, gram_low = split(gram)
    image = product(rotation, gram_high) + product(rotation, gram_low)
    high, low = split(image)
    return product(high, rotation, True) + product(low, rotation, True)


def pack(gram):
    size = gram.shape[0] // 2
    rows = lax.broadcasted_iota(jnp.int32, (size, size), 0)
    columns = lax.broadcasted_iota(jnp.int32, (size, size), 1)
    first, second = gram[:size, :size], gram[size:, size:]
    diagonal = jnp.sum(jnp.where(rows == columns, second, 0.0), axis=0, keepdims=True)
    diagonal = jnp.broadcast_to(diagonal, (8, size))
    low = jnp.concatenate([jnp.where(rows <= columns, first, second), diagonal], axis=0)
    high = jnp.concatenate([gram[:size, size:], diagonal], axis=0)
    return low, high


def unpack(low, high):
    size = low.shape[1]
    rows = lax.broadcasted_iota(jnp.int32, (size, size), 0)
    columns = lax.broadcasted_iota(jnp.int32, (size, size), 1)
    both, cross = low[:size], high[:size]
    flipped = both.T
    first = jnp.where(rows <= columns, both, flipped)
    second = jnp.where(rows > columns, both, flipped)
    diagonal = jnp.broadcast_to(low[size : size + 1], (size, size))
    second = jnp.where(rows == columns, diagonal, second)
    top = jnp.concatenate([first, cross], axis=1)
    return jnp.concatenate([top, jnp.concatenate([cross.T, second], axis=1)], axis=0)


def place_kernel(rows_ref, all_ref, own_ref, near_ref, corner_ref, raw_ref, rest_ref, semaphores):
    core, far = bit_of(("snap", 0)), bit_of(("snap", 1))
    quarters = (
        (2 * far + 1 - core, (near_ref,)),
        (3 - 2 * far - core, (corner_ref,)),
        (2 - 2 * far + core, (raw_ref, rest_ref)),
        (2 * far + core, (own_ref,)),
    )
    copies = [
        pltpu.make_async_copy(rows_ref.at[place], all_ref.at[number], semaphores.at[number])
        for number, (place, _) in enumerate(quarters)
    ]
    for copy in copies:
        copy.start()
    moves = []
    for number, (_, targets) in enumerate(quarters):
        copies[number].wait()
        start = 0
        for target in targets:
            source = all_ref.at[number, pl.ds(start, target.shape[0])]
            moves.append(pltpu.make_async_copy(source, target, semaphores.at[4 + len(moves)]))
            moves[-1].start()
            start += target.shape[0]
    for move in moves:
        move.wait()


def turn_kernel(local_ref, pair_ref, root_ref, *turned_refs):
    far = bit_of(("snap", 1))
    turned_refs[0][...] = local_ref[...].T
    turned_refs[1][...] = pair_ref[far].T
    turned_refs[2][...] = root_ref[...].T


def orient_kernel(cross_ref, kept_ref, sent_ref):
    core = bit_of(("snap", 0)) == 1
    rank = kept_ref.shape[0]
    cross = cross_ref[...]
    turned = cross.T
    kept_ref[...] = jnp.where(core, turned[rank:], cross[:rank])
    sent_ref[...] = jnp.where(core, turned[:rank], cross[rank:])


def pack_kernel(side_step, gram_ref, kept_ref, sent_ref):
    side = bit_of(side_step) == 1
    low, high = pack(gram_ref[...])
    kept_ref[...] = jnp.where(side, high, low)
    sent_ref[...] = jnp.where(side, low, high)


def leaf_kernel(scale, side_step, kept_ref, other_ref, start_ref, out_ref):
    side = bit_of(side_step) == 1
    kept, other = kept_ref[...], other_ref[...]
    low = jnp.where(side, other, kept)
    high = jnp.where(side, kept, other)
    gram = unpack(low, high) * scale
    rank = start_ref.shape[0]
    rotation = subspace_steps(gram, start_ref[...], POWER).astype(BF16)
    out_ref[:rank] = rotation
    out_ref[rank:] = jnp.concatenate(split(kept_gram(rotation, gram)), axis=1)


def far_leaf_kernel(chunk, rows_ref, leaf_ref, out_ref):
    rank = leaf_ref.shape[0] // 2
    rotation = leaf_ref[:rank]
    count = rows_ref.shape[0]
    for start in range(0, count, chunk):
        rows = pl.ds(start, chunk)
        out_ref[rows] = product(rows_ref[rows], rotation, True).astype(BF16)
    out_ref[pl.ds(count, rank)] = rotation[:, :rank]
    out_ref[pl.ds(count + rank, rank)] = rotation[:, rank:]


def pair_kernel(
    scale, own_ref, other_ref, own_slab_ref, other_slab_ref, start_ref, out_ref, gram_ref
):
    core = bit_of(("snap", 0)) == 1
    rank = start_ref.shape[0]
    own, other = own_ref[...].astype(F32), other_ref[...].astype(F32)
    first, second = jnp.where(core, other, own), jnp.where(core, own, other)
    own, other = own_slab_ref[...], other_slab_ref[...]
    cross = jnp.concatenate([jnp.where(core, other, own), jnp.where(core, own, other)], axis=0)
    cross_high, cross_low = split(cross * scale)
    first_rotation, second_rotation = first[:rank].astype(BF16), second[:rank].astype(BF16)
    image = product(first_rotation, cross_high) + product(first_rotation, cross_low)
    high, low = split(image)
    cross = product(high, second_rotation, True) + product(low, second_rotation, True)
    first, second = first[rank:], second[rank:]
    top = jnp.concatenate([first[:, :rank] + first[:, rank:], cross], axis=1)
    bottom = jnp.concatenate([cross.T, second[:, :rank] + second[:, rank:]], axis=1)
    gram = jnp.concatenate([top, bottom], axis=0)
    gram_ref[...] = gram
    out_ref[...] = subspace_steps(gram, start_ref[...], POWER).astype(BF16)


def kept_kernel(rotation_ref, gram_ref, kept_ref):
    kept_ref[...] = kept_gram(rotation_ref[...], gram_ref[...])


def core_halves(ref):
    core = bit_of(("snap", 0)) == 1
    value = ref[...].astype(F32)
    rank = value.shape[0]
    left, right = value[:, :rank], value[:, rank:]
    own, other = jnp.where(core, right, left), jnp.where(core, left, right)
    return own.astype(BF16), other.astype(BF16)


def mine_kernel(chunk, own_ref, near_ref, leaf_ref, other_leaf_ref, rotation_ref, out_ref):
    rank = rotation_ref.shape[0]
    own_part, near_part = core_halves(rotation_ref)
    own = product(own_part, leaf_ref[:rank]).astype(BF16)
    near = product(near_part, other_leaf_ref[:rank]).astype(BF16)
    for start in range(0, own_ref.shape[0], chunk):
        rows = pl.ds(start, chunk)
        total = product(own_ref[rows], own, True) + product(near_ref[rows], near, True)
        out_ref[rows] = total.astype(BF16)


def branch_kernel(
    chunk, mine_ref, raw_ref, far_ref, corner_ref, far_other_ref, far_rotation_ref,
    lower_ref, upper_ref,
):
    high_bit = bit_of(("snap", 1)) == 1
    rank = far_rotation_ref.shape[0]
    far_part, corner_part = core_halves(far_rotation_ref)
    raw, below = raw_ref.shape[0], mine_ref.shape[0] - raw_ref.shape[0]

    def turned(part, ref, place):
        pieces = [ref[pl.ds(place + offset, rank)] for offset in (0, rank)]
        return product(part, jnp.concatenate(pieces, axis=1)).astype(BF16)

    far = turned(far_part, far_ref, below)
    corner = turned(corner_part, far_other_ref, 0)
    for start in range(0, mine_ref.shape[0], chunk):
        rows = pl.ds(start, chunk)
        if start < raw:
            theirs = product(raw_ref[rows], far, True)
        else:
            theirs = product(far_ref[pl.ds(start - raw, chunk)], far_part, True)
        theirs = theirs + product(corner_ref[rows], corner, True)
        mine = mine_ref[rows].astype(F32)
        lower_ref[rows] = jnp.where(high_bit, theirs, mine).astype(BF16)
        upper_ref[rows] = jnp.where(high_bit, mine, theirs).astype(BF16)


def root_kernel(
    scale, chunk, kept_ref, other_ref, cross_ref, start_ref, lower_ref, upper_ref, out_ref
):
    high_bit = bit_of(("snap", 1)) == 1
    kept, other = kept_ref[...], other_ref[...]
    cross = cross_ref[...] * scale
    top = jnp.concatenate([jnp.where(high_bit, other, kept), cross], axis=1)
    bottom = jnp.concatenate([cross.T, jnp.where(high_bit, kept, other)], axis=1)
    gram = jnp.concatenate([top, bottom], axis=0)
    rotation = subspace_steps(gram, start_ref[...], POWER).astype(BF16)
    for start in range(0, lower_ref.shape[0], chunk):
        rows = pl.ds(start, chunk)
        root = jnp.concatenate([lower_ref[rows], upper_ref[rows]], axis=1)
        out_ref[rows] = product(root, rotation, True).astype(BF16)


def call(kernel, out_shape, *operands, microseconds=8, limit=8 * MIB):
    vmem = pl.BlockSpec(memory_space=pltpu.VMEM)
    return pl.pallas_call(
        kernel,
        out_shape=out_shape,
        in_specs=[vmem] * len(operands),
        out_specs=jax.tree.map(lambda _: vmem, out_shape),
        compiler_params=pltpu.CompilerParams(vmem_limit_bytes=limit),
        cost_estimate=pl.CostEstimate(
            flops=microseconds * 10**9, bytes_accessed=MIB, transcendentals=0
        ),
    )(*operands)


def on_device(fields, start_local, start_pair, start_root):
    local_rows, snaps = fields.shape
    rank = start_local.shape[1]
    quarter = local_rows // 4
    chunk = quarter // 6
    scale = 1.0 / (local_rows * lax.axis_size("grid"))
    core_step, far_step = ("snap", 0), ("snap", 1)
    grid_steps = axis_steps("grid")

    rows = jax.ShapeDtypeStruct((quarter, snaps), fields.dtype)
    raw = quarter // 2
    raw_part = jax.ShapeDtypeStruct((raw, snaps), fields.dtype)
    rest_part = jax.ShapeDtypeStruct((quarter - raw, snaps), fields.dtype)
    everything = jax.ShapeDtypeStruct((4, quarter, snaps), fields.dtype)
    placed = pl.pallas_call(
        place_kernel,
        out_shape=(everything,) + (rows,) * 3 + (raw_part, rest_part),
        in_specs=[pl.BlockSpec(memory_space=pltpu.HBM)],
        out_specs=(pl.BlockSpec(memory_space=pltpu.VMEM),) * 6,
        scratch_shapes=[pltpu.SemaphoreType.DMA((9,))],
        name="place",
        compiler_params=pltpu.CompilerParams(vmem_limit_bytes=46 * MIB),
    )(fields.reshape(4, quarter, snaps))
    everything, own_rows, near_sent, corner_sent, raw_sent, rest_sent = placed
    everything = everything.reshape(local_rows, snaps)
    near_rows = exchange(near_sent, core_step)
    far_core_rows = exchange(corner_sent, core_step)
    corner_rows = exchange(far_core_rows, far_step)
    raw_rows = exchange(raw_sent, far_step)

    piece = jax.ShapeDtypeStruct((rank + 8, rank), F32)
    kept, sent = call(
        lambda *refs: pack_kernel(grid_steps[0], *refs),
        (piece, piece), inner_product(everything, everything),
        microseconds=1, limit=2 * MIB,
    )
    kept = kept + exchange(sent, grid_steps[0])
    for step in grid_steps[1:]:
        kept = kept + exchange(kept, step)
    other = exchange(kept, grid_steps[0])

    cross = inner_product(own_rows, near_rows)
    cross = cross + inner_product(raw_sent, far_core_rows[:raw])
    cross = cross + inner_product(rest_sent, far_core_rows[raw:])
    half = jax.ShapeDtypeStruct((rank, snaps), F32)
    slab, slab_sent = call(orient_kernel, (half, half), cross, microseconds=1)
    slab = slab + exchange(slab_sent, core_step)
    slab = sum_over(slab, grid_steps)
    other_slab = exchange(slab, core_step)

    turned = jax.ShapeDtypeStruct((rank, snaps), F32)
    turned_pair = jax.ShapeDtypeStruct((rank, 2 * rank), F32)
    local_basis, pair_basis, root_basis = call(
        turn_kernel, (turned, turned_pair, turned_pair),
        start_local, start_pair, start_root,
        microseconds=1,
    )
    square = jax.ShapeDtypeStruct((rank, rank), F32)
    leaf = call(
        lambda *refs: leaf_kernel(scale, grid_steps[0], *refs),
        jax.ShapeDtypeStruct((2 * rank, snaps), BF16),
        kept, other, local_basis,
    )
    other_leaf = exchange(leaf, core_step)
    rows = jax.ShapeDtypeStruct((quarter, rank), BF16)
    rest = jax.ShapeDtypeStruct((quarter - raw + 2 * rank, rank), BF16)
    far_rows = call(
        lambda *refs: far_leaf_kernel(chunk, *refs), rest, rest_sent, leaf,
        microseconds=1,
    )
    far_rows = exchange(far_rows, far_step)
    far_other = exchange(far_rows[quarter - raw :], core_step)

    rotation, gram = call(
        lambda *refs: pair_kernel(scale, *refs),
        (
            jax.ShapeDtypeStruct((rank, 2 * rank), BF16),
            jax.ShapeDtypeStruct((2 * rank, 2 * rank), F32),
        ),
        leaf, other_leaf, slab, other_slab, pair_basis,
    )
    kept = call(kept_kernel, square, rotation, gram, microseconds=1)
    far_rotation = permute(rotation, [far_step, core_step])
    other = permute(kept, [far_step, core_step])
    mine = call(
        lambda *refs: mine_kernel(chunk, *refs), rows,
        own_rows, near_rows, leaf, other_leaf, rotation,
        microseconds=1,
    )
    lower, upper = call(
        lambda *refs: branch_kernel(chunk, *refs), (rows, rows),
        mine, raw_rows, far_rows, corner_rows, far_other, far_rotation,
        microseconds=1, limit=16 * MIB,
    )
    steps = [far_step] + grid_steps
    cross = sum_everywhere(inner_product(lower, upper), core_step, steps)
    return call(
        lambda *refs: root_kernel(scale, chunk, *refs),
        rows,
        kept, other, cross, root_basis, lower, upper,
        limit=16 * MIB,
    )


def solution(mesh):
    in_specs = (P("grid", "snap"), P("snap", None), P(), P())
    out_specs = P(("grid", "snap"), None)
    return jax.shard_map(
        on_device, mesh=mesh, in_specs=in_specs, out_specs=out_specs, check_vma=False
    )
```

```python
import jax
import jax.numpy as jnp
from jax import lax
from jax.experimental import pallas as pl
from jax.experimental.pallas import tpu as pltpu
from jax.sharding import PartitionSpec as P


POWER = 2
NEWTON = 8
F32 = jnp.float32
BF16 = jnp.bfloat16
MIB = 2**20


def permute(value, steps):
    axes = tuple(axis for axis in ("grid", "snap") if any(axis == on for on, _ in steps))
    places = [0]
    for axis in axes:
        mask = sum(2**bit for on, bit in steps if on == axis)
        size = lax.axis_size(axis)
        places = [place * size + (own ^ mask) for place in places for own in range(size)]
    pairs = list(enumerate(places))
    return lax.ppermute(value, axes, pairs)


def exchange(value, step):
    return permute(value, [step])


def bit_of(step):
    axis, bit = step
    return (lax.axis_index(axis) // 2**bit) % 2


def axis_steps(axis):
    return [(axis, bit) for bit in range(lax.axis_size(axis).bit_length() - 1)]


def sum_over(value, steps):
    for step in steps:
        sent = value.astype(BF16)
        received = exchange(sent, step)
        value = sent.astype(F32) + received.astype(F32)
    return value


def sum_everywhere(value, through, steps):
    value = sum_over(value, [through])
    groups = [steps[:2]] + [[step] for step in steps[2:]]
    for group in groups:
        hops = [[step, through] for step in group]
        if len(group) == 2:
            hops.append(group)
        sent = value.astype(BF16)
        received = [permute(sent, hop) for hop in hops]
        value = sum((part.astype(F32) for part in received), sent.astype(F32))
    return value


def split(x):
    high = x.astype(BF16)
    return high, (x - high.astype(F32)).astype(BF16)


def product(a, b, transposed=False):
    return lax.dot_general(
        a, b, (((1,), (1 if transposed else 0,)), ((), ())), preferred_element_type=F32
    )


def inner_product(left, right):
    return lax.dot_general(
        left, right, (((0,), (0,)), ((), ())), preferred_element_type=F32
    )


def subspace_steps(gram, basis, count):
    gram_high, gram_low = split(gram)
    rank = basis.shape[0]
    rows = lax.broadcasted_iota(jnp.int32, (rank, rank), 0)
    columns = lax.broadcasted_iota(jnp.int32, (rank, rank), 1)
    identity = (rows == columns).astype(F32)

    def times_right(x, right):
        out = product(jnp.concatenate(split(x), axis=1), right)
        return out[:, :rank] + out[:, rank:]

    for _ in range(count):
        high, low = split(basis)
        out = product(jnp.concatenate([high, low], axis=0), gram_high)
        image = out[:rank] + out[rank:] + product(high, gram_low)
        size = jnp.sum(image * image) + 1e-06
        image_high, image_low = split(image)
        stacked = jnp.concatenate([image_high, image_low], axis=0)
        out = product(stacked, stacked, transposed=True)
        inner = (out[:rank, :rank] + out[:rank, rank:] + out[rank:, :rank]) * (1.0 / size)
        total = None
        for step in range(NEWTON):
            factor = 1.5 * identity - 0.5 * inner
            row = jnp.concatenate(split(factor), axis=1)
            right = jnp.concatenate([row, row], axis=0)
            if total is None:
                total = factor
                inner = times_right(times_right(inner, right), right)
            elif step < NEWTON - 1:
                both = times_right(jnp.concatenate([inner, total], axis=0), right)
                inner, total = times_right(both[:rank], right), both[rank:]
            else:
                total = times_right(total, right)
        total_high, total_low = split(total * lax.rsqrt(size))
        basis = product(
            jnp.concatenate([total_high, total_low], axis=1),
            jnp.concatenate([image_high, image_high], axis=0),
        ) + product(total_high, image_low)
    return basis


def kept_gram(rotation, gram):
    gram_high, gram_low = split(gram)
    image = product(rotation, gram_high) + product(rotation, gram_low)
    high, low = split(image)
    return product(high, rotation, True) + product(low, rotation, True)


def pack(gram):
    size = gram.shape[0] // 2
    rows = lax.broadcasted_iota(jnp.int32, (size, size), 0)
    columns = lax.broadcasted_iota(jnp.int32, (size, size), 1)
    first, second = gram[:size, :size], gram[size:, size:]
    diagonal = jnp.sum(jnp.where(rows == columns, second, 0.0), axis=0, keepdims=True)
    diagonal = jnp.broadcast_to(diagonal, (8, size))
    low = jnp.concatenate([jnp.where(rows <= columns, first, second), diagonal], axis=0)
    high = jnp.concatenate([gram[:size, size:], diagonal], axis=0)
    return low, high


def unpack(low, high):
    size = low.shape[1]
    rows = lax.broadcasted_iota(jnp.int32, (size, size), 0)
    columns = lax.broadcasted_iota(jnp.int32, (size, size), 1)
    both, cross = low[:size], high[:size]
    flipped = both.T
    first = jnp.where(rows <= columns, both, flipped)
    second = jnp.where(rows > columns, both, flipped)
    diagonal = jnp.broadcast_to(low[size : size + 1], (size, size))
    second = jnp.where(rows == columns, diagonal, second)
    top = jnp.concatenate([first, cross], axis=1)
    return jnp.concatenate([top, jnp.concatenate([cross.T, second], axis=1)], axis=0)


def place_kernel(rows_ref, all_ref, own_ref, near_ref, corner_ref, raw_ref, rest_ref, semaphores):
    core, far = bit_of(("snap", 0)), bit_of(("snap", 1))
    quarters = (
        (2 * far + 1 - core, (near_ref,)),
        (3 - 2 * far - core, (corner_ref,)),
        (2 - 2 * far + core, (raw_ref, rest_ref)),
        (2 * far + core, (own_ref,)),
    )
    copies = [
        pltpu.make_async_copy(rows_ref.at[place], all_ref.at[number], semaphores.at[number])
        for number, (place, _) in enumerate(quarters)
    ]
    for copy in copies:
        copy.start()
    moves = []
    for number, (_, targets) in enumerate(quarters):
        copies[number].wait()
        start = 0
        for target in targets:
            source = all_ref.at[number, pl.ds(start, target.shape[0])]
            moves.append(pltpu.make_async_copy(source, target, semaphores.at[4 + len(moves)]))
            moves[-1].start()
            start += target.shape[0]
    for move in moves:
        move.wait()


def turn_kernel(local_ref, pair_ref, root_ref, *turned_refs):
    far = bit_of(("snap", 1))
    turned_refs[0][...] = local_ref[...].T
    turned_refs[1][...] = pair_ref[far].T
    turned_refs[2][...] = root_ref[...].T


def orient_kernel(cross_ref, kept_ref, sent_ref):
    core = bit_of(("snap", 0)) == 1
    rank = kept_ref.shape[0]
    cross = cross_ref[...]
    turned = cross.T
    kept_ref[...] = jnp.where(core, turned[rank:], cross[:rank])
    sent_ref[...] = jnp.where(core, turned[:rank], cross[rank:])


def pack_kernel(side_step, gram_ref, kept_ref, sent_ref):
    side = bit_of(side_step) == 1
    low, high = pack(gram_ref[...])
    kept_ref[...] = jnp.where(side, high, low)
    sent_ref[...] = jnp.where(side, low, high)


def leaf_kernel(scale, side_step, kept_ref, other_ref, start_ref, out_ref):
    side = bit_of(side_step) == 1
    kept, other = kept_ref[...], other_ref[...]
    low = jnp.where(side, other, kept)
    high = jnp.where(side, kept, other)
    gram = unpack(low, high) * scale
    rank = start_ref.shape[0]
    rotation = subspace_steps(gram, start_ref[...], POWER).astype(BF16)
    out_ref[:rank] = rotation
    out_ref[rank:] = jnp.concatenate(split(kept_gram(rotation, gram)), axis=1)


def far_leaf_kernel(chunk, rows_ref, leaf_ref, out_ref):
    rank = leaf_ref.shape[0] // 2
    rotation = leaf_ref[:rank]
    count = rows_ref.shape[0]
    for start in range(0, count, chunk):
        rows = pl.ds(start, chunk)
        out_ref[rows] = product(rows_ref[rows], rotation, True).astype(BF16)
    out_ref[pl.ds(count, rank)] = rotation[:, :rank]
    out_ref[pl.ds(count + rank, rank)] = rotation[:, rank:]


def pair_kernel(
    scale, own_ref, other_ref, own_slab_ref, other_slab_ref, start_ref, out_ref, gram_ref
):
    core = bit_of(("snap", 0)) == 1
    rank = start_ref.shape[0]
    own, other = own_ref[...].astype(F32), other_ref[...].astype(F32)
    first, second = jnp.where(core, other, own), jnp.where(core, own, other)
    own, other = own_slab_ref[...], other_slab_ref[...]
    cross = jnp.concatenate([jnp.where(core, other, own), jnp.where(core, own, other)], axis=0)
    cross_high, cross_low = split(cross * scale)
    first_rotation, second_rotation = first[:rank].astype(BF16), second[:rank].astype(BF16)
    image = product(first_rotation, cross_high) + product(first_rotation, cross_low)
    high, low = split(image)
    cross = product(high, second_rotation, True) + product(low, second_rotation, True)
    first, second = first[rank:], second[rank:]
    top = jnp.concatenate([first[:, :rank] + first[:, rank:], cross], axis=1)
    bottom = jnp.concatenate([cross.T, second[:, :rank] + second[:, rank:]], axis=1)
    gram = jnp.concatenate([top, bottom], axis=0)
    gram_ref[...] = gram
    out_ref[...] = subspace_steps(gram, start_ref[...], POWER).astype(BF16)


def kept_kernel(rotation_ref, gram_ref, kept_ref):
    kept_ref[...] = kept_gram(rotation_ref[...], gram_ref[...])


def core_halves(ref):
    core = bit_of(("snap", 0)) == 1
    value = ref[...].astype(F32)
    rank = value.shape[0]
    left, right = value[:, :rank], value[:, rank:]
    own, other = jnp.where(core, right, left), jnp.where(core, left, right)
    return own.astype(BF16), other.astype(BF16)


def mine_kernel(chunk, own_ref, near_ref, leaf_ref, other_leaf_ref, rotation_ref, out_ref):
    rank = rotation_ref.shape[0]
    own_part, near_part = core_halves(rotation_ref)
    own = product(own_part, leaf_ref[:rank]).astype(BF16)
    near = product(near_part, other_leaf_ref[:rank]).astype(BF16)
    for start in range(0, own_ref.shape[0], chunk):
        rows = pl.ds(start, chunk)
        total = product(own_ref[rows], own, True) + product(near_ref[rows], near, True)
        out_ref[rows] = total.astype(BF16)


def branch_kernel(
    chunk, mine_ref, raw_ref, far_ref, corner_ref, far_other_ref, far_rotation_ref,
    lower_ref, upper_ref,
):
    high_bit = bit_of(("snap", 1)) == 1
    rank = far_rotation_ref.shape[0]
    far_part, corner_part = core_halves(far_rotation_ref)
    raw, below = raw_ref.shape[0], mine_ref.shape[0] - raw_ref.shape[0]

    def turned(part, ref, place):
        pieces = [ref[pl.ds(place + offset, rank)] for offset in (0, rank)]
        return product(part, jnp.concatenate(pieces, axis=1)).astype(BF16)

    far = turned(far_part, far_ref, below)
    corner = turned(corner_part, far_other_ref, 0)
    for start in range(0, mine_ref.shape[0], chunk):
        rows = pl.ds(start, chunk)
        if start < raw:
            theirs = product(raw_ref[rows], far, True)
        else:
            theirs = product(far_ref[pl.ds(start - raw, chunk)], far_part, True)
        theirs = theirs + product(corner_ref[rows], corner, True)
        mine = mine_ref[rows].astype(F32)
        lower_ref[rows] = jnp.where(high_bit, theirs, mine).astype(BF16)
        upper_ref[rows] = jnp.where(high_bit, mine, theirs).astype(BF16)


def root_kernel(
    scale, chunk, kept_ref, other_ref, cross_ref, start_ref, lower_ref, upper_ref, out_ref,
    rows_ref, semaphores,
):
    high_bit = bit_of(("snap", 1)) == 1
    kept, other = kept_ref[...], other_ref[...]
    cross = cross_ref[...] * scale
    top = jnp.concatenate([jnp.where(high_bit, other, kept), cross], axis=1)
    bottom = jnp.concatenate([cross.T, jnp.where(high_bit, kept, other)], axis=1)
    gram = jnp.concatenate([top, bottom], axis=0)
    rotation = subspace_steps(gram, start_ref[...], POWER).astype(BF16)
    copies = []
    for start in range(0, lower_ref.shape[0], chunk):
        rows = pl.ds(start, chunk)
        root = jnp.concatenate([lower_ref[rows], upper_ref[rows]], axis=1)
        rows_ref[rows] = product(root, rotation, True).astype(BF16)
        copies.append(
            pltpu.make_async_copy(
                rows_ref.at[rows], out_ref.at[rows], semaphores.at[len(copies)]
            )
        )
        copies[-1].start()
    for copy in copies:
        copy.wait()


def call(kernel, out_shape, *operands, microseconds=8, limit=8 * MIB, scratch=(), out=pltpu.VMEM):
    vmem = pl.BlockSpec(memory_space=pltpu.VMEM)
    return pl.pallas_call(
        kernel,
        out_shape=out_shape,
        in_specs=[vmem] * len(operands),
        out_specs=jax.tree.map(lambda _: pl.BlockSpec(memory_space=out), out_shape),
        scratch_shapes=scratch,
        compiler_params=pltpu.CompilerParams(vmem_limit_bytes=limit),
        cost_estimate=pl.CostEstimate(
            flops=microseconds * 10**9, bytes_accessed=MIB, transcendentals=0
        ),
    )(*operands)


def on_device(fields, start_local, start_pair, start_root):
    local_rows, snaps = fields.shape
    rank = start_local.shape[1]
    quarter = local_rows // 4
    chunk = quarter // 6
    scale = 1.0 / (local_rows * lax.axis_size("grid"))
    core_step, far_step = ("snap", 0), ("snap", 1)
    grid_steps = axis_steps("grid")

    rows = jax.ShapeDtypeStruct((quarter, snaps), fields.dtype)
    raw = quarter // 2
    raw_part = jax.ShapeDtypeStruct((raw, snaps), fields.dtype)
    rest_part = jax.ShapeDtypeStruct((quarter - raw, snaps), fields.dtype)
    everything = jax.ShapeDtypeStruct((4, quarter, snaps), fields.dtype)
    placed = pl.pallas_call(
        place_kernel,
        out_shape=(everything,) + (rows,) * 3 + (raw_part, rest_part),
        in_specs=[pl.BlockSpec(memory_space=pltpu.HBM)],
        out_specs=(pl.BlockSpec(memory_space=pltpu.VMEM),) * 6,
        scratch_shapes=[pltpu.SemaphoreType.DMA((9,))],
        name="place",
        compiler_params=pltpu.CompilerParams(vmem_limit_bytes=46 * MIB),
    )(fields.reshape(4, quarter, snaps))
    everything, own_rows, near_sent, corner_sent, raw_sent, rest_sent = placed
    everything = everything.reshape(local_rows, snaps)
    near_rows = exchange(near_sent, core_step)
    far_core_rows = exchange(corner_sent, core_step)
    corner_rows = exchange(far_core_rows, far_step)
    raw_rows = exchange(raw_sent, far_step)

    piece = jax.ShapeDtypeStruct((rank + 8, rank), F32)
    kept, sent = call(
        lambda *refs: pack_kernel(grid_steps[0], *refs),
        (piece, piece), inner_product(everything, everything),
        microseconds=1, limit=2 * MIB,
    )
    kept = kept + exchange(sent, grid_steps[0])
    for step in grid_steps[1:]:
        kept = kept + exchange(kept, step)
    other = exchange(kept, grid_steps[0])

    cross = inner_product(own_rows, near_rows)
    cross = cross + inner_product(raw_sent, far_core_rows[:raw])
    cross = cross + inner_product(rest_sent, far_core_rows[raw:])
    half = jax.ShapeDtypeStruct((rank, snaps), F32)
    slab, slab_sent = call(orient_kernel, (half, half), cross, microseconds=1)
    slab = slab + exchange(slab_sent, core_step)
    slab = sum_over(slab, grid_steps)
    other_slab = exchange(slab, core_step)

    turned = jax.ShapeDtypeStruct((rank, snaps), F32)
    turned_pair = jax.ShapeDtypeStruct((rank, 2 * rank), F32)
    local_basis, pair_basis, root_basis = call(
        turn_kernel, (turned, turned_pair, turned_pair),
        start_local, start_pair, start_root,
        microseconds=1,
    )
    square = jax.ShapeDtypeStruct((rank, rank), F32)
    leaf = call(
        lambda *refs: leaf_kernel(scale, grid_steps[0], *refs),
        jax.ShapeDtypeStruct((2 * rank, snaps), BF16),
        kept, other, local_basis,
    )
    other_leaf = exchange(leaf, core_step)
    rows = jax.ShapeDtypeStruct((quarter, rank), BF16)
    rest = jax.ShapeDtypeStruct((quarter - raw + 2 * rank, rank), BF16)
    far_rows = call(
        lambda *refs: far_leaf_kernel(chunk, *refs), rest, rest_sent, leaf,
        microseconds=1,
    )
    far_rows = exchange(far_rows, far_step)
    far_other = exchange(far_rows[quarter - raw :], core_step)

    rotation, gram = call(
        lambda *refs: pair_kernel(scale, *refs),
        (
            jax.ShapeDtypeStruct((rank, 2 * rank), BF16),
            jax.ShapeDtypeStruct((2 * rank, 2 * rank), F32),
        ),
        leaf, other_leaf, slab, other_slab, pair_basis,
    )
    kept = call(kept_kernel, square, rotation, gram, microseconds=1)
    far_rotation = permute(rotation, [far_step, core_step])
    other = permute(kept, [far_step, core_step])
    mine = call(
        lambda *refs: mine_kernel(chunk, *refs), rows,
        own_rows, near_rows, leaf, other_leaf, rotation,
        microseconds=1,
    )
    lower, upper = call(
        lambda *refs: branch_kernel(chunk, *refs), (rows, rows),
        mine, raw_rows, far_rows, corner_rows, far_other, far_rotation,
        microseconds=1, limit=16 * MIB,
    )
    steps = [far_step] + grid_steps
    cross = sum_everywhere(inner_product(lower, upper), core_step, steps)
    return call(
        lambda *refs: root_kernel(scale, chunk, *refs),
        rows,
        kept, other, cross, root_basis, lower, upper,
        limit=16 * MIB, out=pltpu.HBM,
        scratch=[pltpu.VMEM(rows.shape, BF16), pltpu.SemaphoreType.DMA((quarter // chunk,))],
    )


def solution(mesh):
    in_specs = (P("grid", "snap"), P("snap", None), P(), P())
    out_specs = P(("grid", "snap"), None)
    return jax.shard_map(
        on_device, mesh=mesh, in_specs=in_specs, out_specs=out_specs, check_vma=False
    )
```

```python
import jax
import jax.numpy as jnp
from jax import lax
from jax.experimental import pallas as pl
from jax.experimental.pallas import tpu as pltpu
from jax.sharding import PartitionSpec as P


POWER = 2
NEWTON = 8
F32 = jnp.float32
BF16 = jnp.bfloat16
MIB = 2**20


def permute(value, steps):
    axes = tuple(axis for axis in ("grid", "snap") if any(axis == on for on, _ in steps))
    places = [0]
    for axis in axes:
        mask = sum(2**bit for on, bit in steps if on == axis)
        size = lax.axis_size(axis)
        places = [place * size + (own ^ mask) for place in places for own in range(size)]
    pairs = list(enumerate(places))
    return lax.ppermute(value, axes, pairs)


def exchange(value, step):
    return permute(value, [step])


def bit_of(step):
    axis, bit = step
    return (lax.axis_index(axis) // 2**bit) % 2


def axis_steps(axis):
    return [(axis, bit) for bit in range(lax.axis_size(axis).bit_length() - 1)]


def sum_over(value, steps):
    for step in steps:
        sent = value.astype(BF16)
        received = exchange(sent, step)
        value = sent.astype(F32) + received.astype(F32)
    return value


def sum_everywhere(value, through, steps):
    value = sum_over(value, [through])
    groups = [steps[:2]] + [[step] for step in steps[2:]]
    for group in groups:
        hops = [[step, through] for step in group]
        if len(group) == 2:
            hops.append(group)
        sent = value.astype(BF16)
        received = [permute(sent, hop) for hop in hops]
        value = sum((part.astype(F32) for part in received), sent.astype(F32))
    return value


def split(x):
    high = x.astype(BF16)
    return high, (x - high.astype(F32)).astype(BF16)


def product(a, b, transposed=False):
    return lax.dot_general(
        a, b, (((1,), (1 if transposed else 0,)), ((), ())), preferred_element_type=F32
    )


def inner_product(left, right):
    return lax.dot_general(
        left, right, (((0,), (0,)), ((), ())), preferred_element_type=F32
    )


def subspace_steps(gram, basis, count):
    gram_high, gram_low = split(gram)
    rank = basis.shape[0]
    rows = lax.broadcasted_iota(jnp.int32, (rank, rank), 0)
    columns = lax.broadcasted_iota(jnp.int32, (rank, rank), 1)
    identity = (rows == columns).astype(F32)

    def times_right(x, right):
        out = product(jnp.concatenate(split(x), axis=1), right)
        return out[:, :rank] + out[:, rank:]

    for _ in range(count):
        high, low = split(basis)
        out = product(jnp.concatenate([high, low], axis=0), gram_high)
        image = out[:rank] + out[rank:] + product(high, gram_low)
        size = jnp.sum(image * image) + 1e-06
        image_high, image_low = split(image)
        stacked = jnp.concatenate([image_high, image_low], axis=0)
        out = product(stacked, stacked, transposed=True)
        inner = (out[:rank, :rank] + out[:rank, rank:] + out[rank:, :rank]) * (1.0 / size)
        total = None
        for step in range(NEWTON):
            factor = 1.5 * identity - 0.5 * inner
            row = jnp.concatenate(split(factor), axis=1)
            right = jnp.concatenate([row, row], axis=0)
            if total is None:
                total = factor
                inner = times_right(times_right(inner, right), right)
            elif step < NEWTON - 1:
                both = times_right(jnp.concatenate([inner, total], axis=0), right)
                inner, total = times_right(both[:rank], right), both[rank:]
            else:
                total = times_right(total, right)
        total_high, total_low = split(total * lax.rsqrt(size))
        basis = product(
            jnp.concatenate([total_high, total_low], axis=1),
            jnp.concatenate([image_high, image_high], axis=0),
        ) + product(total_high, image_low)
    return basis


def kept_gram(rotation, gram):
    gram_high, gram_low = split(gram)
    image = product(rotation, gram_high) + product(rotation, gram_low)
    high, low = split(image)
    return product(high, rotation, True) + product(low, rotation, True)


def pack(gram):
    size = gram.shape[0] // 2
    rows = lax.broadcasted_iota(jnp.int32, (size, size), 0)
    columns = lax.broadcasted_iota(jnp.int32, (size, size), 1)
    first, second = gram[:size, :size], gram[size:, size:]
    diagonal = jnp.sum(jnp.where(rows == columns, second, 0.0), axis=0, keepdims=True)
    diagonal = jnp.broadcast_to(diagonal, (8, size))
    low = jnp.concatenate([jnp.where(rows <= columns, first, second), diagonal], axis=0)
    high = jnp.concatenate([gram[:size, size:], diagonal], axis=0)
    return low, high


def unpack(low, high):
    size = low.shape[1]
    rows = lax.broadcasted_iota(jnp.int32, (size, size), 0)
    columns = lax.broadcasted_iota(jnp.int32, (size, size), 1)
    both, cross = low[:size], high[:size]
    flipped = both.T
    first = jnp.where(rows <= columns, both, flipped)
    second = jnp.where(rows > columns, both, flipped)
    diagonal = jnp.broadcast_to(low[size : size + 1], (size, size))
    second = jnp.where(rows == columns, diagonal, second)
    top = jnp.concatenate([first, cross], axis=1)
    return jnp.concatenate([top, jnp.concatenate([cross.T, second], axis=1)], axis=0)


def place_kernel(rows_ref, all_ref, own_ref, near_ref, corner_ref, raw_ref, rest_ref, semaphores):
    core, far = bit_of(("snap", 0)), bit_of(("snap", 1))
    quarters = (
        (2 * far + 1 - core, (near_ref,)),
        (3 - 2 * far - core, (corner_ref,)),
        (2 - 2 * far + core, (raw_ref, rest_ref)),
        (2 * far + core, (own_ref,)),
    )
    copies = [
        pltpu.make_async_copy(rows_ref.at[place], all_ref.at[number], semaphores.at[number])
        for number, (place, _) in enumerate(quarters)
    ]
    for copy in copies:
        copy.start()
    moves = []
    for number, (_, targets) in enumerate(quarters):
        copies[number].wait()
        start = 0
        for target in targets:
            source = all_ref.at[number, pl.ds(start, target.shape[0])]
            moves.append(pltpu.make_async_copy(source, target, semaphores.at[4 + len(moves)]))
            moves[-1].start()
            start += target.shape[0]
    for move in moves:
        move.wait()


def turn_kernel(local_ref, pair_ref, root_ref, *turned_refs):
    far = bit_of(("snap", 1))
    turned_refs[0][...] = local_ref[...].T
    turned_refs[1][...] = pair_ref[far].T
    turned_refs[2][...] = root_ref[...].T


def orient_kernel(cross_ref, kept_ref, sent_ref):
    core = bit_of(("snap", 0)) == 1
    rank = kept_ref.shape[0]
    cross = cross_ref[...]
    turned = cross.T
    kept_ref[...] = jnp.where(core, turned[rank:], cross[:rank])
    sent_ref[...] = jnp.where(core, turned[:rank], cross[rank:])


def pack_kernel(side_step, gram_ref, kept_ref, sent_ref):
    side = bit_of(side_step) == 1
    low, high = pack(gram_ref[...])
    kept_ref[...] = jnp.where(side, high, low)
    sent_ref[...] = jnp.where(side, low, high)


def leaf_kernel(scale, side_step, kept_ref, other_ref, start_ref, out_ref):
    side = bit_of(side_step) == 1
    kept, other = kept_ref[...], other_ref[...]
    low = jnp.where(side, other, kept)
    high = jnp.where(side, kept, other)
    gram = unpack(low, high) * scale
    rank = start_ref.shape[0]
    rotation = subspace_steps(gram, start_ref[...], POWER).astype(BF16)
    out_ref[:rank] = rotation
    out_ref[rank:] = jnp.concatenate(split(kept_gram(rotation, gram)), axis=1)


def far_leaf_kernel(chunk, rows_ref, leaf_ref, out_ref):
    rank = leaf_ref.shape[0] // 2
    rotation = leaf_ref[:rank]
    count = rows_ref.shape[0]
    for start in range(0, count, chunk):
        rows = pl.ds(start, chunk)
        out_ref[rows] = product(rows_ref[rows], rotation, True).astype(BF16)
    out_ref[pl.ds(count, rank)] = rotation[:, :rank]
    out_ref[pl.ds(count + rank, rank)] = rotation[:, rank:]


def pair_kernel(
    scale, own_ref, other_ref, own_slab_ref, other_slab_ref, start_ref, out_ref, gram_ref
):
    core = bit_of(("snap", 0)) == 1
    rank = start_ref.shape[0]
    own, other = own_ref[...].astype(F32), other_ref[...].astype(F32)
    first, second = jnp.where(core, other, own), jnp.where(core, own, other)
    own, other = own_slab_ref[...], other_slab_ref[...]
    cross = jnp.concatenate([jnp.where(core, other, own), jnp.where(core, own, other)], axis=0)
    cross_high, cross_low = split(cross * scale)
    first_rotation, second_rotation = first[:rank].astype(BF16), second[:rank].astype(BF16)
    image = product(first_rotation, cross_high) + product(first_rotation, cross_low)
    high, low = split(image)
    cross = product(high, second_rotation, True) + product(low, second_rotation, True)
    first, second = first[rank:], second[rank:]
    top = jnp.concatenate([first[:, :rank] + first[:, rank:], cross], axis=1)
    bottom = jnp.concatenate([cross.T, second[:, :rank] + second[:, rank:]], axis=1)
    gram = jnp.concatenate([top, bottom], axis=0)
    gram_ref[...] = gram
    out_ref[...] = subspace_steps(gram, start_ref[...], POWER).astype(BF16)


def kept_kernel(rotation_ref, gram_ref, kept_ref):
    kept_ref[...] = kept_gram(rotation_ref[...], gram_ref[...])


def core_halves(ref):
    core = bit_of(("snap", 0)) == 1
    value = ref[...].astype(F32)
    rank = value.shape[0]
    left, right = value[:, :rank], value[:, rank:]
    own, other = jnp.where(core, right, left), jnp.where(core, left, right)
    return own.astype(BF16), other.astype(BF16)


def mine_kernel(chunk, own_ref, near_ref, leaf_ref, other_leaf_ref, rotation_ref, out_ref):
    rank = rotation_ref.shape[0]
    own_part, near_part = core_halves(rotation_ref)
    own = product(own_part, leaf_ref[:rank]).astype(BF16)
    near = product(near_part, other_leaf_ref[:rank]).astype(BF16)
    for start in range(0, own_ref.shape[0], chunk):
        rows = pl.ds(start, chunk)
        total = product(own_ref[rows], own, True) + product(near_ref[rows], near, True)
        out_ref[rows] = total.astype(BF16)


def branch_kernel(
    chunk, mine_ref, raw_ref, far_ref, corner_ref, far_other_ref, far_rotation_ref,
    lower_ref, upper_ref,
):
    high_bit = bit_of(("snap", 1)) == 1
    rank = far_rotation_ref.shape[0]
    far_part, corner_part = core_halves(far_rotation_ref)
    raw, below = raw_ref.shape[0], mine_ref.shape[0] - raw_ref.shape[0]

    def turned(part, ref, place):
        pieces = [ref[pl.ds(place + offset, rank)] for offset in (0, rank)]
        return product(part, jnp.concatenate(pieces, axis=1)).astype(BF16)

    far = turned(far_part, far_ref, below)
    corner = turned(corner_part, far_other_ref, 0)
    for start in range(0, mine_ref.shape[0], chunk):
        rows = pl.ds(start, chunk)
        if start < raw:
            theirs = product(raw_ref[rows], far, True)
        else:
            theirs = product(far_ref[pl.ds(start - raw, chunk)], far_part, True)
        theirs = theirs + product(corner_ref[rows], corner, True)
        mine = mine_ref[rows].astype(F32)
        lower_ref[rows] = jnp.where(high_bit, theirs, mine).astype(BF16)
        upper_ref[rows] = jnp.where(high_bit, mine, theirs).astype(BF16)


def root_kernel(
    scale, chunk, kept_ref, other_ref, cross_ref, start_ref, lower_ref, upper_ref, out_ref
):
    high_bit = bit_of(("snap", 1)) == 1
    kept, other = kept_ref[...], other_ref[...]
    cross = cross_ref[...] * scale
    top = jnp.concatenate([jnp.where(high_bit, other, kept), cross], axis=1)
    bottom = jnp.concatenate([cross.T, jnp.where(high_bit, kept, other)], axis=1)
    gram = jnp.concatenate([top, bottom], axis=0)
    rotation = subspace_steps(gram, start_ref[...], POWER).astype(BF16)
    for start in range(0, lower_ref.shape[0], chunk):
        rows = pl.ds(start, chunk)
        root = jnp.concatenate([lower_ref[rows], upper_ref[rows]], axis=1)
        out_ref[rows] = product(root, rotation, True).astype(BF16)


def call(kernel, out_shape, *operands, microseconds=8, limit=8 * MIB):
    vmem = pl.BlockSpec(memory_space=pltpu.VMEM)
    return pl.pallas_call(
        kernel,
        out_shape=out_shape,
        in_specs=[vmem] * len(operands),
        out_specs=jax.tree.map(lambda _: vmem, out_shape),
        compiler_params=pltpu.CompilerParams(vmem_limit_bytes=limit),
        cost_estimate=pl.CostEstimate(
            flops=microseconds * 10**9, bytes_accessed=MIB, transcendentals=0
        ),
    )(*operands)


def on_device(fields, start_local, start_pair, start_root):
    local_rows, snaps = fields.shape
    rank = start_local.shape[1]
    quarter = local_rows // 4
    chunk = quarter // 6
    scale = 1.0 / (local_rows * lax.axis_size("grid"))
    core_step, far_step = ("snap", 0), ("snap", 1)
    grid_steps = axis_steps("grid")

    rows = jax.ShapeDtypeStruct((quarter, snaps), fields.dtype)
    raw = quarter // 2
    raw_part = jax.ShapeDtypeStruct((raw, snaps), fields.dtype)
    rest_part = jax.ShapeDtypeStruct((quarter - raw, snaps), fields.dtype)
    everything = jax.ShapeDtypeStruct((4, quarter, snaps), fields.dtype)
    placed = pl.pallas_call(
        place_kernel,
        out_shape=(everything,) + (rows,) * 3 + (raw_part, rest_part),
        in_specs=[pl.BlockSpec(memory_space=pltpu.HBM)],
        out_specs=(pl.BlockSpec(memory_space=pltpu.VMEM),) * 6,
        scratch_shapes=[pltpu.SemaphoreType.DMA((9,))],
        name="place",
        compiler_params=pltpu.CompilerParams(vmem_limit_bytes=46 * MIB),
    )(fields.reshape(4, quarter, snaps))
    everything, own_rows, near_sent, corner_sent, raw_sent, rest_sent = placed
    everything = everything.reshape(local_rows, snaps)
    near_rows = exchange(near_sent, core_step)
    far_core_rows = exchange(corner_sent, core_step)
    corner_rows = exchange(far_core_rows, far_step)
    raw_rows = exchange(raw_sent, far_step)

    piece = jax.ShapeDtypeStruct((rank + 8, rank), F32)
    kept, sent = call(
        lambda *refs: pack_kernel(grid_steps[0], *refs),
        (piece, piece), inner_product(everything, everything),
        microseconds=1, limit=2 * MIB,
    )
    kept = kept + exchange(sent, grid_steps[0])
    for step in grid_steps[1:]:
        kept = kept + exchange(kept, step)
    other = exchange(kept, grid_steps[0])

    cross = inner_product(own_rows, near_rows)
    cross = cross + inner_product(raw_sent, far_core_rows[:raw])
    cross = cross + inner_product(rest_sent, far_core_rows[raw:])
    half = jax.ShapeDtypeStruct((rank, snaps), F32)
    slab, slab_sent = call(orient_kernel, (half, half), cross, microseconds=1)
    slab = slab + exchange(slab_sent, core_step)
    slab = sum_over(slab, grid_steps)
    other_slab = exchange(slab, core_step)

    turned = jax.ShapeDtypeStruct((rank, snaps), F32)
    turned_pair = jax.ShapeDtypeStruct((rank, 2 * rank), F32)
    local_basis, pair_basis, root_basis = call(
        turn_kernel, (turned, turned_pair, turned_pair),
        start_local, start_pair, start_root,
        microseconds=1,
    )
    square = jax.ShapeDtypeStruct((rank, rank), F32)
    leaf = call(
        lambda *refs: leaf_kernel(scale, grid_steps[0], *refs),
        jax.ShapeDtypeStruct((2 * rank, snaps), BF16),
        kept, other, local_basis,
    )
    other_leaf = exchange(leaf, core_step)
    rows = jax.ShapeDtypeStruct((quarter, rank), BF16)
    rest = jax.ShapeDtypeStruct((quarter - raw + 2 * rank, rank), BF16)
    far_rows = call(
        lambda *refs: far_leaf_kernel(chunk, *refs), rest, rest_sent, leaf,
        microseconds=1,
    )
    far_rows = exchange(far_rows, far_step)
    far_other = exchange(far_rows[quarter - raw :], core_step)

    rotation, gram = call(
        lambda *refs: pair_kernel(scale, *refs),
        (
            jax.ShapeDtypeStruct((rank, 2 * rank), BF16),
            jax.ShapeDtypeStruct((2 * rank, 2 * rank), F32),
        ),
        leaf, other_leaf, slab, other_slab, pair_basis,
    )
    kept = call(kept_kernel, square, rotation, gram, microseconds=1)
    far_rotation = permute(rotation, [far_step, core_step])
    other = permute(kept, [far_step, core_step])
    mine = call(
        lambda *refs: mine_kernel(chunk, *refs), rows,
        own_rows, near_rows, leaf, other_leaf, rotation,
        microseconds=1,
    )
    lower, upper = call(
        lambda *refs: branch_kernel(chunk, *refs), (rows, rows),
        mine, raw_rows, far_rows, corner_rows, far_other, far_rotation,
        microseconds=1, limit=16 * MIB,
    )
    steps = [far_step] + grid_steps
    cross = sum_everywhere(inner_product(lower, upper), core_step, steps)
    return call(
        lambda *refs: root_kernel(scale, chunk, *refs),
        rows,
        kept, other, cross, root_basis, lower, upper,
        limit=16 * MIB,
    )


def solution(mesh):
    in_specs = (P("grid", "snap"), P("snap", None), P(), P())
    out_specs = P(("grid", "snap"), None)
    return jax.shard_map(
        on_device, mesh=mesh, in_specs=in_specs, out_specs=out_specs, check_vma=False
    )
```
